256 devices in a mesh: tm: 64 (over z, y, core), site: 4 (over x).
Axes of the slice: x: 4, y: 4, z: 8, core: 2. Of those that a mesh axis runs over, the one named last changes fastest.
Arguments:
- obs_rows: bfloat16 [131072, 256], P(('tm', 'site')), may hold values from -2 to 2
- obs_values: bfloat16 [131072], P(('tm', 'site')), may hold values from -6 to 6
- obs_hours: int32 [131072], P(('tm', 'site')), may hold values from 0 to 3
- prior_precision: float32 [256, 256], replicated, may hold values from -1 to 3, as said below
- transition: float32 [256, 256], replicated, may hold values from -1 to 1
- site_basis: bfloat16 [1048576, 256], P(('tm', 'site')), may hold values from -0.375 to 0.375
Outputs:
- prediction: bfloat16 [256, 1048576], P(None, ('tm', 'site'))
The draws below stay inside these ranges and needn't reach their ends.
Inputs may be any that keep to these rules, and one draw needn't show every extreme that they name: `prior_precision`: symmetric and positive definite.
All inputs are finite; a program needn't handle non-finite values. Where the reference program divides by a largest or mean magnitude, that divisor is 1e-20 or more.
Results may differ from the reference program's by a relative error of at most 0.0049.
Values may be sent and summed in bfloat16 or wider, within the bound.
A program may use at most 64 MiB of HBM per device.

```python
import jax
import jax.numpy as jnp
from jax import lax

S = 256
NS_ITERS = 8
OBS_DEV = 512
HR = 4
HOURS = 256
OBS = 131072
SITES = 1048576
N_TM = 64
N_SITE = 4


def draw_obs_rows(key, part):
    scale_key, block_key, entry_key = jax.random.split(jax.random.fold_in(key, 31), 3)
    lowest, highest = (0.03, 0.6)
    column_scale = jnp.exp(jax.random.uniform(scale_key, (S,), jnp.float32, jnp.log(lowest), jnp.log(highest)))
    blocks = HOURS // HR
    block_scale = jnp.exp(jax.random.uniform(block_key, (blocks, 1, S), jnp.float32, jnp.log(0.5), jnp.log(2.0)))
    entries = jnp.clip(jax.random.normal(entry_key, (blocks, OBS // blocks, S), jnp.float32), -4.0, 4.0)
    scaled = entries * (column_scale * OBS_DEV ** (-0.5))[None, None, :] * block_scale
    return scaled.reshape(OBS, S).astype(jnp.bfloat16)


def draw_prior_precision(key, part):
    first_key, second_key = jax.random.split(jax.random.fold_in(key, 11))
    lowest, highest = (0.25, 1.5)
    diagonal = jnp.exp(jax.random.uniform(first_key, (S,), jnp.float32, jnp.log(lowest), jnp.log(highest)))
    factor = jax.random.normal(second_key, (S, S), jnp.float32)
    return jnp.diag(diagonal) + 0.5 * jnp.dot(factor, factor.T, precision=lax.Precision.HIGHEST) / S


def draw_transition(key, part):
    first_key, second_key = jax.random.split(jax.random.fold_in(key, 23))
    slowest, fastest = (0.25 / HOURS, 0.1)
    rates = jnp.exp(jax.random.uniform(first_key, (S,), jnp.float32, jnp.log(slowest), jnp.log(fastest)))
    mixing = jnp.eye(S, dtype=jnp.float32) + jax.random.normal(second_key, (S, S), jnp.float32) * (0.05 * S ** (-0.5))
    for sweep in range(12):
        square = jnp.dot(mixing, mixing.T, precision=lax.Precision.HIGHEST)
        mixing = 1.5 * mixing - 0.5 * jnp.dot(square, mixing, precision=lax.Precision.HIGHEST)
    return jnp.exp(-rates)[:, None] * mixing


def place_ends(drawn, own_key, least, top_value):
    shape = drawn.shape
    spot = [jax.random.randint(jax.random.fold_in(own_key, axis), (), 0, shape[axis]) for axis in range(len(shape))]
    drawn = drawn.at[tuple(spot)].set(least)
    longest = shape.index(max(shape))
    spot[longest] = (spot[longest] + 1) % shape[longest]
    return drawn.at[tuple(spot)].set(top_value)


def level_of(own_key, extent, cuts, low, high):
    def one(dim, shards_of):
        draws = jax.random.uniform(jax.random.fold_in(jax.random.fold_in(own_key, 6), dim), (shards_of,), jnp.float32, low / len(cuts), high / len(cuts))
        return jnp.repeat(jnp.exp(draws), extent[dim] // shards_of).reshape((-1,) + (1,) * (len(extent) - dim - 1))

    factor_of = one(*cuts[0])
    for cut in cuts[1:]:
        factor_of = factor_of * one(*cut)
    return factor_of


def scatter_about(own_key, extent, width, most, shards=(), held_as=jnp.bfloat16):
    values = jax.random.normal(own_key, extent, jnp.float32) * width
    if len(shards) > 0:
        values = level_of(own_key, extent, shards, -0.22, 0.18) * values
    return jnp.clip(values, min=-most, max=most).astype(held_as)


def setup_inputs(seed: int = 0) -> dict:
    key_of = jax.random.split(jax.random.key(seed), 7)
    return {
        "obs_rows": draw_obs_rows(jax.random.fold_in(key_of[6], 71), 0),
        "obs_values": scatter_about(key_of[1], (OBS,), 1.0, 6.0, ((0, 256),)),
        "obs_hours": place_ends(jax.random.randint(key_of[2], (OBS,), 0, HR), jax.random.fold_in(key_of[2], 1), 0, HR - 1).astype(jnp.int32),
        "prior_precision": draw_prior_precision(jax.random.fold_in(key_of[6], 71), 0),
        "transition": draw_transition(jax.random.fold_in(key_of[6], 71), 0),
        "site_basis": scatter_about(key_of[5], (SITES, S), S ** -0.5, 0.375, ((0, 256),)),
    }


def reference(obs_rows, obs_values, obs_hours, prior_precision, transition, site_basis):
    block_rows = N_SITE * OBS_DEV
    features = obs_rows.reshape(N_TM, block_rows, S)
    values = obs_values.reshape(N_TM, block_rows)
    labels = obs_hours.reshape(N_TM, block_rows)
    coupled = jnp.dot(prior_precision, transition, precision=lax.Precision.HIGHEST)

    def block_step(running, inputs):
        feature_block, value_block, label_block = inputs
        hour_slot = lax.broadcasted_iota(jnp.int32, (N_SITE, block_rows), 0)
        member = label_block[None, :] == hour_slot
        wide_rows = feature_block.astype(jnp.float32)
        masked = jnp.where(member[:, :, None], wide_rows[None], jnp.float32(0.0))
        grams = jnp.einsum("hrs,rt->hst", masked, wide_rows, precision=lax.Precision.HIGHEST)
        weighted = jnp.where(member, value_block.astype(jnp.float32)[None], jnp.float32(0.0))
        drives = jnp.einsum("hr,rs->hs", weighted, wide_rows, precision=lax.Precision.HIGHEST)
        state_mean = running
        results = []
        for position in range(N_SITE):
            precision_mat = prior_precision + grams[position]
            bound = jnp.max(jnp.sum(jnp.abs(precision_mat), axis=1))
            source = jnp.dot(coupled, state_mean, precision=lax.Precision.HIGHEST) + drives[position]

            def series_step(counter, state):
                current, summed = state
                summed = summed + current
                current = current - jnp.dot(precision_mat, current, precision=lax.Precision.HIGHEST) / bound
                return current, summed

            finished = lax.fori_loop(0, 2 ** NS_ITERS, series_step, (source, jnp.zeros_like(source)))
            state_mean = finished[1] / bound
            results.append(state_mean)
        return state_mean, jnp.stack(results)

    final_mean, means = lax.scan(block_step, jnp.zeros((S,), jnp.float32), (features, values, labels))
    rounded = means.reshape(HOURS, S).astype(jnp.bfloat16)
    return jnp.dot(rounded, site_basis.T, preferred_element_type=jnp.float32).astype(jnp.bfloat16)
```

```python
import jax
import jax.numpy as jnp
from jax import lax
from jax.experimental import pallas as pl
from jax.experimental.pallas import tpu as pltpu
from jax.sharding import PartitionSpec as P

F32, BF16 = jnp.float32, jnp.bfloat16
MESH = pl.DeviceIdType.MESH

S = 256
NS_ITERS = 8
HR = 4
PAD = 16
ROWS = S + PAD
NX, NY, NC, NZ = 4, 4, 2, 8
PLANE = NY * NC


def split(a):
    high = a.astype(BF16)
    return high, (a - high.astype(F32)).astype(BF16)


def mm(a, b):
    return jnp.dot(a, b, preferred_element_type=F32)


def dot3(a, b):
    ah, al = a
    bh, bl = b
    return mm(ah, bh) + mm(al, bh) + mm(ah, bl)


def wide(row):
    return jnp.broadcast_to(row, (PAD, S))


def kernel(
    rows_hbm, vals_hbm, hours_hbm, prior_hbm, trans_hbm,
    out_ref,
    xs, vs, hs, prior, trans, coupled, power, grams, drives, work, prefix, partner,
    ydiff, yoff, pre, full, handed, planemap, qhi, qlo, qoff, sin, sout, means,
    load_sem, xsend, xrecv, asend, arecv, csend, crecv, ysend, yrecv, osend, orecv,
    ssend, srecv, psend, precv, zsend, zrecv,
):
    tm = lax.axis_index("tm")
    x = lax.axis_index("site")
    spot = lax.rem(tm, PLANE)
    core = lax.rem(tm, NC)
    y = lax.div(spot, NC)
    z = lax.div(tm, PLANE)

    def at(zz, yy, cc):
        return zz * PLANE + yy * NC + cc

    loads = [
        pltpu.make_async_copy(rows_hbm.at[pl.ds(0, 256)], xs.at[3, 0], load_sem.at[0]),
        pltpu.make_async_copy(rows_hbm.at[pl.ds(256, 256)], xs.at[3, 1], load_sem.at[1]),
        pltpu.make_async_copy(vals_hbm, vs.at[3], load_sem.at[2]),
        pltpu.make_async_copy(hours_hbm, hs.at[3], load_sem.at[3]),
        pltpu.make_async_copy(prior_hbm, prior, load_sem.at[4]),
        pltpu.make_async_copy(trans_hbm, trans, load_sem.at[5]),
    ]
    for copy in loads:
        copy.start()

    barrier = pltpu.get_barrier_semaphore()
    greeted = [(tm, lax.rem(x + k, NX)) for k in range(1, NX)]
    greeted += [(z * PLANE + lax.rem(spot + k, PLANE), x) for k in range(1, PLANE)]
    greeted += [(lax.rem(z + k, NZ) * PLANE + spot, x) for k in range(1, NZ)]
    greeted += [(at(lax.rem(z + NZ + 1 - 2 * core, NZ), y, 1 - core), x)]
    for device in greeted:
        pl.semaphore_signal(barrier, inc=1, device_id=device, device_id_type=MESH)
    pl.semaphore_wait(barrier, len(greeted))

    started = []

    def remote(src, dst, send_sem, recv_sem, device):
        return pltpu.make_async_remote_copy(
            src_ref=src, dst_ref=dst, send_sem=send_sem, recv_sem=recv_sem,
            device_id=device, device_id_type=MESH,
        )

    def send(*args):
        copy = remote(*args)
        copy.start()
        started.append(copy)

    def arrived(ref, send_sem, recv_sem):
        remote(ref, ref, send_sem, recv_sem, (tm, x)).wait_recv()

    right, left, across = ((tm, lax.rem(x + k, NX)) for k in (1, 3, 2))
    for half in (0, 1):
        part = rows_hbm.at[pl.ds(half * 256, 256)]
        send(part, xs.at[0, half], xsend.at[0, half], xrecv.at[0, half], right)
        part = rows_hbm.at[pl.ds((1 - half) * 256, 256)]
        send(part, xs.at[1, 1 - half], xsend.at[1, 1 - half], xrecv.at[1, 1 - half], left)
    for slot, device in ((0, right), (1, left), (2, across)):
        send(vals_hbm, vs.at[slot], asend.at[0, slot], arecv.at[0, slot], device)
        send(hours_hbm, hs.at[slot], asend.at[1, slot], arecv.at[1, slot], device)

    for copy in loads:
        copy.wait()

    transposed = trans[...].T
    coupled[...] = dot3(split(transposed), split(prior[...]))
    power[...] = transposed
    for _ in range(3):
        parts = split(power[...])
        power[...] = dot3(parts, parts)

    def add_rows(slot, first):
        hour = hs[slot]
        value = vs[slot].astype(F32)
        sub = lax.broadcasted_iota(jnp.int32, (PAD, 512), 0)
        marked = jnp.where(sub == hour, value, 0.0).astype(BF16)
        shape = (2 * 256, S)
        block = xs[slot].reshape(shape)
        turned = block.T
        total = mm(marked, block)
        drives[...] = total if first else drives[...] + total
        for h in range(HR):
            member = jnp.where(hour == h, 1.0, 0.0).astype(BF16)
            product = mm(turned * member, block)
            grams[h] = product if first else grams[h] + product

    add_rows(3, True)
    arrived(xs.at[0, 0], xsend.at[0, 0], xrecv.at[0, 0])
    send(xs.at[0, 0], xs.at[2, 0], xsend.at[2, 0], xrecv.at[2, 0], right)
    arrived(xs.at[1, 1], xsend.at[1, 1], xrecv.at[1, 1])
    send(xs.at[1, 1], xs.at[2, 1], xsend.at[2, 1], xrecv.at[2, 1], left)
    for slot in range(3):
        arrived(vs.at[slot], asend.at[0, slot], arecv.at[0, slot])
        arrived(hs.at[slot], asend.at[1, slot], arecv.at[1, slot])
    arrived(xs.at[0, 1], xsend.at[0, 1], xrecv.at[0, 1])
    add_rows(0, False)
    arrived(xs.at[1, 0], xsend.at[1, 0], xrecv.at[1, 0])
    add_rows(1, False)
    arrived(xs.at[2, 0], xsend.at[2, 0], xrecv.at[2, 0])
    arrived(xs.at[2, 1], xsend.at[2, 1], xrecv.at[2, 1])
    add_rows(2, False)

    eye = (
        lax.broadcasted_iota(jnp.int32, (S, S), 0) == lax.broadcasted_iota(jnp.int32, (S, S), 1)
    ).astype(F32)
    for h in range(HR):
        lam = prior[...] + grams[h]
        bound = jnp.max(jnp.sum(jnp.abs(lam), axis=0, keepdims=True), axis=1, keepdims=True)
        scale = 1.0 / bound
        work[h, 0:S] = eye - lam * scale
        work[h, S:2 * S] = coupled[...] * scale
        work[h, 2 * S:2 * S + PAD] = drives[...] * scale

    def level(k, carry):
        for h in range(HR):
            held = work[h]
            parts = split(held)
            factor = (parts[0][0:S], parts[1][0:S])
            product = dot3(parts, factor)
            work[h, 0:S] = product[0:S]
            work[h, S:2 * S + PAD] = held[S:2 * S + PAD] + product[S:2 * S + PAD]
        return carry

    lax.fori_loop(0, NS_ITERS, level, 0)

    prefix[0, 0:S] = work[0, S:2 * S]
    prefix[0, S:ROWS] = wide(work[0, 2 * S:2 * S + 1])
    for h in range(1, HR):
        joined = dot3(split(prefix[h - 1]), split(work[h, S:2 * S]))
        prefix[h, 0:S] = joined[0:S]
        prefix[h, S:ROWS] = joined[S:ROWS] + wide(work[h, 2 * S + h:2 * S + h + 1])

    def after(earlier, later_map, later_off):
        joined = dot3(split(earlier), split(later_map))
        return joined[0:S], joined[S:ROWS] + wide(later_off)

    to_core0 = remote(prefix.at[HR - 1], partner, csend, crecv, (at(z, y, 0), x))
    to_core1 = remote(handed, full, psend.at[7], precv.at[7], (at(z, y, 1), x))

    def to_ring(src, dst, s, r, device):
        return remote(src, dst, s, r, device)

    y_right, y_left, y_across = ((at(z, lax.rem(y + k, NY), 0), x) for k in (1, 3, 2))
    ring = []
    for half in (0, 1):
        ring.append(to_ring(ydiff.at[y, half], ydiff.at[y, half], ysend.at[0, half], yrecv.at[0, half], y_right))
        ring.append(to_ring(ydiff.at[y, 1 - half], ydiff.at[y, 1 - half], ysend.at[1, 1 - half], yrecv.at[1, 1 - half], y_left))
    for slot, device in ((0, y_right), (1, y_left), (2, y_across)):
        ring.append(to_ring(yoff.at[y], yoff.at[y], osend.at[slot], orecv.at[slot], device))
    behind, ahead, opposite = (lax.rem(y + k, NY) for k in (3, 1, 2))
    ring_relay = [
        to_ring(ydiff.at[behind, 0], ydiff.at[behind, 0], ysend.at[2, 0], yrecv.at[2, 0], y_right),
        to_ring(ydiff.at[ahead, 1], ydiff.at[ahead, 1], ysend.at[2, 1], yrecv.at[2, 1], y_left),
    ]
    up = lax.rem(z + 1, NZ)
    steps = [
        remote(sout, sin, ssend.at[0], srecv, (at(up, y, 0), x)),
        remote(sout, sin, ssend.at[1], srecv, (at(up, y, 1), x)),
    ]

    def pass_on():
        for copy in steps:
            copy.start()

    def ready_means():
        for h in range(HR):
            m, o = after(full[...], prefix[h, 0:S], prefix[h, S:S + 1])
            high, low = split(m)
            qhi[h] = high
            qlo[h] = low
            qoff[h] = o[0:8]

    def apply(state, high, low):
        sh, sl = split(wide(state))
        both = mm(jnp.concatenate([sh, sl], axis=0), high)
        return both[0:1] + both[PAD:PAD + 1] + mm(sh, low)[0:1]

    @pl.when(core == 1)
    def _():
        to_core0.start()
        arrived(full, psend.at[7], precv.at[7])

    @pl.when(core == 0)
    def _():
        arrived(partner, csend, crecv)
        m, o = after(prefix[HR - 1], partner[0:S], partner[S:S + 1])
        diff = (power[...] - m).astype(BF16)
        ydiff[y, 0] = diff[0:128]
        ydiff[y, 1] = diff[128:256]
        yoff[y] = o[0:8]
        for copy in ring:
            copy.start()
        arrived(ydiff.at[behind, 0], ysend.at[0, 0], yrecv.at[0, 0])
        ring_relay[0].start()
        arrived(ydiff.at[ahead, 1], ysend.at[1, 1], yrecv.at[1, 1])
        ring_relay[1].start()
        arrived(ydiff.at[behind, 1], ysend.at[0, 1], yrecv.at[0, 1])
        arrived(ydiff.at[ahead, 0], ysend.at[1, 0], yrecv.at[1, 0])
        arrived(ydiff.at[opposite, 0], ysend.at[2, 0], yrecv.at[2, 0])
        arrived(ydiff.at[opposite, 1], ysend.at[2, 1], yrecv.at[2, 1])
        for slot, origin in ((0, behind), (1, ahead), (2, opposite)):
            arrived(yoff.at[origin], osend.at[slot], orecv.at[slot])

        def chip(j):
            return power[...] - ydiff[j].reshape(S, S).astype(F32), yoff[j, 0:1]

        pre[0, 0:S] = eye
        pre[0, S:ROWS] = jnp.zeros((PAD, S), F32)
        m, o = chip(0)
        pre[1, 0:S] = m
        pre[1, S:ROWS] = wide(o)
        for j in (1, 2, 3):
            m, o = after(pre[j], *chip(j))
            pre[j + 1, 0:S] = m
            pre[j + 1, S:ROWS] = o

        @pl.when(z == 0)
        def _():
            sout[...] = pre[NY, S:S + 1]
            pass_on()

        high, low = split(pre[NY, 0:S])
        planemap[0] = high
        planemap[1] = low
        full[...] = pre[y]
        m, o = after(pre[y], prefix[HR - 1, 0:S], prefix[HR - 1, S:S + 1])
        handed[0:S] = m
        handed[S:ROWS] = o
        to_core1.start()

    @pl.when(z >= 2)
    def _():
        ready_means()

    @pl.when(z == 0)
    def _():
        sin[...] = jnp.zeros((1, S), F32)

    @pl.when(z > 0)
    def _():
        arrived(sin, ssend.at[0], srecv)

    @pl.when(jnp.logical_and(core == 0, jnp.logical_and(z > 0, z < NZ - 1)))
    def _():
        sout[...] = apply(sin[...], planemap[0], planemap[1]) + pre[NY, S:S + 1]
        pass_on()

    @pl.when(z < 2)
    def _():
        ready_means()

    found = [apply(sin[...], qhi[h], qlo[h]) + qoff[h, 0:1] for h in range(HR)]
    means[tm] = jnp.concatenate(found, axis=0).astype(BF16)

    for k in range(1, PLANE):
        device = (z * PLANE + lax.rem(spot + k, PLANE), x)
        send(means.at[tm], means.at[tm], psend.at[k - 1], precv.at[k - 1], device)
    for k in range(1, PLANE):
        origin = z * PLANE + lax.rem(spot + PLANE - k, PLANE)
        arrived(means.at[origin], psend.at[k - 1], precv.at[k - 1])
    own = means.at[pl.ds(z * PLANE, PLANE)]
    for k in range(1, NZ):
        device = (lax.rem(z + k, NZ) * PLANE + spot, x)
        send(own, own, zsend.at[k - 1], zrecv.at[k - 1], device)
    for k in range(1, NZ):
        origin = lax.rem(z + NZ - k, NZ)
        arrived(means.at[pl.ds(origin * PLANE, PLANE)], zsend.at[k - 1], zrecv.at[k - 1])
    out_ref[...] = means[...]

    for copy in started:
        copy.wait_send()

    @pl.when(core == 1)
    def _():
        to_core0.wait_send()

    @pl.when(core == 0)
    def _():
        for copy in ring + ring_relay + [to_core1]:
            copy.wait_send()

    @pl.when(jnp.logical_and(core == 0, z < NZ - 1))
    def _():
        for copy in steps:
            copy.wait_send()


def filtered_means(obs_rows, obs_values, obs_hours, prior_precision, transition):
    any_space = pl.BlockSpec(memory_space=pl.ANY)
    dma = pltpu.SemaphoreType.DMA
    return pl.pallas_call(
        kernel,
        out_shape=jax.ShapeDtypeStruct((NZ * PLANE, HR, S), BF16),
        in_specs=[any_space] * 5,
        out_specs=pl.BlockSpec(memory_space=pltpu.VMEM),
        scratch_shapes=[
            pltpu.VMEM((4, 2, 256, S), BF16),
            pltpu.VMEM((4, 1, 512), BF16),
            pltpu.VMEM((4, 1, 512), jnp.int32),
            pltpu.VMEM((S, S), F32),
            pltpu.VMEM((S, S), F32),
            pltpu.VMEM((S, S), F32),
            pltpu.VMEM((S, S), F32),
            pltpu.VMEM((HR, S, S), F32),
            pltpu.VMEM((PAD, S), F32),
            pltpu.VMEM((HR, 2 * S + PAD, S), F32),
            pltpu.VMEM((HR, ROWS, S), F32),
            pltpu.VMEM((ROWS, S), F32),
            pltpu.VMEM((NY, 2, 128, S), BF16),
            pltpu.VMEM((NY, 8, S), F32),
            pltpu.VMEM((NY + 1, ROWS, S), F32),
            pltpu.VMEM((ROWS, S), F32),
            pltpu.VMEM((ROWS, S), F32),
            pltpu.VMEM((2, S, S), BF16),
            pltpu.VMEM((HR, S, S), BF16),
            pltpu.VMEM((HR, S, S), BF16),
            pltpu.VMEM((HR, 8, S), F32),
            pltpu.VMEM((1, S), F32),
            pltpu.VMEM((1, S), F32),
            pltpu.VMEM((NZ * PLANE, HR, S), BF16),
            dma((6,)),
            dma((3, 2)), dma((3, 2)),
            dma((2, 3)), dma((2, 3)),
            dma(()), dma(()),
            dma((3, 2)), dma((3, 2)),
            dma((3,)), dma((3,)),
            dma((2,)), dma(()),
            dma((8,)), dma((8,)),
            dma((7,)), dma((7,)),
        ],
        compiler_params=pltpu.CompilerParams(
            collective_id=0, has_side_effects=True, vmem_limit_bytes=32 * 1024 * 1024
        ),
    )(obs_rows, obs_values[None], obs_hours[None], prior_precision, transition)


def body(obs_rows, obs_values, obs_hours, prior_precision, transition, site_basis):
    means = filtered_means(obs_rows, obs_values, obs_hours, prior_precision, transition)
    return jnp.einsum(
        "hs,ns->hn", means.reshape(NZ * PLANE * HR, S), site_basis, preferred_element_type=F32
    ).astype(BF16)


def solution(mesh):
    in_specs = (
        P(("tm", "site"), None),
        P(("tm", "site")),
        P(("tm", "site")),
        P(),
        P(),
        P(("tm", "site"), None),
    )
    out_specs = P(None, ("tm", "site"))
    return jax.shard_map(body, mesh=mesh, in_specs=in_specs, out_specs=out_specs, check_vma=False)
```

```python
import jax
import jax.numpy as jnp
from jax import lax
from jax.experimental import pallas as pl
from jax.experimental.pallas import tpu as pltpu
from jax.sharding import PartitionSpec as P

F32, BF16 = jnp.float32, jnp.bfloat16
MESH = pl.DeviceIdType.MESH

S = 256
NS_ITERS = 8
HR = 4
PAD = 16
ROWS = S + PAD
NX, NY, NC, NZ = 4, 4, 2, 8
PLANE = NY * NC


def split(a):
    high = a.astype(BF16)
    return high, (a - high.astype(F32)).astype(BF16)


def mm(a, b):
    return jnp.dot(a, b, preferred_element_type=F32)


def dot3(a, b):
    ah, al = a
    bh, bl = b
    return mm(ah, bh) + mm(al, bh) + mm(ah, bl)


def wide(row):
    return jnp.broadcast_to(row, (PAD, S))


def kernel(
    rows_hbm, vals_hbm, hours_hbm, prior_hbm, trans_hbm,
    out_ref,
    xs, vs, hs, prior, trans, coupled, power, grams, drives, work, prefix, partner,
    ydiff, yoff, pre, full, handed, planemap, qhi, qlo, qoff, sin, sout, means,
    load_sem, xsend, xrecv, asend, arecv, csend, crecv, ysend, yrecv, osend, orecv,
    ssend, srecv, psend, precv, zsend, zrecv, heard,
):
    tm = lax.axis_index("tm")
    x = lax.axis_index("site")
    spot = lax.rem(tm, PLANE)
    core = lax.rem(tm, NC)
    y = lax.div(spot, NC)
    z = lax.div(tm, PLANE)

    def at(zz, yy, cc):
        return zz * PLANE + yy * NC + cc

    loads = [
        pltpu.make_async_copy(rows_hbm.at[pl.ds(0, 256)], xs.at[3, 0], load_sem.at[0]),
        pltpu.make_async_copy(rows_hbm.at[pl.ds(256, 256)], xs.at[3, 1], load_sem.at[1]),
        pltpu.make_async_copy(vals_hbm, vs.at[3], load_sem.at[2]),
        pltpu.make_async_copy(hours_hbm, hs.at[3], load_sem.at[3]),
        pltpu.make_async_copy(prior_hbm, prior, load_sem.at[4]),
        pltpu.make_async_copy(trans_hbm, trans, load_sem.at[5]),
    ]
    for copy in loads:
        copy.start()

    barrier = pltpu.get_barrier_semaphore()
    near = [(at(z, y, 1 - core), x)]
    near += [(at(z, lax.rem(y + k, NY), core), x) for k in (1, NY - 1)]
    near += [(at(lax.rem(z + k, NZ), y, core), x) for k in (1, NZ - 1)]
    greeted = [(tm, lax.rem(x + k, NX)) for k in (1, NX - 1)] + near
    for device in greeted:
        pl.semaphore_signal(barrier, inc=1, device_id=device, device_id_type=MESH)
    pl.semaphore_wait(barrier, len(greeted))

    def tell(turn):
        for device in near:
            pl.semaphore_signal(heard.at[turn], inc=1, device_id=device, device_id_type=MESH)

    def hear(turn):
        pl.semaphore_wait(heard.at[turn], len(near))

    started = []

    def remote(src, dst, send_sem, recv_sem, device):
        return pltpu.make_async_remote_copy(
            src_ref=src, dst_ref=dst, send_sem=send_sem, recv_sem=recv_sem,
            device_id=device, device_id_type=MESH,
        )

    def send(*args):
        copy = remote(*args)
        copy.start()
        started.append(copy)

    def arrived(ref, send_sem, recv_sem):
        remote(ref, ref, send_sem, recv_sem, (tm, x)).wait_recv()

    right, left = ((tm, lax.rem(x + k, NX)) for k in (1, 3))
    for half in (0, 1):
        part = rows_hbm.at[pl.ds(half * 256, 256)]
        send(part, xs.at[0, half], xsend.at[0, half], xrecv.at[0, half], right)
        part = rows_hbm.at[pl.ds((1 - half) * 256, 256)]
        send(part, xs.at[1, 1 - half], xsend.at[1, 1 - half], xrecv.at[1, 1 - half], left)
    for slot, device in ((0, right), (1, left)):
        send(vals_hbm, vs.at[slot], asend.at[0, slot], arecv.at[0, slot], device)
        send(hours_hbm, hs.at[slot], asend.at[1, slot], arecv.at[1, slot], device)
    tell(0)

    for copy in loads:
        copy.wait()

    transposed = trans[...].T
    coupled[...] = dot3(split(transposed), split(prior[...]))
    power[...] = transposed
    for _ in range(3):
        parts = split(power[...])
        power[...] = dot3(parts, parts)

    def add_rows(slot, first):
        hour = hs[slot]
        value = vs[slot].astype(F32)
        value = jnp.concatenate([value[i:i + 1] for i in range(4)], axis=1)
        sub = lax.broadcasted_iota(jnp.int32, (PAD, 512), 0)
        marked = jnp.where(sub == hour, value, 0.0).astype(BF16)
        shape = (2 * 256, S)
        block = xs[slot].reshape(shape)
        turned = block.T
        total = mm(marked, block)
        drives[...] = total if first else drives[...] + total
        for h in range(HR):
            member = jnp.where(hour == h, 1.0, 0.0).astype(BF16)
            product = mm(turned * member, block)
            grams[h] = product if first else grams[h] + product

    hear(0)
    tell(1)
    add_rows(3, True)
    hear(1)
    tell(2)
    arrived(xs.at[0, 0], xsend.at[0, 0], xrecv.at[0, 0])
    send(xs.at[0, 0], xs.at[2, 0], xsend.at[2, 0], xrecv.at[2, 0], right)
    arrived(xs.at[1, 1], xsend.at[1, 1], xrecv.at[1, 1])
    send(xs.at[1, 1], xs.at[2, 1], xsend.at[2, 1], xrecv.at[2, 1], left)
    for slot in range(2):
        arrived(vs.at[slot], asend.at[0, slot], arecv.at[0, slot])
        arrived(hs.at[slot], asend.at[1, slot], arecv.at[1, slot])
    send(vs.at[0], vs.at[2], asend.at[0, 2], arecv.at[0, 2], right)
    send(hs.at[0], hs.at[2], asend.at[1, 2], arecv.at[1, 2], right)
    hear(2)
    tell(3)
    arrived(xs.at[0, 1], xsend.at[0, 1], xrecv.at[0, 1])
    add_rows(0, False)
    hear(3)
    tell(4)
    arrived(xs.at[1, 0], xsend.at[1, 0], xrecv.at[1, 0])
    add_rows(1, False)
    hear(4)
    tell(5)
    hear(5)
    arrived(vs.at[2], asend.at[0, 2], arecv.at[0, 2])
    arrived(hs.at[2], asend.at[1, 2], arecv.at[1, 2])
    arrived(xs.at[2, 0], xsend.at[2, 0], xrecv.at[2, 0])
    arrived(xs.at[2, 1], xsend.at[2, 1], xrecv.at[2, 1])
    add_rows(2, False)

    eye = (
        lax.broadcasted_iota(jnp.int32, (S, S), 0) == lax.broadcasted_iota(jnp.int32, (S, S), 1)
    ).astype(F32)
    for h in range(HR):
        lam = prior[...] + grams[h]
        bound = jnp.max(jnp.sum(jnp.abs(lam), axis=0, keepdims=True), axis=1, keepdims=True)
        scale = 1.0 / bound
        work[h, 0:S] = eye - lam * scale
        work[h, S:2 * S] = coupled[...] * scale
        work[h, 2 * S:2 * S + PAD] = drives[...] * scale

    def level(k, carry):
        for h in range(HR):
            held = work[h]
            parts = split(held)
            factor = (parts[0][0:S], parts[1][0:S])
            product = dot3(parts, factor)
            work[h, 0:S] = product[0:S]
            work[h, S:2 * S + PAD] = held[S:2 * S + PAD] + product[S:2 * S + PAD]
        return carry

    lax.fori_loop(0, NS_ITERS, level, 0)

    prefix[0, 0:S] = work[0, S:2 * S]
    prefix[0, S:ROWS] = wide(work[0, 2 * S:2 * S + 1])
    for h in range(1, HR):
        joined = dot3(split(prefix[h - 1]), split(work[h, S:2 * S]))
        prefix[h, 0:S] = joined[0:S]
        prefix[h, S:ROWS] = joined[S:ROWS] + wide(work[h, 2 * S + h:2 * S + h + 1])

    def after(earlier, later_map, later_off):
        joined = dot3(split(earlier), split(later_map))
        return joined[0:S], joined[S:ROWS] + wide(later_off)

    to_core0 = remote(prefix.at[HR - 1], partner, csend, crecv, (at(z, y, 0), x))
    to_core1 = remote(handed, full, psend.at[7], precv.at[7], (at(z, y, 1), x))

    def to_ring(src, dst, s, r, device):
        return remote(src, dst, s, r, device)

    y_right, y_left, y_across = ((at(z, lax.rem(y + k, NY), 0), x) for k in (1, 3, 2))
    ring = []
    for half in (0, 1):
        ring.append(to_ring(ydiff.at[y, half], ydiff.at[y, half], ysend.at[0, half], yrecv.at[0, half], y_right))
        ring.append(to_ring(ydiff.at[y, 1 - half], ydiff.at[y, 1 - half], ysend.at[1, 1 - half], yrecv.at[1, 1 - half], y_left))
    for slot, device in ((0, y_right), (1, y_left), (2, y_across)):
        ring.append(to_ring(yoff.at[y], yoff.at[y], osend.at[slot], orecv.at[slot], device))
    behind, ahead, opposite = (lax.rem(y + k, NY) for k in (3, 1, 2))
    ring_relay = [
        to_ring(ydiff.at[behind, 0], ydiff.at[behind, 0], ysend.at[2, 0], yrecv.at[2, 0], y_right),
        to_ring(ydiff.at[ahead, 1], ydiff.at[ahead, 1], ysend.at[2, 1], yrecv.at[2, 1], y_left),
    ]
    up = lax.rem(z + 1, NZ)
    steps = [
        remote(sout, sin, ssend.at[0], srecv, (at(up, y, 0), x)),
        remote(sout, sin, ssend.at[1], srecv, (at(up, y, 1), x)),
    ]

    def pass_on():
        for copy in steps:
            copy.start()

    def ready_means():
        for h in range(HR):
            m, o = after(full[...], prefix[h, 0:S], prefix[h, S:S + 1])
            high, low = split(m)
            qhi[h] = high
            qlo[h] = low
            qoff[h] = o[0:8]

    def apply(state, high, low):
        sh, sl = split(wide(state))
        both = mm(jnp.concatenate([sh, sl], axis=0), high)
        return both[0:1] + both[PAD:PAD + 1] + mm(sh, low)[0:1]

    @pl.when(core == 1)
    def _():
        to_core0.start()
        arrived(full, psend.at[7], precv.at[7])

    @pl.when(core == 0)
    def _():
        arrived(partner, csend, crecv)
        m, o = after(prefix[HR - 1], partner[0:S], partner[S:S + 1])
        diff = (power[...] - m).astype(BF16)
        ydiff[y, 0] = diff[0:128]
        ydiff[y, 1] = diff[128:256]
        yoff[y] = o[0:8]
        for copy in ring:
            copy.start()
        arrived(ydiff.at[behind, 0], ysend.at[0, 0], yrecv.at[0, 0])
        ring_relay[0].start()
        arrived(ydiff.at[ahead, 1], ysend.at[1, 1], yrecv.at[1, 1])
        ring_relay[1].start()
        arrived(ydiff.at[behind, 1], ysend.at[0, 1], yrecv.at[0, 1])
        arrived(ydiff.at[ahead, 0], ysend.at[1, 0], yrecv.at[1, 0])
        arrived(ydiff.at[opposite, 0], ysend.at[2, 0], yrecv.at[2, 0])
        arrived(ydiff.at[opposite, 1], ysend.at[2, 1], yrecv.at[2, 1])
        for slot, origin in ((0, behind), (1, ahead), (2, opposite)):
            arrived(yoff.at[origin], osend.at[slot], orecv.at[slot])

        def chip(j):
            return power[...] - ydiff[j].reshape(S, S).astype(F32), yoff[j, 0:1]

        pre[0, 0:S] = eye
        pre[0, S:ROWS] = jnp.zeros((PAD, S), F32)
        m, o = chip(0)
        pre[1, 0:S] = m
        pre[1, S:ROWS] = wide(o)
        for j in (1, 2, 3):
            m, o = after(pre[j], *chip(j))
            pre[j + 1, 0:S] = m
            pre[j + 1, S:ROWS] = o

        @pl.when(z == 0)
        def _():
            sout[...] = pre[NY, S:S + 1]
            pass_on()

        high, low = split(pre[NY, 0:S])
        planemap[0] = high
        planemap[1] = low
        full[...] = pre[y]
        m, o = after(pre[y], prefix[HR - 1, 0:S], prefix[HR - 1, S:S + 1])
        handed[0:S] = m
        handed[S:ROWS] = o
        to_core1.start()

    @pl.when(z >= 2)
    def _():
        ready_means()

    @pl.when(z == 0)
    def _():
        sin[...] = jnp.zeros((1, S), F32)

    @pl.when(z > 0)
    def _():
        arrived(sin, ssend.at[0], srecv)

    @pl.when(jnp.logical_and(core == 0, jnp.logical_and(z > 0, z < NZ - 1)))
    def _():
        sout[...] = apply(sin[...], planemap[0], planemap[1]) + pre[NY, S:S + 1]
        pass_on()

    @pl.when(z < 2)
    def _():
        ready_means()

    found = [apply(sin[...], qhi[h], qlo[h]) + qoff[h, 0:1] for h in range(HR)]
    means[z, spot] = jnp.concatenate(found, axis=0).astype(BF16)

    for k in (4, 3, 5, 2, 6, 1, 7):
        device = (lax.rem(z + k, NZ) * PLANE + spot, x)
        send(means.at[z, spot], means.at[z, spot], zsend.at[k - 1], zrecv.at[k - 1], device)

    def spread(origin):
        for j in range(1, PLANE):
            device = (z * PLANE + lax.rem(spot + j, PLANE), x)
            remote(
                means.at[origin, spot], means.at[origin, spot],
                psend.at[j - 1], precv.at[j - 1], device,
            ).start()

    spread(z)
    for k in (1, 7, 2, 6, 3, 5, 4):
        origin = lax.rem(z + NZ - k, NZ)
        arrived(means.at[origin, spot], zsend.at[k - 1], zrecv.at[k - 1])
        spread(origin)
    for j in range(1, PLANE):
        origin = lax.rem(spot + PLANE - j, PLANE)
        arrived(means.at[:, origin], psend.at[j - 1], precv.at[j - 1])
    out_ref[...] = means[...]

    for copy in started:
        copy.wait_send()
    for j in range(1, PLANE):
        device = (z * PLANE + lax.rem(spot + j, PLANE), x)
        remote(
            means.at[:, spot], means.at[:, spot], psend.at[j - 1], precv.at[j - 1], device
        ).wait_send()

    @pl.when(core == 1)
    def _():
        to_core0.wait_send()

    @pl.when(core == 0)
    def _():
        for copy in ring + ring_relay + [to_core1]:
            copy.wait_send()

    @pl.when(jnp.logical_and(core == 0, z < NZ - 1))
    def _():
        for copy in steps:
            copy.wait_send()


def filtered_means(obs_rows, obs_values, obs_hours, prior_precision, transition):
    any_space = pl.BlockSpec(memory_space=pltpu.MemorySpace.HBM)
    dma = pltpu.SemaphoreType.DMA
    return pl.pallas_call(
        kernel,
        out_shape=jax.ShapeDtypeStruct((NZ, PLANE, HR, S), BF16),
        in_specs=[any_space] * 5,
        out_specs=pl.BlockSpec(memory_space=pltpu.VMEM),
        scratch_shapes=[
            pltpu.VMEM((4, 2, 256, S), BF16),
            pltpu.VMEM((4, 4, 128), BF16),
            pltpu.VMEM((4, 1, 512), jnp.int32),
            pltpu.VMEM((S, S), F32),
            pltpu.VMEM((S, S), F32),
            pltpu.VMEM((S, S), F32),
            pltpu.VMEM((S, S), F32),
            pltpu.VMEM((HR, S, S), F32),
            pltpu.VMEM((PAD, S), F32),
            pltpu.VMEM((HR, 2 * S + PAD, S), F32),
            pltpu.VMEM((HR, ROWS, S), F32),
            pltpu.VMEM((ROWS, S), F32),
            pltpu.VMEM((NY, 2, 128, S), BF16),
            pltpu.VMEM((NY, 8, S), F32),
            pltpu.VMEM((NY + 1, ROWS, S), F32),
            pltpu.VMEM((ROWS, S), F32),
            pltpu.VMEM((ROWS, S), F32),
            pltpu.VMEM((2, S, S), BF16),
            pltpu.VMEM((HR, S, S), BF16),
            pltpu.VMEM((HR, S, S), BF16),
            pltpu.VMEM((HR, 8, S), F32),
            pltpu.VMEM((1, S), F32),
            pltpu.VMEM((1, S), F32),
            pltpu.VMEM((NZ, PLANE, HR, S), BF16),
            dma((6,)),
            dma((3, 2)), dma((3, 2)),
            dma((2, 3)), dma((2, 3)),
            dma(()), dma(()),
            dma((3, 2)), dma((3, 2)),
            dma((3,)), dma((3,)),
            dma((2,)), dma(()),
            dma((8,)), dma((8,)),
            dma((7,)), dma((7,)),
            pltpu.SemaphoreType.REGULAR((6,)),
        ],
        compiler_params=pltpu.CompilerParams(
            collective_id=0, has_side_effects=True, vmem_limit_bytes=32 * 1024 * 1024
        ),
    )(*(
        pltpu.with_memory_space_constraint(a, pltpu.MemorySpace.HBM)
        for a in (obs_rows, obs_values.reshape(4, 128), obs_hours[None], prior_precision, transition)
    ))


def body(obs_rows, obs_values, obs_hours, prior_precision, transition, site_basis):
    means = filtered_means(obs_rows, obs_values, obs_hours, prior_precision, transition)
    return jnp.einsum(
        "hs,ns->hn", means.reshape(NZ * PLANE * HR, S), site_basis, preferred_element_type=F32
    ).astype(BF16)


def solution(mesh):
    in_specs = (
        P(("tm", "site"), None),
        P(("tm", "site")),
        P(("tm", "site")),
        P(),
        P(),
        P(("tm", "site"), None),
    )
    out_specs = P(None, ("tm", "site"))
    return jax.shard_map(body, mesh=mesh, in_specs=in_specs, out_specs=out_specs, check_vma=False)
```

```python
import jax
import jax.numpy as jnp
from jax import lax
from jax.experimental import pallas as pl
from jax.experimental.pallas import tpu as pltpu
from jax.sharding import PartitionSpec as P

F32, BF16 = jnp.float32, jnp.bfloat16
MESH = pl.DeviceIdType.MESH

S = 256
NS_ITERS = 8
HR = 4
PAD = 16
ROWS = S + PAD
NX, NY, NC, NZ = 4, 4, 2, 8
PLANE = NY * NC


def split(a):
    high = a.astype(BF16)
    return high, (a - high.astype(F32)).astype(BF16)


def mm(a, b):
    return jnp.dot(a, b, preferred_element_type=F32)


def dot3(a, b):
    ah, al = a
    bh, bl = b
    return mm(ah, bh) + mm(al, bh) + mm(ah, bl)


def wide(row):
    return jnp.broadcast_to(row, (PAD, S))


def kernel(
    rows_hbm, vals_hbm, hours_hbm, prior_hbm, trans_hbm,
    out_ref,
    xs, vs, hs, prior, trans, coupled, power, grams, drives, work, prefix, partner,
    ydiff, yoff, pre, full, handed, planemap, qhi, qlo, qoff, sin, sout, means,
    load_sem, xsend, xrecv, asend, arecv, csend, crecv, ysend, yrecv, osend, orecv,
    ssend, srecv, psend, precv, zsend, zrecv, heard,
):
    tm = lax.axis_index("tm")
    x = lax.axis_index("site")
    spot = lax.rem(tm, PLANE)
    core = lax.rem(tm, NC)
    y = lax.div(spot, NC)
    z = lax.div(tm, PLANE)

    def at(zz, yy, cc):
        return zz * PLANE + yy * NC + cc

    loads = [
        pltpu.make_async_copy(rows_hbm.at[pl.ds(0, 256)], xs.at[3, 0], load_sem.at[0]),
        pltpu.make_async_copy(rows_hbm.at[pl.ds(256, 256)], xs.at[3, 1], load_sem.at[1]),
        pltpu.make_async_copy(vals_hbm, vs.at[3], load_sem.at[2]),
        pltpu.make_async_copy(hours_hbm, hs.at[3], load_sem.at[3]),
        pltpu.make_async_copy(prior_hbm, prior, load_sem.at[4]),
        pltpu.make_async_copy(trans_hbm, trans, load_sem.at[5]),
    ]
    for copy in loads:
        copy.start()

    barrier = pltpu.get_barrier_semaphore()
    near = [(at(z, y, 1 - core), x)]
    near += [(at(z, lax.rem(y + k, NY), core), x) for k in (1, NY - 1)]
    beside = [(tm, lax.rem(x + k, NX)) for k in (1, NX - 1)]
    inner = jnp.where(z > 0, 1, 0) + jnp.where(z < NZ - 1, 1, 0)

    def greet(sem, devices):
        for device in devices:
            pl.semaphore_signal(sem, inc=1, device_id=device, device_id_type=MESH)

        @pl.when(z > 0)
        def _():
            pl.semaphore_signal(sem, inc=1, device_id=(tm - PLANE, x), device_id_type=MESH)

        @pl.when(z < NZ - 1)
        def _():
            pl.semaphore_signal(sem, inc=1, device_id=(tm + PLANE, x), device_id_type=MESH)

    greet(barrier, beside + near)
    pl.semaphore_wait(barrier, len(beside + near) + inner)

    def tell(turn):
        greet(heard.at[turn], near)

    def hear(turn):
        pl.semaphore_wait(heard.at[turn], len(near) + inner)

    started = []

    def remote(src, dst, send_sem, recv_sem, device):
        return pltpu.make_async_remote_copy(
            src_ref=src, dst_ref=dst, send_sem=send_sem, recv_sem=recv_sem,
            device_id=device, device_id_type=MESH,
        )

    def send(*args):
        copy = remote(*args)
        copy.start()
        started.append(copy)

    def arrived(ref, send_sem, recv_sem):
        remote(ref, ref, send_sem, recv_sem, (tm, x)).wait_recv()

    right, left = ((tm, lax.rem(x + k, NX)) for k in (1, 3))
    for half in (0, 1):
        part = rows_hbm.at[pl.ds(half * 256, 256)]
        send(part, xs.at[0, half], xsend.at[0, half], xrecv.at[0, half], right)
        part = rows_hbm.at[pl.ds((1 - half) * 256, 256)]
        send(part, xs.at[1, 1 - half], xsend.at[1, 1 - half], xrecv.at[1, 1 - half], left)
    for slot, device in ((0, right), (1, left)):
        send(vals_hbm, vs.at[slot], asend.at[0, slot], arecv.at[0, slot], device)
        send(hours_hbm, hs.at[slot], asend.at[1, slot], arecv.at[1, slot], device)
    tell(0)

    for copy in loads:
        copy.wait()

    transposed = trans[...].T
    coupled[...] = dot3(split(transposed), split(prior[...]))
    power[...] = transposed
    for _ in range(3):
        parts = split(power[...])
        power[...] = dot3(parts, parts)

    def add_rows(slot, first):
        hour = hs[slot]
        value = vs[slot].astype(F32)
        value = jnp.concatenate([value[i:i + 1] for i in range(4)], axis=1)
        sub = lax.broadcasted_iota(jnp.int32, (PAD, 512), 0)
        marked = jnp.where(sub == hour, value, 0.0).astype(BF16)
        shape = (2 * 256, S)
        block = xs[slot].reshape(shape)
        turned = block.T
        total = mm(marked, block)
        drives[...] = total if first else drives[...] + total
        for h in range(HR):
            member = jnp.where(hour == h, 1.0, 0.0).astype(BF16)
            product = mm(turned * member, block)
            grams[h] = product if first else grams[h] + product

    add_rows(3, True)
    arrived(xs.at[0, 0], xsend.at[0, 0], xrecv.at[0, 0])
    send(xs.at[0, 0], xs.at[2, 0], xsend.at[2, 0], xrecv.at[2, 0], right)
    arrived(xs.at[1, 1], xsend.at[1, 1], xrecv.at[1, 1])
    send(xs.at[1, 1], xs.at[2, 1], xsend.at[2, 1], xrecv.at[2, 1], left)
    for slot in range(2):
        arrived(vs.at[slot], asend.at[0, slot], arecv.at[0, slot])
        arrived(hs.at[slot], asend.at[1, slot], arecv.at[1, slot])
    send(vs.at[0], vs.at[2], asend.at[0, 2], arecv.at[0, 2], right)
    send(hs.at[0], hs.at[2], asend.at[1, 2], arecv.at[1, 2], right)
    arrived(xs.at[0, 1], xsend.at[0, 1], xrecv.at[0, 1])
    add_rows(0, False)
    arrived(xs.at[1, 0], xsend.at[1, 0], xrecv.at[1, 0])
    add_rows(1, False)
    arrived(vs.at[2], asend.at[0, 2], arecv.at[0, 2])
    arrived(hs.at[2], asend.at[1, 2], arecv.at[1, 2])
    arrived(xs.at[2, 0], xsend.at[2, 0], xrecv.at[2, 0])
    arrived(xs.at[2, 1], xsend.at[2, 1], xrecv.at[2, 1])
    add_rows(2, False)

    hear(0)
    tell(1)
    eye = (
        lax.broadcasted_iota(jnp.int32, (S, S), 0) == lax.broadcasted_iota(jnp.int32, (S, S), 1)
    ).astype(F32)
    for h in range(HR):
        lam = prior[...] + grams[h]
        bound = jnp.max(jnp.sum(jnp.abs(lam), axis=0, keepdims=True), axis=1, keepdims=True)
        scale = 1.0 / bound
        work[h, 0:S] = eye - lam * scale
        work[h, S:2 * S] = coupled[...] * scale
        work[h, 2 * S:2 * S + PAD] = drives[...] * scale

    def level(k, carry):
        for h in range(HR):
            held = work[h]
            parts = split(held)
            factor = (parts[0][0:S], parts[1][0:S])
            product = dot3(parts, factor)
            work[h, 0:S] = product[0:S]
            work[h, S:2 * S + PAD] = held[S:2 * S + PAD] + product[S:2 * S + PAD]
        return carry

    lax.fori_loop(0, NS_ITERS, level, 0)

    hear(1)
    tell(2)
    prefix[0, 0:S] = work[0, S:2 * S]
    prefix[0, S:ROWS] = wide(work[0, 2 * S:2 * S + 1])
    for h in range(1, HR):
        joined = dot3(split(prefix[h - 1]), split(work[h, S:2 * S]))
        prefix[h, 0:S] = joined[0:S]
        prefix[h, S:ROWS] = joined[S:ROWS] + wide(work[h, 2 * S + h:2 * S + h + 1])

    def after(earlier, later_map, later_off):
        joined = dot3(split(earlier), split(later_map))
        return joined[0:S], joined[S:ROWS] + wide(later_off)

    to_core0 = remote(prefix.at[HR - 1], partner, csend, crecv, (at(z, y, 0), x))
    to_core1 = remote(handed, full, psend.at[7], precv.at[7], (at(z, y, 1), x))

    def to_ring(src, dst, s, r, device):
        return remote(src, dst, s, r, device)

    y_right, y_left, y_across = ((at(z, lax.rem(y + k, NY), 0), x) for k in (1, 3, 2))
    ring = []
    for half in (0, 1):
        ring.append(to_ring(ydiff.at[y, half], ydiff.at[y, half], ysend.at[0, half], yrecv.at[0, half], y_right))
        ring.append(to_ring(ydiff.at[y, 1 - half], ydiff.at[y, 1 - half], ysend.at[1, 1 - half], yrecv.at[1, 1 - half], y_left))
    for slot, device in ((0, y_right), (1, y_left), (2, y_across)):
        ring.append(to_ring(yoff.at[y], yoff.at[y], osend.at[slot], orecv.at[slot], device))
    behind, ahead, opposite = (lax.rem(y + k, NY) for k in (3, 1, 2))
    ring_relay = [
        to_ring(ydiff.at[behind, 0], ydiff.at[behind, 0], ysend.at[2, 0], yrecv.at[2, 0], y_right),
        to_ring(ydiff.at[ahead, 1], ydiff.at[ahead, 1], ysend.at[2, 1], yrecv.at[2, 1], y_left),
    ]
    up = lax.rem(z + 1, NZ)
    steps = [
        remote(sout, sin, ssend.at[0], srecv, (at(up, y, 0), x)),
        remote(sout, sin, ssend.at[1], srecv, (at(up, y, 1), x)),
    ]

    def pass_on():
        for copy in steps:
            copy.start()

    def ready_means():
        for h in range(HR):
            m, o = after(full[...], prefix[h, 0:S], prefix[h, S:S + 1])
            high, low = split(m)
            qhi[h] = high
            qlo[h] = low
            qoff[h] = o[0:8]

    def apply(state, high, low):
        sh, sl = split(wide(state))
        both = mm(jnp.concatenate([sh, sl], axis=0), high)
        return both[0:1] + both[PAD:PAD + 1] + mm(sh, low)[0:1]

    @pl.when(core == 1)
    def _():
        to_core0.start()
        arrived(full, psend.at[7], precv.at[7])

    @pl.when(core == 0)
    def _():
        arrived(partner, csend, crecv)
        m, o = after(prefix[HR - 1], partner[0:S], partner[S:S + 1])
        diff = (power[...] - m).astype(BF16)
        ydiff[y, 0] = diff[0:128]
        ydiff[y, 1] = diff[128:256]
        yoff[y] = o[0:8]
        for copy in ring:
            copy.start()
        arrived(ydiff.at[behind, 0], ysend.at[0, 0], yrecv.at[0, 0])
        ring_relay[0].start()
        arrived(ydiff.at[ahead, 1], ysend.at[1, 1], yrecv.at[1, 1])
        ring_relay[1].start()
        arrived(ydiff.at[behind, 1], ysend.at[0, 1], yrecv.at[0, 1])
        arrived(ydiff.at[ahead, 0], ysend.at[1, 0], yrecv.at[1, 0])
        arrived(ydiff.at[opposite, 0], ysend.at[2, 0], yrecv.at[2, 0])
        arrived(ydiff.at[opposite, 1], ysend.at[2, 1], yrecv.at[2, 1])
        for slot, origin in ((0, behind), (1, ahead), (2, opposite)):
            arrived(yoff.at[origin], osend.at[slot], orecv.at[slot])

        def chip(j):
            return power[...] - ydiff[j].reshape(S, S).astype(F32), yoff[j, 0:1]

        pre[0, 0:S] = eye
        pre[0, S:ROWS] = jnp.zeros((PAD, S), F32)
        m, o = chip(0)
        pre[1, 0:S] = m
        pre[1, S:ROWS] = wide(o)
        for j in (1, 2, 3):
            m, o = after(pre[j], *chip(j))
            pre[j + 1, 0:S] = m
            pre[j + 1, S:ROWS] = o

        @pl.when(z == 0)
        def _():
            sout[...] = pre[NY, S:S + 1]
            pass_on()

        high, low = split(pre[NY, 0:S])
        planemap[0] = high
        planemap[1] = low
        full[...] = pre[y]
        m, o = after(pre[y], prefix[HR - 1, 0:S], prefix[HR - 1, S:S + 1])
        handed[0:S] = m
        handed[S:ROWS] = o
        to_core1.start()

    hear(2)
    tell(3)
    @pl.when(z >= 2)
    def _():
        ready_means()

    @pl.when(z == 0)
    def _():
        sin[...] = jnp.zeros((1, S), F32)

    @pl.when(z > 0)
    def _():
        arrived(sin, ssend.at[0], srecv)

    @pl.when(jnp.logical_and(core == 0, jnp.logical_and(z > 0, z < NZ - 1)))
    def _():
        sout[...] = apply(sin[...], planemap[0], planemap[1]) + pre[NY, S:S + 1]
        pass_on()

    hear(3)
    tell(4)

    @pl.when(z < 2)
    def _():
        ready_means()

    found = [apply(sin[...], qhi[h], qlo[h]) + qoff[h, 0:1] for h in range(HR)]
    means[z, spot] = jnp.concatenate(found, axis=0).astype(BF16)

    hear(4)
    tell(5)
    hear(5)
    for k in (4, 3, 5, 2, 6, 1, 7):
        device = (lax.rem(z + k, NZ) * PLANE + spot, x)
        send(means.at[z, spot], means.at[z, spot], zsend.at[k - 1], zrecv.at[k - 1], device)

    def spread(origin):
        for j in range(1, PLANE):
            device = (z * PLANE + lax.rem(spot + j, PLANE), x)
            remote(
                means.at[origin, spot], means.at[origin, spot],
                psend.at[j - 1], precv.at[j - 1], device,
            ).start()

    spread(z)
    for k in (1, 7, 2, 6, 3, 5, 4):
        origin = lax.rem(z + NZ - k, NZ)
        arrived(means.at[origin, spot], zsend.at[k - 1], zrecv.at[k - 1])
        spread(origin)
    for j in range(1, PLANE):
        origin = lax.rem(spot + PLANE - j, PLANE)
        arrived(means.at[:, origin], psend.at[j - 1], precv.at[j - 1])
    out_ref[...] = means[...]

    for copy in started:
        copy.wait_send()
    for j in range(1, PLANE):
        device = (z * PLANE + lax.rem(spot + j, PLANE), x)
        remote(
            means.at[:, spot], means.at[:, spot], psend.at[j - 1], precv.at[j - 1], device
        ).wait_send()

    @pl.when(core == 1)
    def _():
        to_core0.wait_send()

    @pl.when(core == 0)
    def _():
        for copy in ring + ring_relay + [to_core1]:
            copy.wait_send()

    @pl.when(jnp.logical_and(core == 0, z < NZ - 1))
    def _():
        for copy in steps:
            copy.wait_send()


def filtered_means(obs_rows, obs_values, obs_hours, prior_precision, transition):
    any_space = pl.BlockSpec(memory_space=pltpu.MemorySpace.HBM)
    dma = pltpu.SemaphoreType.DMA
    return pl.pallas_call(
        kernel,
        out_shape=jax.ShapeDtypeStruct((NZ, PLANE, HR, S), BF16),
        in_specs=[any_space] * 5,
        out_specs=pl.BlockSpec(memory_space=pltpu.VMEM),
        scratch_shapes=[
            pltpu.VMEM((4, 2, 256, S), BF16),
            pltpu.VMEM((4, 4, 128), BF16),
            pltpu.VMEM((4, 1, 512), jnp.int32),
            pltpu.VMEM((S, S), F32),
            pltpu.VMEM((S, S), F32),
            pltpu.VMEM((S, S), F32),
            pltpu.VMEM((S, S), F32),
            pltpu.VMEM((HR, S, S), F32),
            pltpu.VMEM((PAD, S), F32),
            pltpu.VMEM((HR, 2 * S + PAD, S), F32),
            pltpu.VMEM((HR, ROWS, S), F32),
            pltpu.VMEM((ROWS, S), F32),
            pltpu.VMEM((NY, 2, 128, S), BF16),
            pltpu.VMEM((NY, 8, S), F32),
            pltpu.VMEM((NY + 1, ROWS, S), F32),
            pltpu.VMEM((ROWS, S), F32),
            pltpu.VMEM((ROWS, S), F32),
            pltpu.VMEM((2, S, S), BF16),
            pltpu.VMEM((HR, S, S), BF16),
            pltpu.VMEM((HR, S, S), BF16),
            pltpu.VMEM((HR, 8, S), F32),
            pltpu.VMEM((1, S), F32),
            pltpu.VMEM((1, S), F32),
            pltpu.VMEM((NZ, PLANE, HR, S), BF16),
            dma((6,)),
            dma((3, 2)), dma((3, 2)),
            dma((2, 3)), dma((2, 3)),
            dma(()), dma(()),
            dma((3, 2)), dma((3, 2)),
            dma((3,)), dma((3,)),
            dma((2,)), dma(()),
            dma((8,)), dma((8,)),
            dma((7,)), dma((7,)),
            pltpu.SemaphoreType.REGULAR((6,)),
        ],
        compiler_params=pltpu.CompilerParams(
            collective_id=0, has_side_effects=True, vmem_limit_bytes=32 * 1024 * 1024
        ),
    )(*(
        pltpu.with_memory_space_constraint(a, pltpu.MemorySpace.HBM)
        for a in (obs_rows, obs_values.reshape(4, 128), obs_hours[None], prior_precision, transition)
    ))


def body(obs_rows, obs_values, obs_hours, prior_precision, transition, site_basis):
    means = filtered_means(obs_rows, obs_values, obs_hours, prior_precision, transition)
    return jnp.einsum(
        "hs,ns->hn", means.reshape(NZ * PLANE * HR, S), site_basis, preferred_element_type=F32
    ).astype(BF16)


def solution(mesh):
    in_specs = (
        P(("tm", "site"), None),
        P(("tm", "site")),
        P(("tm", "site")),
        P(),
        P(),
        P(("tm", "site"), None),
    )
    out_specs = P(None, ("tm", "site"))
    return jax.shard_map(body, mesh=mesh, in_specs=in_specs, out_specs=out_specs, check_vma=False)
```

```python
import jax
import jax.numpy as jnp
from jax import lax
from jax.experimental import pallas as pl
from jax.experimental.pallas import tpu as pltpu
from jax.sharding import PartitionSpec as P

F32, BF16 = jnp.float32, jnp.bfloat16
MESH = pl.DeviceIdType.MESH

S = 256
NS_ITERS = 8
HR = 4
PAD = 16
ROWS = S + PAD
NX, NY, NC, NZ = 4, 4, 2, 8
PLANE = NY * NC


def split(a):
    high = a.astype(BF16)
    return high, (a - high.astype(F32)).astype(BF16)


def mm(a, b):
    return jnp.dot(a, b, preferred_element_type=F32)


def dot3(a, b):
    ah, al = a
    bh, bl = b
    return mm(ah, bh) + mm(al, bh) + mm(ah, bl)


def wide(row):
    return jnp.broadcast_to(row, (PAD, S))


def kernel(
    rows_hbm, vals_hbm, hours_hbm, prior_hbm, trans_hbm,
    out_ref,
    xs, vs, hs, prior, trans, coupled, power, grams, drives, work, prefix, partner,
    ydiff, yoff, pre, full, handed, planemap, planeoff, lower, lowermap, entry,
    qhi, qlo, qoff, sin, sout, means,
    load_sem, xsend, xrecv, asend, arecv, csend, crecv, ysend, yrecv, osend, orecv,
    ssend, srecv, psend, precv, zsend, zrecv, msend, mrecv, heard,
):
    tm = lax.axis_index("tm")
    x = lax.axis_index("site")
    spot = lax.rem(tm, PLANE)
    core = lax.rem(tm, NC)
    y = lax.div(spot, NC)
    z = lax.div(tm, PLANE)

    def at(zz, yy, cc):
        return zz * PLANE + yy * NC + cc

    loads = [
        pltpu.make_async_copy(rows_hbm.at[pl.ds(0, 256)], xs.at[3, 0], load_sem.at[0]),
        pltpu.make_async_copy(rows_hbm.at[pl.ds(256, 256)], xs.at[3, 1], load_sem.at[1]),
        pltpu.make_async_copy(vals_hbm, vs.at[3], load_sem.at[2]),
        pltpu.make_async_copy(hours_hbm, hs.at[3], load_sem.at[3]),
        pltpu.make_async_copy(prior_hbm, prior, load_sem.at[4]),
        pltpu.make_async_copy(trans_hbm, trans, load_sem.at[5]),
    ]
    for copy in loads:
        copy.start()

    barrier = pltpu.get_barrier_semaphore()
    near = [(at(z, y, 1 - core), x)]
    near += [(at(z, lax.rem(y + k, NY), core), x) for k in (1, NY - 1)]
    beside = [(tm, lax.rem(x + k, NX)) for k in (1, NX - 1)]
    inner = jnp.where(z > 0, 1, 0) + jnp.where(z < NZ - 1, 1, 0)

    def greet(sem, devices):
        for device in devices:
            pl.semaphore_signal(sem, inc=1, device_id=device, device_id_type=MESH)

        @pl.when(z > 0)
        def _():
            pl.semaphore_signal(sem, inc=1, device_id=(tm - PLANE, x), device_id_type=MESH)

        @pl.when(z < NZ - 1)
        def _():
            pl.semaphore_signal(sem, inc=1, device_id=(tm + PLANE, x), device_id_type=MESH)

    greet(barrier, beside + near)
    pl.semaphore_wait(barrier, len(beside + near) + inner)

    def tell(turn):
        greet(heard.at[turn], near)

    def hear(turn):
        pl.semaphore_wait(heard.at[turn], len(near) + inner)

    started = []

    def remote(src, dst, send_sem, recv_sem, device):
        return pltpu.make_async_remote_copy(
            src_ref=src, dst_ref=dst, send_sem=send_sem, recv_sem=recv_sem,
            device_id=device, device_id_type=MESH,
        )

    def send(*args):
        copy = remote(*args)
        copy.start()
        started.append(copy)

    def arrived(ref, send_sem, recv_sem):
        remote(ref, ref, send_sem, recv_sem, (tm, x)).wait_recv()

    right, left = ((tm, lax.rem(x + k, NX)) for k in (1, 3))
    for half in (0, 1):
        part = rows_hbm.at[pl.ds(half * 256, 256)]
        send(part, xs.at[0, half], xsend.at[0, half], xrecv.at[0, half], right)
        part = rows_hbm.at[pl.ds((1 - half) * 256, 256)]
        send(part, xs.at[1, 1 - half], xsend.at[1, 1 - half], xrecv.at[1, 1 - half], left)
    for slot, device in ((0, right), (1, left)):
        send(vals_hbm, vs.at[slot], asend.at[0, slot], arecv.at[0, slot], device)
        send(hours_hbm, hs.at[slot], asend.at[1, slot], arecv.at[1, slot], device)
    tell(0)

    for copy in loads:
        copy.wait()

    transposed = trans[...].T
    coupled[...] = dot3(split(transposed), split(prior[...]))
    power[...] = transposed
    for _ in range(3):
        parts = split(power[...])
        power[...] = dot3(parts, parts)

    def add_rows(slot, first):
        hour = hs[slot]
        value = vs[slot].astype(F32)
        value = jnp.concatenate([value[i:i + 1] for i in range(4)], axis=1)
        sub = lax.broadcasted_iota(jnp.int32, (PAD, 512), 0)
        marked = jnp.where(sub == hour, value, 0.0).astype(BF16)
        shape = (2 * 256, S)
        block = xs[slot].reshape(shape)
        turned = block.T
        total = mm(marked, block)
        drives[...] = total if first else drives[...] + total
        for h in range(HR):
            member = jnp.where(hour == h, 1.0, 0.0).astype(BF16)
            product = mm(turned * member, block)
            grams[h] = product if first else grams[h] + product

    add_rows(3, True)
    hear(0)
    tell(1)
    arrived(xs.at[0, 0], xsend.at[0, 0], xrecv.at[0, 0])
    send(xs.at[0, 0], xs.at[2, 0], xsend.at[2, 0], xrecv.at[2, 0], right)
    arrived(xs.at[1, 1], xsend.at[1, 1], xrecv.at[1, 1])
    send(xs.at[1, 1], xs.at[2, 1], xsend.at[2, 1], xrecv.at[2, 1], left)
    for slot in range(2):
        arrived(vs.at[slot], asend.at[0, slot], arecv.at[0, slot])
        arrived(hs.at[slot], asend.at[1, slot], arecv.at[1, slot])
    send(vs.at[0], vs.at[2], asend.at[0, 2], arecv.at[0, 2], right)
    send(hs.at[0], hs.at[2], asend.at[1, 2], arecv.at[1, 2], right)
    arrived(xs.at[0, 1], xsend.at[0, 1], xrecv.at[0, 1])
    add_rows(0, False)
    arrived(xs.at[1, 0], xsend.at[1, 0], xrecv.at[1, 0])
    add_rows(1, False)
    arrived(vs.at[2], asend.at[0, 2], arecv.at[0, 2])
    arrived(hs.at[2], asend.at[1, 2], arecv.at[1, 2])
    arrived(xs.at[2, 0], xsend.at[2, 0], xrecv.at[2, 0])
    arrived(xs.at[2, 1], xsend.at[2, 1], xrecv.at[2, 1])
    add_rows(2, False)

    hear(1)
    tell(2)
    eye = (
        lax.broadcasted_iota(jnp.int32, (S, S), 0) == lax.broadcasted_iota(jnp.int32, (S, S), 1)
    ).astype(F32)
    for h in range(HR):
        lam = prior[...] + grams[h]
        bound = jnp.max(jnp.sum(jnp.abs(lam), axis=0, keepdims=True), axis=1, keepdims=True)
        scale = 1.0 / bound
        work[h, 0:S] = eye - lam * scale
        work[h, S:2 * S] = coupled[...] * scale
        work[h, 2 * S:2 * S + PAD] = drives[...] * scale

    def level(k, carry):
        for h in range(HR):
            held = work[h]
            parts = split(held)
            factor = (parts[0][0:S], parts[1][0:S])
            product = dot3(parts, factor)
            work[h, 0:S] = product[0:S]
            work[h, S:2 * S + PAD] = held[S:2 * S + PAD] + product[S:2 * S + PAD]

        @pl.when(lax.rem(k, 2) == 1)
        def _():
            turn = 2 + lax.div(k, 2)
            hear(turn)
            tell(turn + 1)

        return carry

    lax.fori_loop(0, NS_ITERS, level, 0)

    prefix[0, 0:S] = work[0, S:2 * S]
    prefix[0, S:ROWS] = wide(work[0, 2 * S:2 * S + 1])
    for h in range(1, HR):
        joined = dot3(split(prefix[h - 1]), split(work[h, S:2 * S]))
        prefix[h, 0:S] = joined[0:S]
        prefix[h, S:ROWS] = joined[S:ROWS] + wide(work[h, 2 * S + h:2 * S + h + 1])

    def after(earlier, later_map, later_off):
        joined = dot3(split(earlier), split(later_map))
        return joined[0:S], joined[S:ROWS] + wide(later_off)

    to_core0 = remote(prefix.at[HR - 1], partner, csend, crecv, (at(z, y, 0), x))
    to_core1 = remote(handed, full, psend.at[7], precv.at[7], (at(z, y, 1), x))

    def to_ring(src, dst, s, r, device):
        return remote(src, dst, s, r, device)

    y_right, y_left, y_across = ((at(z, lax.rem(y + k, NY), 0), x) for k in (1, 3, 2))
    ring = []
    for half in (0, 1):
        ring.append(to_ring(ydiff.at[y, half], ydiff.at[y, half], ysend.at[0, half], yrecv.at[0, half], y_right))
        ring.append(to_ring(ydiff.at[y, 1 - half], ydiff.at[y, 1 - half], ysend.at[1, 1 - half], yrecv.at[1, 1 - half], y_left))
    for slot, device in ((0, y_right), (1, y_left), (2, y_across)):
        ring.append(to_ring(yoff.at[y], yoff.at[y], osend.at[slot], orecv.at[slot], device))
    behind, ahead, opposite = (lax.rem(y + k, NY) for k in (3, 1, 2))
    ring_relay = [
        to_ring(ydiff.at[behind, 0], ydiff.at[behind, 0], ysend.at[2, 0], yrecv.at[2, 0], y_right),
        to_ring(ydiff.at[ahead, 1], ydiff.at[ahead, 1], ysend.at[2, 1], yrecv.at[2, 1], y_left),
    ]
    def state_to(slot, zz, cc):
        return remote(sout, sin, ssend.at[slot], srecv, (at(jnp.minimum(zz, NZ - 1), y, cc), x))

    steps = [state_to(0, z + 1, 0), state_to(1, z + 1, 1)]
    far_steps = [state_to(2, z + 2, 0), state_to(3, z + 2, 1)]
    to_odd = [
        remote(pre.at[NY], lower, msend.at[c], mrecv, (at(jnp.minimum(z + 1, NZ - 1), y, c), x))
        for c in range(NC)
    ]
    odd = lax.rem(z, 2) == 1
    paired = jnp.logical_and(odd, z >= 3)
    lends = jnp.logical_and(jnp.logical_not(odd), z >= 2)
    sends_state = jnp.logical_or(z == 0, jnp.logical_and(odd, z < NZ - 1))
    sends_far = jnp.logical_and(odd, z < NZ - 1)

    def ready_means():
        for h in range(HR):
            m, o = after(full[...], prefix[h, 0:S], prefix[h, S:S + 1])
            high, low = split(m)
            qhi[h] = high
            qlo[h] = low
            qoff[h] = o[0:8]

    def apply(state, high, low):
        sh, sl = split(wide(state))
        both = mm(jnp.concatenate([sh, sl], axis=0), high)
        return both[0:1] + both[PAD:PAD + 1] + mm(sh, low)[0:1]

    @pl.when(core == 1)
    def _():
        to_core0.start()

    @pl.when(core == 0)
    def _():
        arrived(partner, csend, crecv)
        m, o = after(prefix[HR - 1], partner[0:S], partner[S:S + 1])
        diff = (power[...] - m).astype(BF16)
        ydiff[y, 0] = diff[0:128]
        ydiff[y, 1] = diff[128:256]
        yoff[y] = o[0:8]
        for copy in ring:
            copy.start()

    hear(6)
    tell(7)

    @pl.when(core == 1)
    def _():
        hear(7)
        tell(8)
        arrived(full, psend.at[7], precv.at[7])

    @pl.when(core == 0)
    def _():
        arrived(ydiff.at[behind, 0], ysend.at[0, 0], yrecv.at[0, 0])
        ring_relay[0].start()
        arrived(ydiff.at[ahead, 1], ysend.at[1, 1], yrecv.at[1, 1])
        ring_relay[1].start()
        hear(7)
        tell(8)
        arrived(ydiff.at[behind, 1], ysend.at[0, 1], yrecv.at[0, 1])
        arrived(ydiff.at[ahead, 0], ysend.at[1, 0], yrecv.at[1, 0])
        arrived(ydiff.at[opposite, 0], ysend.at[2, 0], yrecv.at[2, 0])
        arrived(ydiff.at[opposite, 1], ysend.at[2, 1], yrecv.at[2, 1])
        for slot, origin in ((0, behind), (1, ahead), (2, opposite)):
            arrived(yoff.at[origin], osend.at[slot], orecv.at[slot])

        def chip(j):
            return power[...] - ydiff[j].reshape(S, S).astype(F32), yoff[j, 0:1]

        pre[0, 0:S] = eye
        pre[0, S:ROWS] = jnp.zeros((PAD, S), F32)
        m, o = chip(0)
        pre[1, 0:S] = m
        pre[1, S:ROWS] = wide(o)
        for j in (1, 2, 3):
            m, o = after(pre[j], *chip(j))
            pre[j + 1, 0:S] = m
            pre[j + 1, S:ROWS] = o

        @pl.when(z == 0)
        def _():
            sout[...] = pre[NY, S:S + 1]
            for copy in steps:
                copy.start()

        @pl.when(lends)
        def _():
            for copy in to_odd:
                copy.start()

        @pl.when(z == 1)
        def _():
            high, low = split(pre[NY, 0:S])
            planemap[0] = high
            planemap[1] = low
            planeoff[...] = pre[NY, S:S + 1]

        full[...] = pre[y]
        m, o = after(pre[y], prefix[HR - 1, 0:S], prefix[HR - 1, S:S + 1])
        handed[0:S] = m
        handed[S:ROWS] = o
        to_core1.start()

    hear(8)
    @pl.when(z >= 2)
    def _():
        ready_means()

    @pl.when(paired)
    def _():
        arrived(lower, msend.at[0], mrecv)
        high, low = split(lower[0:S])
        lowermap[0] = high
        lowermap[1] = low

    @pl.when(jnp.logical_and(paired, core == 0))
    def _():
        m, o = after(lower[...], pre[NY, 0:S], pre[NY, S:S + 1])
        high, low = split(m)
        planemap[0] = high
        planemap[1] = low
        planeoff[...] = o[0:1]

    @pl.when(z == 0)
    def _():
        sin[...] = jnp.zeros((1, S), F32)

    @pl.when(z > 0)
    def _():
        arrived(sin, ssend.at[0], srecv)

    entry[...] = sin[...]

    @pl.when(jnp.logical_and(core == 0, sends_far))
    def _():
        sout[...] = apply(sin[...], planemap[0], planemap[1]) + planeoff[...]
        for copy in far_steps + steps:
            copy.start()

    @pl.when(paired)
    def _():
        entry[...] = apply(sin[...], lowermap[0], lowermap[1]) + lower[S:S + 1]

    @pl.when(z < 2)
    def _():
        ready_means()

    found = [apply(entry[...], qhi[h], qlo[h]) + qoff[h, 0:1] for h in range(HR)]
    means[z, spot] = jnp.concatenate(found, axis=0).astype(BF16)

    mine = means.at[z, spot]
    for k in (4, 3, 5, 2, 6, 1, 7):
        zz = lax.rem(z + k, NZ)
        for j in range(PLANE):
            device = (zz * PLANE + lax.rem(spot + j, PLANE), x)
            remote(mine, mine, zsend.at[k - 1], zrecv.at[k - 1], device).start()
    for j in range(1, PLANE):
        device = (z * PLANE + lax.rem(spot + j, PLANE), x)
        send(mine, mine, psend.at[j - 1], precv.at[j - 1], device)
    for j in range(1, PLANE):
        origin = lax.rem(spot + PLANE - j, PLANE)
        arrived(means.at[z, origin], psend.at[j - 1], precv.at[j - 1])
    for k in (1, 7, 2, 6, 3, 5, 4):
        origin = lax.rem(z + NZ - k, NZ)
        arrived(means.at[origin], zsend.at[k - 1], zrecv.at[k - 1])
    out_ref[...] = means[...]

    for copy in started:
        copy.wait_send()
    for k in range(1, NZ):
        device = (lax.rem(z + k, NZ) * PLANE + spot, x)
        remote(means.at[z], means.at[z], zsend.at[k - 1], zrecv.at[k - 1], device).wait_send()

    @pl.when(core == 1)
    def _():
        to_core0.wait_send()

    @pl.when(core == 0)
    def _():
        for copy in ring + ring_relay + [to_core1]:
            copy.wait_send()

    @pl.when(jnp.logical_and(core == 0, sends_state))
    def _():
        for copy in steps:
            copy.wait_send()

    @pl.when(jnp.logical_and(core == 0, sends_far))
    def _():
        for copy in far_steps:
            copy.wait_send()

    @pl.when(jnp.logical_and(core == 0, lends))
    def _():
        for copy in to_odd:
            copy.wait_send()


def filtered_means(obs_rows, obs_values, obs_hours, prior_precision, transition):
    any_space = pl.BlockSpec(memory_space=pltpu.MemorySpace.HBM)
    dma = pltpu.SemaphoreType.DMA
    return pl.pallas_call(
        kernel,
        out_shape=jax.ShapeDtypeStruct((NZ, PLANE, HR, S), BF16),
        in_specs=[any_space] * 5,
        out_specs=pl.BlockSpec(memory_space=pltpu.VMEM),
        scratch_shapes=[
            pltpu.VMEM((4, 2, 256, S), BF16),
            pltpu.VMEM((4, 4, 128), BF16),
            pltpu.VMEM((4, 1, 512), jnp.int32),
            pltpu.VMEM((S, S), F32),
            pltpu.VMEM((S, S), F32),
            pltpu.VMEM((S, S), F32),
            pltpu.VMEM((S, S), F32),
            pltpu.VMEM((HR, S, S), F32),
            pltpu.VMEM((PAD, S), F32),
            pltpu.VMEM((HR, 2 * S + PAD, S), F32),
            pltpu.VMEM((HR, ROWS, S), F32),
            pltpu.VMEM((ROWS, S), F32),
            pltpu.VMEM((NY, 2, 128, S), BF16),
            pltpu.VMEM((NY, 8, S), F32),
            pltpu.VMEM((NY + 1, ROWS, S), F32),
            pltpu.VMEM((ROWS, S), F32),
            pltpu.VMEM((ROWS, S), F32),
            pltpu.VMEM((2, S, S), BF16),
            pltpu.VMEM((1, S), F32),
            pltpu.VMEM((ROWS, S), F32),
            pltpu.VMEM((2, S, S), BF16),
            pltpu.VMEM((1, S), F32),
            pltpu.VMEM((HR, S, S), BF16),
            pltpu.VMEM((HR, S, S), BF16),
            pltpu.VMEM((HR, 8, S), F32),
            pltpu.VMEM((1, S), F32),
            pltpu.VMEM((1, S), F32),
            pltpu.VMEM((NZ, PLANE, HR, S), BF16),
            dma((6,)),
            dma((3, 2)), dma((3, 2)),
            dma((2, 3)), dma((2, 3)),
            dma(()), dma(()),
            dma((3, 2)), dma((3, 2)),
            dma((3,)), dma((3,)),
            dma((4,)), dma(()),
            dma((8,)), dma((8,)),
            dma((7,)), dma((7,)),
            dma((2,)), dma(()),
            pltpu.SemaphoreType.REGULAR((9,)),
        ],
        compiler_params=pltpu.CompilerParams(
            collective_id=0, has_side_effects=True, vmem_limit_bytes=32 * 1024 * 1024
        ),
    )(*(
        pltpu.with_memory_space_constraint(a, pltpu.MemorySpace.HBM)
        for a in (obs_rows, obs_values.reshape(4, 128), obs_hours[None], prior_precision, transition)
    ))


def body(obs_rows, obs_values, obs_hours, prior_precision, transition, site_basis):
    means = filtered_means(obs_rows, obs_values, obs_hours, prior_precision, transition)
    return jnp.einsum(
        "hs,ns->hn", means.reshape(NZ * PLANE * HR, S), site_basis, preferred_element_type=F32
    ).astype(BF16)


def solution(mesh):
    in_specs = (
        P(("tm", "site"), None),
        P(("tm", "site")),
        P(("tm", "site")),
        P(),
        P(),
        P(("tm", "site"), None),
    )
    out_specs = P(None, ("tm", "site"))
    return jax.shard_map(body, mesh=mesh, in_specs=in_specs, out_specs=out_specs, check_vma=False)
```

```python
import jax
import jax.numpy as jnp
from jax import lax
from jax.experimental import pallas as pl
from jax.experimental.pallas import tpu as pltpu
from jax.sharding import PartitionSpec as P

F32, BF16 = jnp.float32, jnp.bfloat16
MESH = pl.DeviceIdType.MESH

S = 256
NS_ITERS = 8
HR = 4
PAD = 16
ROWS = S + PAD
NX, NY, NC, NZ = 4, 4, 2, 8
PLANE = NY * NC


def split(a):
    high = a.astype(BF16)
    return high, (a - high.astype(F32)).astype(BF16)


def mm(a, b):
    return jnp.dot(a, b, preferred_element_type=F32)


def dot3(a, b):
    ah, al = a
    bh, bl = b
    return mm(ah, bh) + mm(al, bh) + mm(ah, bl)


def wide(row):
    return jnp.broadcast_to(row, (PAD, S))


def kernel(
    rows_hbm, vals_hbm, hours_hbm, prior_hbm, trans_hbm,
    out_ref,
    xs, vs, hs, prior, trans, coupled, power, grams, drives, work, prefix, partner,
    ydiff, yoff, pre, full, handed, planemap, planeoff, lower, lowermap, entry,
    qhi, qlo, qoff, sin, sout, means,
    load_sem, xsend, xrecv, asend, arecv, csend, crecv, ysend, yrecv, osend, orecv,
    ssend, srecv, psend, precv, zsend, zrecv, msend, mrecv, heard,
):
    tm = lax.axis_index("tm")
    x = lax.axis_index("site")
    spot = lax.rem(tm, PLANE)
    core = lax.rem(tm, NC)
    y = lax.div(spot, NC)
    z = lax.div(tm, PLANE)

    def at(zz, yy, cc):
        return zz * PLANE + yy * NC + cc

    loads = [
        pltpu.make_async_copy(rows_hbm.at[pl.ds(0, 256)], xs.at[3, 0], load_sem.at[0]),
        pltpu.make_async_copy(rows_hbm.at[pl.ds(256, 256)], xs.at[3, 1], load_sem.at[1]),
        pltpu.make_async_copy(vals_hbm, vs.at[3], load_sem.at[2]),
        pltpu.make_async_copy(hours_hbm, hs.at[3], load_sem.at[3]),
        pltpu.make_async_copy(prior_hbm, prior, load_sem.at[4]),
        pltpu.make_async_copy(trans_hbm, trans, load_sem.at[5]),
    ]
    for copy in loads:
        copy.start()

    barrier = pltpu.get_barrier_semaphore()
    near = [(at(z, y, 1 - core), x)]
    near += [(at(z, lax.rem(y + k, NY), core), x) for k in (1, NY - 1)]
    beside = [(tm, lax.rem(x + k, NX)) for k in (1, NX - 1)]
    inner = jnp.where(z > 0, 1, 0) + jnp.where(z < NZ - 1, 1, 0)

    def greet(sem, devices):
        for device in devices:
            pl.semaphore_signal(sem, inc=1, device_id=device, device_id_type=MESH)

        @pl.when(z > 0)
        def _():
            pl.semaphore_signal(sem, inc=1, device_id=(tm - PLANE, x), device_id_type=MESH)

        @pl.when(z < NZ - 1)
        def _():
            pl.semaphore_signal(sem, inc=1, device_id=(tm + PLANE, x), device_id_type=MESH)

    greet(barrier, beside + near)
    pl.semaphore_wait(barrier, len(beside + near) + inner)

    def tell(turn):
        greet(heard.at[turn], near)

    def hear(turn):
        pl.semaphore_wait(heard.at[turn], len(near) + inner)

    started = []

    def remote(src, dst, send_sem, recv_sem, device):
        return pltpu.make_async_remote_copy(
            src_ref=src, dst_ref=dst, send_sem=send_sem, recv_sem=recv_sem,
            device_id=device, device_id_type=MESH,
        )

    def send(*args):
        copy = remote(*args)
        copy.start()
        started.append(copy)

    def arrived(ref, send_sem, recv_sem):
        remote(ref, ref, send_sem, recv_sem, (tm, x)).wait_recv()

    right, left = ((tm, lax.rem(x + k, NX)) for k in (1, 3))
    for half in (0, 1):
        part = rows_hbm.at[pl.ds(half * 256, 256)]
        send(part, xs.at[0, half], xsend.at[0, half], xrecv.at[0, half], right)
        part = rows_hbm.at[pl.ds((1 - half) * 256, 256)]
        send(part, xs.at[1, 1 - half], xsend.at[1, 1 - half], xrecv.at[1, 1 - half], left)
    for slot, device in ((0, right), (1, left)):
        send(vals_hbm, vs.at[slot], asend.at[0, slot], arecv.at[0, slot], device)
        send(hours_hbm, hs.at[slot], asend.at[1, slot], arecv.at[1, slot], device)
    tell(0)

    for copy in loads:
        copy.wait()

    transposed = trans[...].T
    coupled[...] = dot3(split(transposed), split(prior[...]))
    power[...] = transposed
    for _ in range(3):
        parts = split(power[...])
        power[...] = dot3(parts, parts)

    def add_rows(slot, first):
        hour = hs[slot]
        value = vs[slot].astype(F32)
        value = jnp.concatenate([value[i:i + 1] for i in range(4)], axis=1)
        sub = lax.broadcasted_iota(jnp.int32, (PAD, 512), 0)
        marked = jnp.where(sub == hour, value, 0.0).astype(BF16)
        shape = (2 * 256, S)
        block = xs[slot].reshape(shape)
        turned = block.T
        total = mm(marked, block)
        drives[...] = total if first else drives[...] + total
        for h in range(HR):
            member = jnp.where(hour == h, 1.0, 0.0).astype(BF16)
            product = mm(turned * member, block)
            grams[h] = product if first else grams[h] + product

    add_rows(3, True)
    hear(0)
    tell(1)
    arrived(xs.at[0, 0], xsend.at[0, 0], xrecv.at[0, 0])
    send(xs.at[0, 0], xs.at[2, 0], xsend.at[2, 0], xrecv.at[2, 0], right)
    arrived(xs.at[1, 1], xsend.at[1, 1], xrecv.at[1, 1])
    send(xs.at[1, 1], xs.at[2, 1], xsend.at[2, 1], xrecv.at[2, 1], left)
    for slot in range(2):
        arrived(vs.at[slot], asend.at[0, slot], arecv.at[0, slot])
        arrived(hs.at[slot], asend.at[1, slot], arecv.at[1, slot])
    send(vs.at[0], vs.at[2], asend.at[0, 2], arecv.at[0, 2], right)
    send(hs.at[0], hs.at[2], asend.at[1, 2], arecv.at[1, 2], right)
    arrived(xs.at[0, 1], xsend.at[0, 1], xrecv.at[0, 1])
    add_rows(0, False)
    arrived(xs.at[1, 0], xsend.at[1, 0], xrecv.at[1, 0])
    add_rows(1, False)
    arrived(vs.at[2], asend.at[0, 2], arecv.at[0, 2])
    arrived(hs.at[2], asend.at[1, 2], arecv.at[1, 2])
    arrived(xs.at[2, 0], xsend.at[2, 0], xrecv.at[2, 0])
    arrived(xs.at[2, 1], xsend.at[2, 1], xrecv.at[2, 1])
    add_rows(2, False)

    hear(1)
    tell(2)
    eye = (
        lax.broadcasted_iota(jnp.int32, (S, S), 0) == lax.broadcasted_iota(jnp.int32, (S, S), 1)
    ).astype(F32)
    for h in range(HR):
        lam = prior[...] + grams[h]
        bound = jnp.max(jnp.sum(jnp.abs(lam), axis=0, keepdims=True), axis=1, keepdims=True)
        scale = 1.0 / bound
        work[h, 0:S] = eye - lam * scale
        work[h, S:2 * S] = coupled[...] * scale
        work[h, 2 * S:2 * S + PAD] = drives[...] * scale

    def level(k, carry):
        for h in range(HR):
            held = work[h]
            parts = split(held)
            factor = (parts[0][0:S], parts[1][0:S])
            product = dot3(parts, factor)
            work[h, 0:S] = product[0:S]
            work[h, S:2 * S + PAD] = held[S:2 * S + PAD] + product[S:2 * S + PAD]

        @pl.when(lax.rem(k, 2) == 1)
        def _():
            turn = 2 + lax.div(k, 2)
            hear(turn)
            tell(turn + 1)

        return carry

    lax.fori_loop(0, NS_ITERS - 2, level, 0)

    def closing(h, last):
        held = work[h]
        high, low = split(held)
        factor = high[0:S]
        maps = jnp.concatenate([high[S:2 * S + PAD], low[S:2 * S + PAD]], axis=0)
        both = mm(maps, factor)
        if not last:
            square = (factor, low[0:S])
            work[h, 0:S] = dot3(square, square)
        work[h, S:2 * S + PAD] = held[S:2 * S + PAD] + both[0:ROWS] + both[ROWS:2 * ROWS]

    for h in range(HR):
        closing(h, False)
    hear(5)
    tell(6)
    for h in range(HR):
        closing(h, True)

    def after(earlier, later_map, later_off):
        joined = dot3(split(earlier), split(later_map))
        return joined[0:S], joined[S:ROWS] + wide(later_off)

    def hour(h):
        return work[h, S:2 * S], work[h, 2 * S + h:2 * S + h + 1]

    def put(ref, mapped):
        ref[0:S] = mapped[0]
        ref[S:ROWS] = mapped[1]

    for h in (0, 2):
        put(prefix.at[h], (hour(h)[0], wide(hour(h)[1])))
    put(prefix.at[1], after(prefix[0], *hour(1)))
    put(handed, after(prefix[2], *hour(3)))
    put(prefix.at[3], after(prefix[1], handed[0:S], handed[S:S + 1]))

    to_core0 = remote(prefix.at[HR - 1], partner, csend, crecv, (at(z, y, 0), x))
    to_core1 = remote(handed, full, psend.at[7], precv.at[7], (at(z, y, 1), x))

    y_right, y_left, y_across = ((at(z, lax.rem(y + k, NY), 0), x) for k in (1, 3, 2))
    ring = []
    for slot, device in ((2, y_across), (0, y_right), (1, y_left)):
        ring.append(remote(yoff.at[y], yoff.at[y], osend.at[slot], orecv.at[slot], device))
        ring.append(remote(ydiff.at[y], ydiff.at[y], ysend.at[slot], yrecv.at[slot], device))
    behind, ahead, opposite = (lax.rem(y + k, NY) for k in (3, 1, 2))
    def state_to(slot, zz, cc):
        return remote(sout, sin, ssend.at[slot], srecv, (at(jnp.minimum(zz, NZ - 1), y, cc), x))

    steps = [state_to(0, z + 1, 0), state_to(1, z + 1, 1)]
    far_steps = [state_to(2, z + 2, 0), state_to(3, z + 2, 1)]
    to_odd = [
        remote(pre.at[NY], lower, msend.at[c], mrecv, (at(jnp.minimum(z + 1, NZ - 1), y, c), x))
        for c in range(NC)
    ]
    odd = lax.rem(z, 2) == 1
    paired = jnp.logical_and(odd, z >= 3)
    lends = jnp.logical_and(jnp.logical_not(odd), z >= 2)
    sends_state = jnp.logical_or(z == 0, jnp.logical_and(odd, z < NZ - 1))
    sends_far = jnp.logical_and(odd, z < NZ - 1)

    def ready_means():
        for h in range(HR):
            m, o = after(full[...], prefix[h, 0:S], prefix[h, S:S + 1])
            high, low = split(m)
            qhi[h] = high
            qlo[h] = low
            qoff[h] = o[0:8]

    def apply(state, high, low):
        sh, sl = split(wide(state))
        both = mm(jnp.concatenate([sh, sl], axis=0), high)
        return both[0:1] + both[PAD:PAD + 1] + mm(sh, low)[0:1]

    @pl.when(core == 1)
    def _():
        to_core0.start()

    @pl.when(core == 0)
    def _():
        arrived(partner, csend, crecv)
        m, o = after(prefix[HR - 1], partner[0:S], partner[S:S + 1])
        ydiff[y] = (power[...] - m).astype(BF16)
        yoff[y] = o[0:8]
        for copy in ring:
            copy.start()

    hear(6)
    tell(7)

    put(prefix.at[2], after(prefix[1], *hour(2)))
    hear(7)
    tell(8)

    @pl.when(core == 1)
    def _():
        arrived(full, psend.at[7], precv.at[7])

    @pl.when(core == 0)
    def _():
        for slot, origin in ((0, behind), (1, ahead), (2, opposite)):
            arrived(yoff.at[origin], osend.at[slot], orecv.at[slot])
            arrived(ydiff.at[origin], ysend.at[slot], yrecv.at[slot])

        def chip(j):
            return power[...] - ydiff[j].astype(F32), yoff[j, 0:1]

        put(pre.at[0], (eye, jnp.zeros((PAD, S), F32)))
        m, o = chip(0)
        put(pre.at[1], (m, wide(o)))
        put(pre.at[2], after(pre[1], *chip(1)))
        m, o = chip(2)
        put(pre.at[3], (m, wide(o)))
        put(handed, after(pre[3], *chip(3)))
        put(pre.at[4], after(pre[2], handed[0:S], handed[S:S + 1]))

        @pl.when(z == 0)
        def _():
            sout[...] = pre[NY, S:S + 1]
            for copy in steps:
                copy.start()

        @pl.when(lends)
        def _():
            for copy in to_odd:
                copy.start()

        @pl.when(z == 1)
        def _():
            high, low = split(pre[NY, 0:S])
            planemap[0] = high
            planemap[1] = low
            planeoff[...] = pre[NY, S:S + 1]

        put(pre.at[3], after(pre[2], *chip(2)))
        full[...] = pre[y]
        put(handed, after(pre[y], prefix[HR - 1, 0:S], prefix[HR - 1, S:S + 1]))
        to_core1.start()

    hear(8)
    @pl.when(z >= 2)
    def _():
        ready_means()

    @pl.when(paired)
    def _():
        arrived(lower, msend.at[0], mrecv)
        high, low = split(lower[0:S])
        lowermap[0] = high
        lowermap[1] = low

    @pl.when(jnp.logical_and(paired, core == 0))
    def _():
        m, o = after(lower[...], pre[NY, 0:S], pre[NY, S:S + 1])
        high, low = split(m)
        planemap[0] = high
        planemap[1] = low
        planeoff[...] = o[0:1]

    @pl.when(z == 0)
    def _():
        sin[...] = jnp.zeros((1, S), F32)

    @pl.when(z > 0)
    def _():
        arrived(sin, ssend.at[0], srecv)

    entry[...] = sin[...]

    @pl.when(jnp.logical_and(core == 0, sends_far))
    def _():
        sout[...] = apply(sin[...], planemap[0], planemap[1]) + planeoff[...]
        for copy in far_steps + steps:
            copy.start()

    @pl.when(paired)
    def _():
        entry[...] = apply(sin[...], lowermap[0], lowermap[1]) + lower[S:S + 1]

    @pl.when(z < 2)
    def _():
        ready_means()

    found = [apply(entry[...], qhi[h], qlo[h]) + qoff[h, 0:1] for h in range(HR)]
    means[z, spot] = jnp.concatenate(found, axis=0).astype(BF16)

    mine = means.at[z, spot]
    for k in (4, 3, 5, 2, 6, 1, 7):
        zz = lax.rem(z + k, NZ)
        for j in range(PLANE):
            device = (zz * PLANE + lax.rem(spot + j, PLANE), x)
            remote(mine, mine, zsend.at[k - 1], zrecv.at[k - 1], device).start()
    for j in range(1, PLANE):
        device = (z * PLANE + lax.rem(spot + j, PLANE), x)
        send(mine, mine, psend.at[j - 1], precv.at[j - 1], device)
    for j in range(1, PLANE):
        origin = lax.rem(spot + PLANE - j, PLANE)
        arrived(means.at[z, origin], psend.at[j - 1], precv.at[j - 1])
    for k in (1, 7, 2, 6, 3, 5, 4):
        origin = lax.rem(z + NZ - k, NZ)
        arrived(means.at[origin], zsend.at[k - 1], zrecv.at[k - 1])
    out_ref[...] = means[...]

    for copy in started:
        copy.wait_send()
    for k in range(1, NZ):
        device = (lax.rem(z + k, NZ) * PLANE + spot, x)
        remote(means.at[z], means.at[z], zsend.at[k - 1], zrecv.at[k - 1], device).wait_send()

    @pl.when(core == 1)
    def _():
        to_core0.wait_send()

    @pl.when(core == 0)
    def _():
        for copy in ring + [to_core1]:
            copy.wait_send()

    @pl.when(jnp.logical_and(core == 0, sends_state))
    def _():
        for copy in steps:
            copy.wait_send()

    @pl.when(jnp.logical_and(core == 0, sends_far))
    def _():
        for copy in far_steps:
            copy.wait_send()

    @pl.when(jnp.logical_and(core == 0, lends))
    def _():
        for copy in to_odd:
            copy.wait_send()


def filtered_means(obs_rows, obs_values, obs_hours, prior_precision, transition):
    any_space = pl.BlockSpec(memory_space=pltpu.MemorySpace.HBM)
    dma = pltpu.SemaphoreType.DMA
    return pl.pallas_call(
        kernel,
        out_shape=jax.ShapeDtypeStruct((NZ, PLANE, HR, S), BF16),
        in_specs=[any_space] * 5,
        out_specs=pl.BlockSpec(memory_space=pltpu.VMEM),
        scratch_shapes=[
            pltpu.VMEM((4, 2, 256, S), BF16),
            pltpu.VMEM((4, 4, 128), BF16),
            pltpu.VMEM((4, 1, 512), jnp.int32),
            pltpu.VMEM((S, S), F32),
            pltpu.VMEM((S, S), F32),
            pltpu.VMEM((S, S), F32),
            pltpu.VMEM((S, S), F32),
            pltpu.VMEM((HR, S, S), F32),
            pltpu.VMEM((PAD, S), F32),
            pltpu.VMEM((HR, 2 * S + PAD, S), F32),
            pltpu.VMEM((HR, ROWS, S), F32),
            pltpu.VMEM((ROWS, S), F32),
            pltpu.VMEM((NY, S, S), BF16),
            pltpu.VMEM((NY, 8, S), F32),
            pltpu.VMEM((NY + 1, ROWS, S), F32),
            pltpu.VMEM((ROWS, S), F32),
            pltpu.VMEM((ROWS, S), F32),
            pltpu.VMEM((2, S, S), BF16),
            pltpu.VMEM((1, S), F32),
            pltpu.VMEM((ROWS, S), F32),
            pltpu.VMEM((2, S, S), BF16),
            pltpu.VMEM((1, S), F32),
            pltpu.VMEM((HR, S, S), BF16),
            pltpu.VMEM((HR, S, S), BF16),
            pltpu.VMEM((HR, 8, S), F32),
            pltpu.VMEM((1, S), F32),
            pltpu.VMEM((1, S), F32),
            pltpu.VMEM((NZ, PLANE, HR, S), BF16),
            dma((6,)),
            dma((3, 2)), dma((3, 2)),
            dma((2, 3)), dma((2, 3)),
            dma(()), dma(()),
            dma((3,)), dma((3,)),
            dma((3,)), dma((3,)),
            dma((4,)), dma(()),
            dma((8,)), dma((8,)),
            dma((7,)), dma((7,)),
            dma((2,)), dma(()),
            pltpu.SemaphoreType.REGULAR((9,)),
        ],
        compiler_params=pltpu.CompilerParams(
            collective_id=0, has_side_effects=True, vmem_limit_bytes=32 * 1024 * 1024
        ),
    )(*(
        pltpu.with_memory_space_constraint(a, pltpu.MemorySpace.HBM)
        for a in (obs_rows, obs_values.reshape(4, 128), obs_hours[None], prior_precision, transition)
    ))


def body(obs_rows, obs_values, obs_hours, prior_precision, transition, site_basis):
    means = filtered_means(obs_rows, obs_values, obs_hours, prior_precision, transition)
    return jnp.einsum(
        "hs,ns->hn", means.reshape(NZ * PLANE * HR, S), site_basis, preferred_element_type=F32
    ).astype(BF16)


def solution(mesh):
    in_specs = (
        P(("tm", "site"), None),
        P(("tm", "site")),
        P(("tm", "site")),
        P(),
        P(),
        P(("tm", "site"), None),
    )
    out_specs = P(None, ("tm", "site"))
    return jax.shard_map(body, mesh=mesh, in_specs=in_specs, out_specs=out_specs, check_vma=False)
```

```python
import jax
import jax.numpy as jnp
from jax import lax
from jax.experimental import pallas as pl
from jax.experimental.pallas import tpu as pltpu
from jax.sharding import PartitionSpec as P

F32, BF16 = jnp.float32, jnp.bfloat16
MESH = pl.DeviceIdType.MESH

S = 256
NS_ITERS = 8
HR = 4
PAD = 16
ROWS = S + PAD
NX, NY, NC, NZ = 4, 4, 2, 8
PLANE = NY * NC


def split(a):
    high = a.astype(BF16)
    return high, (a - high.astype(F32)).astype(BF16)


def mm(a, b):
    return jnp.dot(a, b, preferred_element_type=F32)


def dot3(a, b):
    ah, al = a
    bh, bl = b
    return mm(ah, bh) + mm(al, bh) + mm(ah, bl)


def wide(row):
    return jnp.broadcast_to(row, (PAD, S))


def kernel(
    rows_hbm, vals_hbm, hours_hbm, prior_hbm, trans_hbm,
    out_ref,
    xs, vs, hs, prior, trans, coupled, power, grams, drives, work, prefix, partner,
    ydiff, yoff, pre, full, handed, planemap, planeoff, lower, lowermap, entry,
    qhi, qlo, qoff, sin, sout, means,
    load_sem, xsend, xrecv, asend, arecv, csend, crecv, ysend, yrecv, osend, orecv,
    ssend, srecv, psend, precv, zsend, zrecv, msend, mrecv, heard,
):
    tm = lax.axis_index("tm")
    x = lax.axis_index("site")
    spot = lax.rem(tm, PLANE)
    core = lax.rem(tm, NC)
    y = lax.div(spot, NC)
    z = lax.div(tm, PLANE)

    def at(zz, yy, cc):
        return zz * PLANE + yy * NC + cc

    loads = [
        pltpu.make_async_copy(rows_hbm.at[pl.ds(0, 256)], xs.at[3, 0], load_sem.at[0]),
        pltpu.make_async_copy(rows_hbm.at[pl.ds(256, 256)], xs.at[3, 1], load_sem.at[1]),
        pltpu.make_async_copy(vals_hbm, vs.at[3], load_sem.at[2]),
        pltpu.make_async_copy(hours_hbm, hs.at[3], load_sem.at[3]),
        pltpu.make_async_copy(prior_hbm, prior, load_sem.at[4]),
        pltpu.make_async_copy(trans_hbm, trans, load_sem.at[5]),
    ]
    for copy in loads:
        copy.start()

    barrier = pltpu.get_barrier_semaphore()
    beside = [(tm, lax.rem(x + k, NX)) for k in (1, NX - 1)]
    beside += [(z * PLANE + lax.rem(spot + k, PLANE), x) for k in range(1, PLANE)]

    def both_ways(sem, reach):
        @pl.when(z >= reach)
        def _():
            pl.semaphore_signal(
                sem, inc=1, device_id=(tm - reach * PLANE, x), device_id_type=MESH
            )

        @pl.when(z < NZ - reach)
        def _():
            pl.semaphore_signal(
                sem, inc=1, device_id=(tm + reach * PLANE, x), device_id_type=MESH
            )

    def ways(reach):
        return jnp.where(z >= reach, 1, 0) + jnp.where(z < NZ - reach, 1, 0)

    for device in beside:
        pl.semaphore_signal(barrier, inc=1, device_id=device, device_id_type=MESH)
    both_ways(barrier, 1)
    pl.semaphore_wait(barrier, len(beside) + ways(1))

    def tell(turn):
        both_ways(heard.at[turn], 2 ** turn)

    def hear(turn):
        pl.semaphore_wait(heard.at[turn], ways(2 ** turn))

    started = []

    def remote(src, dst, send_sem, recv_sem, device):
        return pltpu.make_async_remote_copy(
            src_ref=src, dst_ref=dst, send_sem=send_sem, recv_sem=recv_sem,
            device_id=device, device_id_type=MESH,
        )

    def send(*args):
        copy = remote(*args)
        copy.start()
        started.append(copy)

    def arrived(ref, send_sem, recv_sem):
        remote(ref, ref, send_sem, recv_sem, (tm, x)).wait_recv()

    right, left = ((tm, lax.rem(x + k, NX)) for k in (1, 3))
    for half in (0, 1):
        part = rows_hbm.at[pl.ds(half * 256, 256)]
        send(part, xs.at[0, half], xsend.at[0, half], xrecv.at[0, half], right)
        part = rows_hbm.at[pl.ds((1 - half) * 256, 256)]
        send(part, xs.at[1, 1 - half], xsend.at[1, 1 - half], xrecv.at[1, 1 - half], left)
    for slot, device in ((0, right), (1, left)):
        send(vals_hbm, vs.at[slot], asend.at[0, slot], arecv.at[0, slot], device)
        send(hours_hbm, hs.at[slot], asend.at[1, slot], arecv.at[1, slot], device)
    tell(0)

    for copy in loads:
        copy.wait()

    transposed = trans[...].T
    coupled[...] = dot3(split(transposed), split(prior[...]))
    power[...] = transposed
    for _ in range(3):
        parts = split(power[...])
        power[...] = dot3(parts, parts)

    def add_rows(slot, first):
        hour = hs[slot]
        value = vs[slot].astype(F32)
        value = jnp.concatenate([value[i:i + 1] for i in range(4)], axis=1)
        sub = lax.broadcasted_iota(jnp.int32, (PAD, 512), 0)
        marked = jnp.where(sub == hour, value, 0.0).astype(BF16)
        shape = (2 * 256, S)
        block = xs[slot].reshape(shape)
        turned = block.T
        total = mm(marked, block)
        drives[...] = total if first else drives[...] + total
        for h in range(HR):
            member = jnp.where(hour == h, 1.0, 0.0).astype(BF16)
            product = mm(turned * member, block)
            grams[h] = product if first else grams[h] + product

    add_rows(3, True)
    hear(0)
    tell(1)
    arrived(xs.at[0, 0], xsend.at[0, 0], xrecv.at[0, 0])
    send(xs.at[0, 0], xs.at[2, 0], xsend.at[2, 0], xrecv.at[2, 0], right)
    arrived(xs.at[1, 1], xsend.at[1, 1], xrecv.at[1, 1])
    send(xs.at[1, 1], xs.at[2, 1], xsend.at[2, 1], xrecv.at[2, 1], left)
    for slot in range(2):
        arrived(vs.at[slot], asend.at[0, slot], arecv.at[0, slot])
        arrived(hs.at[slot], asend.at[1, slot], arecv.at[1, slot])
    send(vs.at[0], vs.at[2], asend.at[0, 2], arecv.at[0, 2], right)
    send(hs.at[0], hs.at[2], asend.at[1, 2], arecv.at[1, 2], right)
    arrived(xs.at[0, 1], xsend.at[0, 1], xrecv.at[0, 1])
    add_rows(0, False)
    arrived(xs.at[1, 0], xsend.at[1, 0], xrecv.at[1, 0])
    add_rows(1, False)
    arrived(vs.at[2], asend.at[0, 2], arecv.at[0, 2])
    arrived(hs.at[2], asend.at[1, 2], arecv.at[1, 2])
    arrived(xs.at[2, 0], xsend.at[2, 0], xrecv.at[2, 0])
    arrived(xs.at[2, 1], xsend.at[2, 1], xrecv.at[2, 1])
    add_rows(2, False)

    hear(1)
    tell(2)
    eye = (
        lax.broadcasted_iota(jnp.int32, (S, S), 0) == lax.broadcasted_iota(jnp.int32, (S, S), 1)
    ).astype(F32)
    for h in range(HR):
        lam = prior[...] + grams[h]
        bound = jnp.max(jnp.sum(jnp.abs(lam), axis=0, keepdims=True), axis=1, keepdims=True)
        scale = 1.0 / bound
        work[h, 0:S] = eye - lam * scale
        work[h, S:2 * S] = coupled[...] * scale
        work[h, 2 * S:2 * S + PAD] = drives[...] * scale

    def level(k, carry):
        for h in range(HR):
            held = work[h]
            parts = split(held)
            factor = (parts[0][0:S], parts[1][0:S])
            product = dot3(parts, factor)
            work[h, 0:S] = product[0:S]
            work[h, S:2 * S + PAD] = held[S:2 * S + PAD] + product[S:2 * S + PAD]
        return carry

    lax.fori_loop(0, NS_ITERS - 2, level, 0)

    def closing(h, last):
        held = work[h]
        high, low = split(held)
        factor = high[0:S]
        maps = jnp.concatenate([high[S:2 * S + PAD], low[S:2 * S + PAD]], axis=0)
        both = mm(maps, factor)
        if not last:
            square = (factor, low[0:S])
            work[h, 0:S] = dot3(square, square)
        work[h, S:2 * S + PAD] = held[S:2 * S + PAD] + both[0:ROWS] + both[ROWS:2 * ROWS]

    for h in range(HR):
        closing(h, False)
    for h in range(HR):
        closing(h, True)

    def after(earlier, later_map, later_off):
        joined = dot3(split(earlier), split(later_map))
        return joined[0:S], joined[S:ROWS] + wide(later_off)

    def hour(h):
        return work[h, S:2 * S], work[h, 2 * S + h:2 * S + h + 1]

    def put(ref, mapped):
        ref[0:S] = mapped[0]
        ref[S:ROWS] = mapped[1]

    for h in (0, 2):
        put(prefix.at[h], (hour(h)[0], wide(hour(h)[1])))
    put(prefix.at[1], after(prefix[0], *hour(1)))
    put(handed, after(prefix[2], *hour(3)))
    put(prefix.at[3], after(prefix[1], handed[0:S], handed[S:S + 1]))

    to_core0 = remote(prefix.at[HR - 1], partner, csend, crecv, (at(z, y, 0), x))
    to_core1 = remote(handed, full, psend.at[7], precv.at[7], (at(z, y, 1), x))

    y_right, y_left, y_across = ((at(z, lax.rem(y + k, NY), 0), x) for k in (1, 3, 2))
    ring = []
    for slot, device in ((2, y_across), (0, y_right), (1, y_left)):
        ring.append(remote(yoff.at[y], yoff.at[y], osend.at[slot], orecv.at[slot], device))
        ring.append(remote(ydiff.at[y], ydiff.at[y], ysend.at[slot], yrecv.at[slot], device))
    behind, ahead, opposite = (lax.rem(y + k, NY) for k in (3, 1, 2))
    def state_to(slot, zz, cc):
        return remote(sout, sin, ssend.at[slot], srecv, (at(jnp.minimum(zz, NZ - 1), y, cc), x))

    steps = [state_to(0, z + 1, 0), state_to(1, z + 1, 1)]
    far_steps = [state_to(2, z + 2, 0), state_to(3, z + 2, 1)]
    to_odd = [
        remote(pre.at[NY], lower, msend.at[c], mrecv, (at(jnp.minimum(z + 1, NZ - 1), y, c), x))
        for c in range(NC)
    ]
    odd = lax.rem(z, 2) == 1
    paired = jnp.logical_and(odd, z >= 3)
    lends = jnp.logical_and(jnp.logical_not(odd), z >= 2)
    sends_state = jnp.logical_or(z == 0, jnp.logical_and(odd, z < NZ - 1))
    sends_far = jnp.logical_and(odd, z < NZ - 1)

    def ready_means():
        for h in range(HR):
            m, o = after(full[...], prefix[h, 0:S], prefix[h, S:S + 1])
            high, low = split(m)
            qhi[h] = high
            qlo[h] = low
            qoff[h] = o[0:8]

    def apply(state, high, low):
        sh, sl = split(wide(state))
        both = mm(jnp.concatenate([sh, sl], axis=0), high)
        return both[0:1] + both[PAD:PAD + 1] + mm(sh, low)[0:1]

    @pl.when(core == 1)
    def _():
        to_core0.start()

    @pl.when(core == 0)
    def _():
        arrived(partner, csend, crecv)
        m, o = after(prefix[HR - 1], partner[0:S], partner[S:S + 1])
        ydiff[y] = (power[...] - m).astype(BF16)
        yoff[y] = o[0:8]
        for copy in ring:
            copy.start()


    put(prefix.at[2], after(prefix[1], *hour(2)))
    @pl.when(core == 1)
    def _():
        arrived(full, psend.at[7], precv.at[7])

    @pl.when(core == 0)
    def _():
        for slot, origin in ((0, behind), (1, ahead), (2, opposite)):
            arrived(yoff.at[origin], osend.at[slot], orecv.at[slot])
            arrived(ydiff.at[origin], ysend.at[slot], yrecv.at[slot])

        def chip(j):
            return power[...] - ydiff[j].astype(F32), yoff[j, 0:1]

        put(pre.at[0], (eye, jnp.zeros((PAD, S), F32)))
        m, o = chip(0)
        put(pre.at[1], (m, wide(o)))
        put(pre.at[2], after(pre[1], *chip(1)))
        m, o = chip(2)
        put(pre.at[3], (m, wide(o)))
        put(handed, after(pre[3], *chip(3)))
        put(pre.at[4], after(pre[2], handed[0:S], handed[S:S + 1]))

        @pl.when(z == 0)
        def _():
            sout[...] = pre[NY, S:S + 1]
            for copy in steps:
                copy.start()

        @pl.when(lends)
        def _():
            for copy in to_odd:
                copy.start()

        @pl.when(z == 1)
        def _():
            high, low = split(pre[NY, 0:S])
            planemap[0] = high
            planemap[1] = low
            planeoff[...] = pre[NY, S:S + 1]

        put(pre.at[3], after(pre[2], *chip(2)))
        full[...] = pre[y]
        put(handed, after(pre[y], prefix[HR - 1, 0:S], prefix[HR - 1, S:S + 1]))
        to_core1.start()

    hear(2)

    @pl.when(z >= 2)
    def _():
        ready_means()

    @pl.when(paired)
    def _():
        arrived(lower, msend.at[0], mrecv)
        high, low = split(lower[0:S])
        lowermap[0] = high
        lowermap[1] = low

    @pl.when(jnp.logical_and(paired, core == 0))
    def _():
        m, o = after(lower[...], pre[NY, 0:S], pre[NY, S:S + 1])
        high, low = split(m)
        planemap[0] = high
        planemap[1] = low
        planeoff[...] = o[0:1]

    @pl.when(z == 0)
    def _():
        sin[...] = jnp.zeros((1, S), F32)

    @pl.when(z > 0)
    def _():
        arrived(sin, ssend.at[0], srecv)

    entry[...] = sin[...]

    @pl.when(jnp.logical_and(core == 0, sends_far))
    def _():
        sout[...] = apply(sin[...], planemap[0], planemap[1]) + planeoff[...]
        for copy in far_steps + steps:
            copy.start()

    @pl.when(paired)
    def _():
        entry[...] = apply(sin[...], lowermap[0], lowermap[1]) + lower[S:S + 1]

    @pl.when(z < 2)
    def _():
        ready_means()

    found = [apply(entry[...], qhi[h], qlo[h]) + qoff[h, 0:1] for h in range(HR)]
    means[z, spot] = jnp.concatenate(found, axis=0).astype(BF16)

    mine = means.at[z, spot]
    for k in (4, 3, 5, 2, 6, 1, 7):
        zz = lax.rem(z + k, NZ)
        for j in range(PLANE):
            device = (zz * PLANE + lax.rem(spot + j, PLANE), x)
            remote(mine, mine, zsend.at[k - 1], zrecv.at[k - 1], device).start()
    for j in range(1, PLANE):
        device = (z * PLANE + lax.rem(spot + j, PLANE), x)
        send(mine, mine, psend.at[j - 1], precv.at[j - 1], device)
    for j in range(1, PLANE):
        origin = lax.rem(spot + PLANE - j, PLANE)
        arrived(means.at[z, origin], psend.at[j - 1], precv.at[j - 1])
    for k in (1, 7, 2, 6, 3, 5, 4):
        origin = lax.rem(z + NZ - k, NZ)
        arrived(means.at[origin], zsend.at[k - 1], zrecv.at[k - 1])
    out_ref[...] = means[...]

    for copy in started:
        copy.wait_send()
    for k in range(1, NZ):
        device = (lax.rem(z + k, NZ) * PLANE + spot, x)
        remote(means.at[z], means.at[z], zsend.at[k - 1], zrecv.at[k - 1], device).wait_send()

    @pl.when(core == 1)
    def _():
        to_core0.wait_send()

    @pl.when(core == 0)
    def _():
        for copy in ring + [to_core1]:
            copy.wait_send()

    @pl.when(jnp.logical_and(core == 0, sends_state))
    def _():
        for copy in steps:
            copy.wait_send()

    @pl.when(jnp.logical_and(core == 0, sends_far))
    def _():
        for copy in far_steps:
            copy.wait_send()

    @pl.when(jnp.logical_and(core == 0, lends))
    def _():
        for copy in to_odd:
            copy.wait_send()


def filtered_means(obs_rows, obs_values, obs_hours, prior_precision, transition):
    any_space = pl.BlockSpec(memory_space=pltpu.MemorySpace.HBM)
    dma = pltpu.SemaphoreType.DMA
    return pl.pallas_call(
        kernel,
        out_shape=jax.ShapeDtypeStruct((NZ, PLANE, HR, S), BF16),
        in_specs=[any_space] * 5,
        out_specs=pl.BlockSpec(memory_space=pltpu.VMEM),
        scratch_shapes=[
            pltpu.VMEM((4, 2, 256, S), BF16),
            pltpu.VMEM((4, 4, 128), BF16),
            pltpu.VMEM((4, 1, 512), jnp.int32),
            pltpu.VMEM((S, S), F32),
            pltpu.VMEM((S, S), F32),
            pltpu.VMEM((S, S), F32),
            pltpu.VMEM((S, S), F32),
            pltpu.VMEM((HR, S, S), F32),
            pltpu.VMEM((PAD, S), F32),
            pltpu.VMEM((HR, 2 * S + PAD, S), F32),
            pltpu.VMEM((HR, ROWS, S), F32),
            pltpu.VMEM((ROWS, S), F32),
            pltpu.VMEM((NY, S, S), BF16),
            pltpu.VMEM((NY, 8, S), F32),
            pltpu.VMEM((NY + 1, ROWS, S), F32),
            pltpu.VMEM((ROWS, S), F32),
            pltpu.VMEM((ROWS, S), F32),
            pltpu.VMEM((2, S, S), BF16),
            pltpu.VMEM((1, S), F32),
            pltpu.VMEM((ROWS, S), F32),
            pltpu.VMEM((2, S, S), BF16),
            pltpu.VMEM((1, S), F32),
            pltpu.VMEM((HR, S, S), BF16),
            pltpu.VMEM((HR, S, S), BF16),
            pltpu.VMEM((HR, 8, S), F32),
            pltpu.VMEM((1, S), F32),
            pltpu.VMEM((1, S), F32),
            pltpu.VMEM((NZ, PLANE, HR, S), BF16),
            dma((6,)),
            dma((3, 2)), dma((3, 2)),
            dma((2, 3)), dma((2, 3)),
            dma(()), dma(()),
            dma((3,)), dma((3,)),
            dma((3,)), dma((3,)),
            dma((4,)), dma(()),
            dma((8,)), dma((8,)),
            dma((7,)), dma((7,)),
            dma((2,)), dma(()),
            pltpu.SemaphoreType.REGULAR((3,)),
        ],
        compiler_params=pltpu.CompilerParams(
            collective_id=0, has_side_effects=True, vmem_limit_bytes=32 * 1024 * 1024
        ),
    )(*(
        pltpu.with_memory_space_constraint(a, pltpu.MemorySpace.HBM)
        for a in (obs_rows, obs_values.reshape(4, 128), obs_hours[None], prior_precision, transition)
    ))


def body(obs_rows, obs_values, obs_hours, prior_precision, transition, site_basis):
    means = filtered_means(obs_rows, obs_values, obs_hours, prior_precision, transition)
    return jnp.einsum(
        "hs,ns->hn", means.reshape(NZ * PLANE * HR, S), site_basis, preferred_element_type=F32
    ).astype(BF16)


def solution(mesh):
    in_specs = (
        P(("tm", "site"), None),
        P(("tm", "site")),
        P(("tm", "site")),
        P(),
        P(),
        P(("tm", "site"), None),
    )
    out_specs = P(None, ("tm", "site"))
    return jax.shard_map(body, mesh=mesh, in_specs=in_specs, out_specs=out_specs, check_vma=False)
```

```python
import jax
import jax.numpy as jnp
from jax import lax
from jax.experimental import pallas as pl
from jax.experimental.pallas import tpu as pltpu
from jax.sharding import PartitionSpec as P

F32, BF16 = jnp.float32, jnp.bfloat16
MESH = pl.DeviceIdType.MESH

S = 256
NS_ITERS = 8
HR = 4
PAD = 16
ROWS = S + PAD
NX, NY, NC, NZ = 4, 4, 2, 8
PLANE = NY * NC
CHUNKS, WIDTH = 8, 512


def split(a):
    high = a.astype(BF16)
    return high, (a - high.astype(F32)).astype(BF16)


def mm(a, b):
    return jnp.dot(a, b, preferred_element_type=F32)


def dot3(a, b):
    ah, al = a
    bh, bl = b
    return mm(ah, bh) + mm(al, bh) + mm(ah, bl)


def wide(row):
    return jnp.broadcast_to(row, (PAD, S))


def kernel(
    rows_hbm, vals_hbm, hours_hbm, prior_hbm, trans_hbm, sites_hbm,
    out_ref, sites_out,
    xs, vs, hs, prior, trans, coupled, power, grams, drives, work, prefix, partner,
    ydiff, yoff, pre, full, handed, planemap, planeoff, lower, lowermap, entry,
    qhi, qlo, qoff, sin, sout, means,
    load_sem, xsend, xrecv, asend, arecv, csend, crecv, ysend, yrecv, osend, orecv,
    ssend, srecv, psend, precv, zsend, zrecv, msend, mrecv, heard,
):
    tm = lax.axis_index("tm")
    x = lax.axis_index("site")
    spot = lax.rem(tm, PLANE)
    core = lax.rem(tm, NC)
    y = lax.div(spot, NC)
    z = lax.div(tm, PLANE)

    def at(zz, yy, cc):
        return zz * PLANE + yy * NC + cc

    loads = [
        pltpu.make_async_copy(rows_hbm.at[pl.ds(0, 256)], xs.at[3, 0], load_sem.at[0]),
        pltpu.make_async_copy(rows_hbm.at[pl.ds(256, 256)], xs.at[3, 1], load_sem.at[1]),
        pltpu.make_async_copy(vals_hbm, vs.at[3], load_sem.at[2]),
        pltpu.make_async_copy(hours_hbm, hs.at[3], load_sem.at[3]),
        pltpu.make_async_copy(prior_hbm, prior, load_sem.at[4]),
        pltpu.make_async_copy(trans_hbm, trans, load_sem.at[5]),
    ]
    held_sites = pltpu.make_async_copy(sites_hbm, sites_out, load_sem.at[6])
    for copy in loads:
        copy.start()

    barrier = pltpu.get_barrier_semaphore()
    beside = [(tm, lax.rem(x + k, NX)) for k in (1, NX - 1)]
    beside += [(z * PLANE + lax.rem(spot + k, PLANE), x) for k in range(1, PLANE)]

    def both_ways(sem, reach):
        @pl.when(z >= reach)
        def _():
            pl.semaphore_signal(
                sem, inc=1, device_id=(tm - reach * PLANE, x), device_id_type=MESH
            )

        @pl.when(z < NZ - reach)
        def _():
            pl.semaphore_signal(
                sem, inc=1, device_id=(tm + reach * PLANE, x), device_id_type=MESH
            )

    def ways(reach):
        return jnp.where(z >= reach, 1, 0) + jnp.where(z < NZ - reach, 1, 0)

    for device in beside:
        pl.semaphore_signal(barrier, inc=1, device_id=device, device_id_type=MESH)
    both_ways(barrier, 1)
    pl.semaphore_wait(barrier, len(beside) + ways(1))

    def tell(turn):
        both_ways(heard.at[turn], 2 ** turn)

    def hear(turn):
        pl.semaphore_wait(heard.at[turn], ways(2 ** turn))

    started = []

    def remote(src, dst, send_sem, recv_sem, device):
        return pltpu.make_async_remote_copy(
            src_ref=src, dst_ref=dst, send_sem=send_sem, recv_sem=recv_sem,
            device_id=device, device_id_type=MESH,
        )

    def send(*args):
        copy = remote(*args)
        copy.start()
        started.append(copy)

    def arrived(ref, send_sem, recv_sem):
        remote(ref, ref, send_sem, recv_sem, (tm, x)).wait_recv()

    right, left = ((tm, lax.rem(x + k, NX)) for k in (1, 3))
    for half in (0, 1):
        part = rows_hbm.at[pl.ds(half * 256, 256)]
        send(part, xs.at[0, half], xsend.at[0, half], xrecv.at[0, half], right)
        part = rows_hbm.at[pl.ds((1 - half) * 256, 256)]
        send(part, xs.at[1, 1 - half], xsend.at[1, 1 - half], xrecv.at[1, 1 - half], left)
    for slot, device in ((0, right), (1, left)):
        send(vals_hbm, vs.at[slot], asend.at[0, slot], arecv.at[0, slot], device)
        send(hours_hbm, hs.at[slot], asend.at[1, slot], arecv.at[1, slot], device)
    tell(0)
    held_sites.start()

    for copy in loads:
        copy.wait()

    transposed = trans[...].T
    coupled[...] = dot3(split(transposed), split(prior[...]))
    power[...] = transposed
    for _ in range(3):
        parts = split(power[...])
        power[...] = dot3(parts, parts)

    def add_rows(slot, first):
        hour = hs[slot]
        value = vs[slot].astype(F32)
        value = jnp.concatenate([value[i:i + 1] for i in range(4)], axis=1)
        sub = lax.broadcasted_iota(jnp.int32, (PAD, 512), 0)
        marked = jnp.where(sub == hour, value, 0.0).astype(BF16)
        shape = (2 * 256, S)
        block = xs[slot].reshape(shape)
        turned = block.T
        total = mm(marked, block)
        drives[...] = total if first else drives[...] + total
        for h in range(HR):
            member = jnp.where(hour == h, 1.0, 0.0).astype(BF16)
            product = mm(turned * member, block)
            grams[h] = product if first else grams[h] + product

    add_rows(3, True)
    hear(0)
    tell(1)
    arrived(xs.at[0, 0], xsend.at[0, 0], xrecv.at[0, 0])
    send(xs.at[0, 0], xs.at[2, 0], xsend.at[2, 0], xrecv.at[2, 0], right)
    arrived(xs.at[1, 1], xsend.at[1, 1], xrecv.at[1, 1])
    send(xs.at[1, 1], xs.at[2, 1], xsend.at[2, 1], xrecv.at[2, 1], left)
    for slot in range(2):
        arrived(vs.at[slot], asend.at[0, slot], arecv.at[0, slot])
        arrived(hs.at[slot], asend.at[1, slot], arecv.at[1, slot])
    send(vs.at[0], vs.at[2], asend.at[0, 2], arecv.at[0, 2], right)
    send(hs.at[0], hs.at[2], asend.at[1, 2], arecv.at[1, 2], right)
    arrived(xs.at[0, 1], xsend.at[0, 1], xrecv.at[0, 1])
    add_rows(0, False)
    arrived(xs.at[1, 0], xsend.at[1, 0], xrecv.at[1, 0])
    add_rows(1, False)
    arrived(vs.at[2], asend.at[0, 2], arecv.at[0, 2])
    arrived(hs.at[2], asend.at[1, 2], arecv.at[1, 2])
    arrived(xs.at[2, 0], xsend.at[2, 0], xrecv.at[2, 0])
    arrived(xs.at[2, 1], xsend.at[2, 1], xrecv.at[2, 1])
    add_rows(2, False)

    hear(1)
    tell(2)
    eye = (
        lax.broadcasted_iota(jnp.int32, (S, S), 0) == lax.broadcasted_iota(jnp.int32, (S, S), 1)
    ).astype(F32)
    for h in range(HR):
        lam = prior[...] + grams[h]
        bound = jnp.max(jnp.sum(jnp.abs(lam), axis=0, keepdims=True), axis=1, keepdims=True)
        scale = 1.0 / bound
        work[h, 0:S] = eye - lam * scale
        work[h, S:2 * S] = coupled[...] * scale
        work[h, 2 * S:2 * S + PAD] = drives[...] * scale

    def level(k, carry):
        for h in range(HR):
            held = work[h]
            parts = split(held)
            factor = (parts[0][0:S], parts[1][0:S])
            product = dot3(parts, factor)
            work[h, 0:S] = product[0:S]
            work[h, S:2 * S + PAD] = held[S:2 * S + PAD] + product[S:2 * S + PAD]
        return carry

    lax.fori_loop(0, NS_ITERS - 2, level, 0)

    def closing(h, last):
        held = work[h]
        high, low = split(held)
        factor = high[0:S]
        maps = jnp.concatenate([high[S:2 * S + PAD], low[S:2 * S + PAD]], axis=0)
        both = mm(maps, factor)
        if not last:
            square = (factor, low[0:S])
            work[h, 0:S] = dot3(square, square)
        work[h, S:2 * S + PAD] = held[S:2 * S + PAD] + both[0:ROWS] + both[ROWS:2 * ROWS]

    for h in range(HR):
        closing(h, False)
    for h in range(HR):
        closing(h, True)

    def after(earlier, later_map, later_off):
        joined = dot3(split(earlier), split(later_map))
        return joined[0:S], joined[S:ROWS] + wide(later_off)

    def hour(h):
        return work[h, S:2 * S], work[h, 2 * S + h:2 * S + h + 1]

    def put(ref, mapped):
        ref[0:S] = mapped[0]
        ref[S:ROWS] = mapped[1]

    for h in (0, 2):
        put(prefix.at[h], (hour(h)[0], wide(hour(h)[1])))
    put(prefix.at[1], after(prefix[0], *hour(1)))
    put(handed, after(prefix[2], *hour(3)))
    put(prefix.at[3], after(prefix[1], handed[0:S], handed[S:S + 1]))

    to_core0 = remote(prefix.at[HR - 1], partner, csend, crecv, (at(z, y, 0), x))
    to_core1 = remote(handed, full, psend.at[7], precv.at[7], (at(z, y, 1), x))

    y_right, y_left, y_across = ((at(z, lax.rem(y + k, NY), 0), x) for k in (1, 3, 2))
    ring = []
    for slot, device in ((2, y_across), (0, y_right), (1, y_left)):
        ring.append(remote(yoff.at[y], yoff.at[y], osend.at[slot], orecv.at[slot], device))
        ring.append(remote(ydiff.at[y], ydiff.at[y], ysend.at[slot], yrecv.at[slot], device))
    behind, ahead, opposite = (lax.rem(y + k, NY) for k in (3, 1, 2))
    def state_to(slot, zz, cc):
        return remote(sout, sin, ssend.at[slot], srecv, (at(jnp.minimum(zz, NZ - 1), y, cc), x))

    steps = [state_to(0, z + 1, 0), state_to(1, z + 1, 1)]
    far_steps = [state_to(2, z + 2, 0), state_to(3, z + 2, 1)]
    to_odd = [
        remote(pre.at[NY], lower, msend.at[c], mrecv, (at(jnp.minimum(z + 1, NZ - 1), y, c), x))
        for c in range(NC)
    ]
    odd = lax.rem(z, 2) == 1
    paired = jnp.logical_and(odd, z >= 3)
    lends = jnp.logical_and(jnp.logical_not(odd), z >= 2)
    sends_state = jnp.logical_or(z == 0, jnp.logical_and(odd, z < NZ - 1))
    sends_far = jnp.logical_and(odd, z < NZ - 1)

    def ready_means():
        for h in range(HR):
            m, o = after(full[...], prefix[h, 0:S], prefix[h, S:S + 1])
            high, low = split(m)
            qhi[h] = high
            qlo[h] = low
            qoff[h] = o[0:8]

    def apply(state, high, low):
        sh, sl = split(wide(state))
        both = mm(jnp.concatenate([sh, sl], axis=0), high)
        return both[0:1] + both[PAD:PAD + 1] + mm(sh, low)[0:1]

    @pl.when(core == 1)
    def _():
        to_core0.start()

    @pl.when(core == 0)
    def _():
        arrived(partner, csend, crecv)
        m, o = after(prefix[HR - 1], partner[0:S], partner[S:S + 1])
        ydiff[y] = (power[...] - m).astype(BF16)
        yoff[y] = o[0:8]
        for copy in ring:
            copy.start()


    put(prefix.at[2], after(prefix[1], *hour(2)))
    @pl.when(core == 1)
    def _():
        arrived(full, psend.at[7], precv.at[7])

    @pl.when(core == 0)
    def _():
        for slot, origin in ((0, behind), (1, ahead), (2, opposite)):
            arrived(yoff.at[origin], osend.at[slot], orecv.at[slot])
            arrived(ydiff.at[origin], ysend.at[slot], yrecv.at[slot])

        def chip(j):
            return power[...] - ydiff[j].astype(F32), yoff[j, 0:1]

        put(pre.at[0], (eye, jnp.zeros((PAD, S), F32)))
        m, o = chip(0)
        put(pre.at[1], (m, wide(o)))
        put(pre.at[2], after(pre[1], *chip(1)))
        m, o = chip(2)
        put(pre.at[3], (m, wide(o)))
        put(handed, after(pre[3], *chip(3)))
        put(pre.at[4], after(pre[2], handed[0:S], handed[S:S + 1]))

        @pl.when(z == 0)
        def _():
            sout[...] = pre[NY, S:S + 1]
            for copy in steps:
                copy.start()

        @pl.when(lends)
        def _():
            for copy in to_odd:
                copy.start()

        @pl.when(z == 1)
        def _():
            high, low = split(pre[NY, 0:S])
            planemap[0] = high
            planemap[1] = low
            planeoff[...] = pre[NY, S:S + 1]

        put(pre.at[3], after(pre[2], *chip(2)))
        full[...] = pre[y]
        put(handed, after(pre[y], prefix[HR - 1, 0:S], prefix[HR - 1, S:S + 1]))
        to_core1.start()

    hear(2)

    @pl.when(z >= 2)
    def _():
        ready_means()

    @pl.when(paired)
    def _():
        arrived(lower, msend.at[0], mrecv)
        high, low = split(lower[0:S])
        lowermap[0] = high
        lowermap[1] = low

    @pl.when(jnp.logical_and(paired, core == 0))
    def _():
        m, o = after(lower[...], pre[NY, 0:S], pre[NY, S:S + 1])
        high, low = split(m)
        planemap[0] = high
        planemap[1] = low
        planeoff[...] = o[0:1]

    @pl.when(z == 0)
    def _():
        sin[...] = jnp.zeros((1, S), F32)

    @pl.when(z > 0)
    def _():
        arrived(sin, ssend.at[0], srecv)

    entry[...] = sin[...]

    @pl.when(jnp.logical_and(core == 0, sends_far))
    def _():
        sout[...] = apply(sin[...], planemap[0], planemap[1]) + planeoff[...]
        for copy in far_steps + steps:
            copy.start()

    @pl.when(paired)
    def _():
        entry[...] = apply(sin[...], lowermap[0], lowermap[1]) + lower[S:S + 1]

    @pl.when(z < 2)
    def _():
        ready_means()

    found = [apply(entry[...], qhi[h], qlo[h]) + qoff[h, 0:1] for h in range(HR)]
    means[z, spot] = jnp.concatenate(found, axis=0).astype(BF16)

    mine = means.at[z, spot]
    for k in (4, 3, 5, 2, 6, 1, 7):
        zz = lax.rem(z + k, NZ)
        for j in range(PLANE):
            device = (zz * PLANE + lax.rem(spot + j, PLANE), x)
            remote(mine, mine, zsend.at[k - 1], zrecv.at[k - 1], device).start()
    for j in range(1, PLANE):
        device = (z * PLANE + lax.rem(spot + j, PLANE), x)
        send(mine, mine, psend.at[j - 1], precv.at[j - 1], device)
    for j in range(1, PLANE):
        origin = lax.rem(spot + PLANE - j, PLANE)
        arrived(means.at[z, origin], psend.at[j - 1], precv.at[j - 1])
    for k in (1, 7, 2, 6, 3, 5, 4):
        origin = lax.rem(z + NZ - k, NZ)
        arrived(means.at[origin], zsend.at[k - 1], zrecv.at[k - 1])
    out_ref[...] = means[...]
    held_sites.wait()

    for copy in started:
        copy.wait_send()
    for k in range(1, NZ):
        device = (lax.rem(z + k, NZ) * PLANE + spot, x)
        remote(means.at[z], means.at[z], zsend.at[k - 1], zrecv.at[k - 1], device).wait_send()

    @pl.when(core == 1)
    def _():
        to_core0.wait_send()

    @pl.when(core == 0)
    def _():
        for copy in ring + [to_core1]:
            copy.wait_send()

    @pl.when(jnp.logical_and(core == 0, sends_state))
    def _():
        for copy in steps:
            copy.wait_send()

    @pl.when(jnp.logical_and(core == 0, sends_far))
    def _():
        for copy in far_steps:
            copy.wait_send()

    @pl.when(jnp.logical_and(core == 0, lends))
    def _():
        for copy in to_odd:
            copy.wait_send()


def filtered_means(obs_rows, obs_values, obs_hours, prior_precision, transition, site_basis):
    any_space = pl.BlockSpec(memory_space=pltpu.MemorySpace.HBM)
    dma = pltpu.SemaphoreType.DMA
    return pl.pallas_call(
        kernel,
        out_shape=(
            jax.ShapeDtypeStruct((NZ, PLANE, HR, S), BF16),
            jax.ShapeDtypeStruct(site_basis.shape, BF16),
        ),
        in_specs=[any_space] * 6,
        out_specs=(pl.BlockSpec(memory_space=pltpu.VMEM),) * 2,
        scratch_shapes=[
            pltpu.VMEM((4, 2, 256, S), BF16),
            pltpu.VMEM((4, 4, 128), BF16),
            pltpu.VMEM((4, 1, 512), jnp.int32),
            pltpu.VMEM((S, S), F32),
            pltpu.VMEM((S, S), F32),
            pltpu.VMEM((S, S), F32),
            pltpu.VMEM((S, S), F32),
            pltpu.VMEM((HR, S, S), F32),
            pltpu.VMEM((PAD, S), F32),
            pltpu.VMEM((HR, 2 * S + PAD, S), F32),
            pltpu.VMEM((HR, ROWS, S), F32),
            pltpu.VMEM((ROWS, S), F32),
            pltpu.VMEM((NY, S, S), BF16),
            pltpu.VMEM((NY, 8, S), F32),
            pltpu.VMEM((NY + 1, ROWS, S), F32),
            pltpu.VMEM((ROWS, S), F32),
            pltpu.VMEM((ROWS, S), F32),
            pltpu.VMEM((2, S, S), BF16),
            pltpu.VMEM((1, S), F32),
            pltpu.VMEM((ROWS, S), F32),
            pltpu.VMEM((2, S, S), BF16),
            pltpu.VMEM((1, S), F32),
            pltpu.VMEM((HR, S, S), BF16),
            pltpu.VMEM((HR, S, S), BF16),
            pltpu.VMEM((HR, 8, S), F32),
            pltpu.VMEM((1, S), F32),
            pltpu.VMEM((1, S), F32),
            pltpu.VMEM((NZ, PLANE, HR, S), BF16),
            dma((7,)),
            dma((3, 2)), dma((3, 2)),
            dma((2, 3)), dma((2, 3)),
            dma(()), dma(()),
            dma((3,)), dma((3,)),
            dma((3,)), dma((3,)),
            dma((4,)), dma(()),
            dma((8,)), dma((8,)),
            dma((7,)), dma((7,)),
            dma((2,)), dma(()),
            pltpu.SemaphoreType.REGULAR((3,)),
        ],
        compiler_params=pltpu.CompilerParams(
            collective_id=0, has_side_effects=True, vmem_limit_bytes=32 * 1024 * 1024
        ),
    )(*(
        pltpu.with_memory_space_constraint(a, pltpu.MemorySpace.HBM)
        for a in (obs_rows, obs_values.reshape(4, 128), obs_hours[None], prior_precision, transition, site_basis)
    ))


def predict_kernel(means_ref, sites_ref, out_hbm, held, sems):
    copies = []
    for c in range(CHUNKS):
        held[c] = lax.dot_general(
            means_ref[...], sites_ref[c * WIDTH:(c + 1) * WIDTH, :],
            (((1,), (1,)), ((), ())), preferred_element_type=F32,
        ).astype(BF16)
        copies.append(
            pltpu.make_async_copy(held.at[c], out_hbm.at[:, pl.ds(c * WIDTH, WIDTH)], sems.at[c])
        )
        copies[-1].start()
    for copy in copies:
        copy.wait()


def predict(means, site_basis):
    vmem = pl.BlockSpec(memory_space=pltpu.MemorySpace.VMEM)
    hours, sites = means.shape[0], site_basis.shape[0]
    return pl.pallas_call(
        predict_kernel,
        out_shape=jax.ShapeDtypeStruct((hours, sites), BF16),
        in_specs=[vmem, vmem],
        out_specs=pl.BlockSpec(memory_space=pltpu.MemorySpace.HBM),
        scratch_shapes=[
            pltpu.VMEM((CHUNKS, hours, WIDTH), BF16),
            pltpu.SemaphoreType.DMA((CHUNKS,)),
        ],
        compiler_params=pltpu.CompilerParams(vmem_limit_bytes=16 * 1024 * 1024),
    )(means, site_basis)


def body(obs_rows, obs_values, obs_hours, prior_precision, transition, site_basis):
    means, sites = filtered_means(
        obs_rows, obs_values, obs_hours, prior_precision, transition, site_basis
    )
    return predict(means.reshape(NZ * PLANE * HR, S), sites)


def solution(mesh):
    in_specs = (
        P(("tm", "site"), None),
        P(("tm", "site")),
        P(("tm", "site")),
        P(),
        P(),
        P(("tm", "site"), None),
    )
    out_specs = P(None, ("tm", "site"))
    return jax.shard_map(body, mesh=mesh, in_specs=in_specs, out_specs=out_specs, check_vma=False)
```

```python
import jax
import jax.numpy as jnp
from jax import lax
from jax.experimental import pallas as pl
from jax.experimental.pallas import tpu as pltpu
from jax.sharding import PartitionSpec as P

F32, BF16 = jnp.float32, jnp.bfloat16
MESH = pl.DeviceIdType.MESH

S = 256
NS_ITERS = 8
HR = 4
PAD = 16
ROWS = S + PAD
NX, NY, NC, NZ = 4, 4, 2, 8
PLANE = NY * NC
CHUNKS, WIDTH = 8, 512


def split(a):
    high = a.astype(BF16)
    return high, (a - high.astype(F32)).astype(BF16)


def mm(a, b):
    return jnp.dot(a, b, preferred_element_type=F32)


def dot3(a, b):
    ah, al = a
    bh, bl = b
    return mm(ah, bh) + mm(al, bh) + mm(ah, bl)


def wide(row):
    return jnp.broadcast_to(row, (PAD, S))


def kernel(
    rows_hbm, vals_hbm, hours_hbm, prior_hbm, trans_hbm, sites_hbm,
    out_ref, sites_out,
    xs, vs, hs, prior, trans, turned_map, power, drives, work, prefix, partner,
    ydiff, yoff, pre, full, handed, planemap, planeoff, lower, lowermap, entry,
    qhi, qlo, qoff, sin, sout, means,
    load_sem, xsend, xrecv, asend, arecv, csend, crecv, ysend, yrecv, osend, orecv,
    ssend, srecv, psend, precv, zsend, zrecv, msend, mrecv, heard,
):
    tm = lax.axis_index("tm")
    x = lax.axis_index("site")
    spot = lax.rem(tm, PLANE)
    core = lax.rem(tm, NC)
    y = lax.div(spot, NC)
    z = lax.div(tm, PLANE)

    def at(zz, yy, cc):
        return zz * PLANE + yy * NC + cc

    loads = [
        pltpu.make_async_copy(rows_hbm.at[pl.ds(0, 256)], xs.at[3, 0], load_sem.at[0]),
        pltpu.make_async_copy(rows_hbm.at[pl.ds(256, 256)], xs.at[3, 1], load_sem.at[1]),
        pltpu.make_async_copy(vals_hbm, vs.at[3], load_sem.at[2]),
        pltpu.make_async_copy(hours_hbm, hs.at[3], load_sem.at[3]),
        pltpu.make_async_copy(prior_hbm, prior, load_sem.at[4]),
        pltpu.make_async_copy(trans_hbm, trans, load_sem.at[5]),
    ]
    held_sites = pltpu.make_async_copy(sites_hbm, sites_out, load_sem.at[6])
    for copy in loads:
        copy.start()

    barrier = pltpu.get_barrier_semaphore()
    beside = [(tm, lax.rem(x + k, NX)) for k in (1, NX - 1)]
    beside += [(z * PLANE + lax.rem(spot + k, PLANE), x) for k in range(1, PLANE)]

    def both_ways(sem, reach):
        @pl.when(z >= reach)
        def _():
            pl.semaphore_signal(
                sem, inc=1, device_id=(tm - reach * PLANE, x), device_id_type=MESH
            )

        @pl.when(z < NZ - reach)
        def _():
            pl.semaphore_signal(
                sem, inc=1, device_id=(tm + reach * PLANE, x), device_id_type=MESH
            )

    def ways(reach):
        return jnp.where(z >= reach, 1, 0) + jnp.where(z < NZ - reach, 1, 0)

    for device in beside:
        pl.semaphore_signal(barrier, inc=1, device_id=device, device_id_type=MESH)
    both_ways(barrier, 1)
    pl.semaphore_wait(barrier, len(beside) + ways(1))

    def tell(turn):
        both_ways(heard.at[turn], 2 ** turn)

    def hear(turn):
        pl.semaphore_wait(heard.at[turn], ways(2 ** turn))

    started = []

    def remote(src, dst, send_sem, recv_sem, device):
        return pltpu.make_async_remote_copy(
            src_ref=src, dst_ref=dst, send_sem=send_sem, recv_sem=recv_sem,
            device_id=device, device_id_type=MESH,
        )

    def send(*args):
        copy = remote(*args)
        copy.start()
        started.append(copy)

    def arrived(ref, send_sem, recv_sem):
        remote(ref, ref, send_sem, recv_sem, (tm, x)).wait_recv()

    right, left = ((tm, lax.rem(x + k, NX)) for k in (1, 3))
    for half in (0, 1):
        part = rows_hbm.at[pl.ds(half * 256, 256)]
        send(part, xs.at[0, half], xsend.at[0, half], xrecv.at[0, half], right)
        part = rows_hbm.at[pl.ds((1 - half) * 256, 256)]
        send(part, xs.at[1, 1 - half], xsend.at[1, 1 - half], xrecv.at[1, 1 - half], left)
    for slot, device in ((0, right), (1, left)):
        send(vals_hbm, vs.at[slot], asend.at[0, slot], arecv.at[0, slot], device)
        send(hours_hbm, hs.at[slot], asend.at[1, slot], arecv.at[1, slot], device)
    tell(0)
    held_sites.start()

    for copy in loads:
        copy.wait()

    transposed = trans[...].T
    turned_map[...] = transposed
    power[...] = transposed
    for _ in range(3):
        parts = split(power[...])
        power[...] = dot3(parts, parts)

    square, drive, gain = slice(0, S), slice(S, ROWS), slice(ROWS, ROWS + S)

    def add_rows(slot, first):
        hour = hs[slot]
        value = vs[slot].astype(F32)
        value = jnp.concatenate([value[i:i + 1] for i in range(4)], axis=1)
        sub = lax.broadcasted_iota(jnp.int32, (PAD, 512), 0)
        marked = jnp.where(sub == hour, value, 0.0).astype(BF16)
        shape = (2 * 256, S)
        block = xs[slot].reshape(shape)
        turned = block.T
        total = mm(marked, block)
        drives[...] = total if first else drives[...] + total
        for h in range(HR):
            member = jnp.where(hour == h, 1.0, 0.0).astype(BF16)
            product = mm(turned * member, block)
            work[h, gain] = product if first else work[h, gain] + product

    add_rows(3, True)
    hear(0)
    tell(1)
    arrived(xs.at[0, 0], xsend.at[0, 0], xrecv.at[0, 0])
    send(xs.at[0, 0], xs.at[2, 0], xsend.at[2, 0], xrecv.at[2, 0], right)
    arrived(xs.at[1, 1], xsend.at[1, 1], xrecv.at[1, 1])
    send(xs.at[1, 1], xs.at[2, 1], xsend.at[2, 1], xrecv.at[2, 1], left)
    for slot in range(2):
        arrived(vs.at[slot], asend.at[0, slot], arecv.at[0, slot])
        arrived(hs.at[slot], asend.at[1, slot], arecv.at[1, slot])
    send(vs.at[0], vs.at[2], asend.at[0, 2], arecv.at[0, 2], right)
    send(hs.at[0], hs.at[2], asend.at[1, 2], arecv.at[1, 2], right)
    arrived(xs.at[0, 1], xsend.at[0, 1], xrecv.at[0, 1])
    add_rows(0, False)
    arrived(xs.at[1, 0], xsend.at[1, 0], xrecv.at[1, 0])
    add_rows(1, False)
    arrived(vs.at[2], asend.at[0, 2], arecv.at[0, 2])
    arrived(hs.at[2], asend.at[1, 2], arecv.at[1, 2])
    arrived(xs.at[2, 0], xsend.at[2, 0], xrecv.at[2, 0])
    arrived(xs.at[2, 1], xsend.at[2, 1], xrecv.at[2, 1])
    add_rows(2, False)

    hear(1)
    tell(2)
    eye = (
        lax.broadcasted_iota(jnp.int32, (S, S), 0) == lax.broadcasted_iota(jnp.int32, (S, S), 1)
    ).astype(F32)
    scales = []
    for h in range(HR):
        lam = prior[...] + work[h, gain]
        bound = jnp.max(jnp.sum(jnp.abs(lam), axis=0, keepdims=True), axis=1, keepdims=True)
        scales.append(1.0 / bound)
        work[h, square] = eye - lam * scales[h]
        work[h, drive] = drives[...]

    def level(k, carry):
        for h in range(HR):
            held = work[h]
            high, low = split(held[0:ROWS])
            rows = jnp.concatenate([high, held[gain].astype(BF16), low], axis=0)
            first = mm(rows, high[square])
            exact = first[0:ROWS] + first[ROWS + S:] + mm(high, low[square])
            work[h, square] = exact[square]
            work[h, drive] = held[drive] + exact[drive]
            work[h, gain] = held[gain] + first[gain]
        return carry

    lax.fori_loop(0, NS_ITERS, level, 0)
    for h in range(HR):
        kept = eye - work[h, square] - work[h, gain] * scales[h]
        work[h, gain] = dot3(split(turned_map[...]), split(kept))
        work[h, drive] = work[h, drive] * scales[h]

    def after(earlier, later_map, later_off):
        joined = dot3(split(earlier), split(later_map))
        return joined[0:S], joined[S:ROWS] + wide(later_off)

    def hour(h):
        return work[h, gain], work[h, S + h:S + h + 1]

    def put(ref, mapped):
        ref[0:S] = mapped[0]
        ref[S:ROWS] = mapped[1]

    for h in (0, 2):
        put(prefix.at[h], (hour(h)[0], wide(hour(h)[1])))
    put(prefix.at[1], after(prefix[0], *hour(1)))
    put(handed, after(prefix[2], *hour(3)))
    put(prefix.at[3], after(prefix[1], handed[0:S], handed[S:S + 1]))

    to_core0 = remote(prefix.at[HR - 1], partner, csend, crecv, (at(z, y, 0), x))
    to_core1 = remote(handed, full, psend.at[7], precv.at[7], (at(z, y, 1), x))

    y_right, y_left, y_across = ((at(z, lax.rem(y + k, NY), 0), x) for k in (1, 3, 2))
    ring = []
    for slot, device in ((2, y_across), (0, y_right), (1, y_left)):
        ring.append(remote(yoff.at[y], yoff.at[y], osend.at[slot], orecv.at[slot], device))
        ring.append(remote(ydiff.at[y], ydiff.at[y], ysend.at[slot], yrecv.at[slot], device))
    behind, ahead, opposite = (lax.rem(y + k, NY) for k in (3, 1, 2))
    def state_to(slot, zz, cc):
        return remote(sout, sin, ssend.at[slot], srecv, (at(jnp.minimum(zz, NZ - 1), y, cc), x))

    steps = [state_to(0, z + 1, 0), state_to(1, z + 1, 1)]
    far_steps = [state_to(2, z + 2, 0), state_to(3, z + 2, 1)]
    to_odd = [
        remote(pre.at[NY], lower, msend.at[c], mrecv, (at(jnp.minimum(z + 1, NZ - 1), y, c), x))
        for c in range(NC)
    ]
    odd = lax.rem(z, 2) == 1
    paired = jnp.logical_and(odd, z >= 3)
    lends = jnp.logical_and(jnp.logical_not(odd), z >= 2)
    sends_state = jnp.logical_or(z == 0, jnp.logical_and(odd, z < NZ - 1))
    sends_far = jnp.logical_and(odd, z < NZ - 1)

    def ready_means():
        for h in range(HR):
            m, o = after(full[...], prefix[h, 0:S], prefix[h, S:S + 1])
            high, low = split(m)
            qhi[h] = high
            qlo[h] = low
            qoff[h] = o[0:8]

    def apply(state, high, low):
        sh, sl = split(wide(state))
        both = mm(jnp.concatenate([sh, sl], axis=0), high)
        return both[0:1] + both[PAD:PAD + 1] + mm(sh, low)[0:1]

    @pl.when(core == 1)
    def _():
        to_core0.start()

    @pl.when(core == 0)
    def _():
        arrived(partner, csend, crecv)
        m, o = after(prefix[HR - 1], partner[0:S], partner[S:S + 1])
        ydiff[y] = (power[...] - m).astype(BF16)
        yoff[y] = o[0:8]
        for copy in ring:
            copy.start()


    put(prefix.at[2], after(prefix[1], *hour(2)))
    @pl.when(core == 1)
    def _():
        arrived(full, psend.at[7], precv.at[7])

    @pl.when(core == 0)
    def _():
        for slot, origin in ((0, behind), (1, ahead), (2, opposite)):
            arrived(yoff.at[origin], osend.at[slot], orecv.at[slot])
            arrived(ydiff.at[origin], ysend.at[slot], yrecv.at[slot])

        def chip(j):
            return power[...] - ydiff[j].astype(F32), yoff[j, 0:1]

        put(pre.at[0], (eye, jnp.zeros((PAD, S), F32)))
        m, o = chip(0)
        put(pre.at[1], (m, wide(o)))
        put(pre.at[2], after(pre[1], *chip(1)))
        m, o = chip(2)
        put(pre.at[3], (m, wide(o)))
        put(handed, after(pre[3], *chip(3)))
        put(pre.at[4], after(pre[2], handed[0:S], handed[S:S + 1]))

        @pl.when(z == 0)
        def _():
            sout[...] = pre[NY, S:S + 1]
            for copy in steps:
                copy.start()

        @pl.when(lends)
        def _():
            for copy in to_odd:
                copy.start()

        @pl.when(z == 1)
        def _():
            high, low = split(pre[NY, 0:S])
            planemap[0] = high
            planemap[1] = low
            planeoff[...] = pre[NY, S:S + 1]

        put(pre.at[3], after(pre[2], *chip(2)))
        full[...] = pre[y]
        put(handed, after(pre[y], prefix[HR - 1, 0:S], prefix[HR - 1, S:S + 1]))
        to_core1.start()

    hear(2)

    @pl.when(z >= 2)
    def _():
        ready_means()

    @pl.when(paired)
    def _():
        arrived(lower, msend.at[0], mrecv)
        high, low = split(lower[0:S])
        lowermap[0] = high
        lowermap[1] = low

    @pl.when(jnp.logical_and(paired, core == 0))
    def _():
        m, o = after(lower[...], pre[NY, 0:S], pre[NY, S:S + 1])
        high, low = split(m)
        planemap[0] = high
        planemap[1] = low
        planeoff[...] = o[0:1]

    @pl.when(z == 0)
    def _():
        sin[...] = jnp.zeros((1, S), F32)

    @pl.when(z > 0)
    def _():
        arrived(sin, ssend.at[0], srecv)

    entry[...] = sin[...]

    @pl.when(jnp.logical_and(core == 0, sends_far))
    def _():
        sout[...] = apply(sin[...], planemap[0], planemap[1]) + planeoff[...]
        for copy in far_steps + steps:
            copy.start()

    @pl.when(paired)
    def _():
        entry[...] = apply(sin[...], lowermap[0], lowermap[1]) + lower[S:S + 1]

    @pl.when(z < 2)
    def _():
        ready_means()

    found = [apply(entry[...], qhi[h], qlo[h]) + qoff[h, 0:1] for h in range(HR)]
    means[z, spot] = jnp.concatenate(found, axis=0).astype(BF16)

    mine = means.at[z, spot]
    for k in (4, 3, 5, 2, 6, 1, 7):
        zz = lax.rem(z + k, NZ)
        for j in range(PLANE):
            device = (zz * PLANE + lax.rem(spot + j, PLANE), x)
            remote(mine, mine, zsend.at[k - 1], zrecv.at[k - 1], device).start()
    for j in range(1, PLANE):
        device = (z * PLANE + lax.rem(spot + j, PLANE), x)
        send(mine, mine, psend.at[j - 1], precv.at[j - 1], device)
    for j in range(1, PLANE):
        origin = lax.rem(spot + PLANE - j, PLANE)
        arrived(means.at[z, origin], psend.at[j - 1], precv.at[j - 1])
    for k in (1, 7, 2, 6, 3, 5, 4):
        origin = lax.rem(z + NZ - k, NZ)
        arrived(means.at[origin], zsend.at[k - 1], zrecv.at[k - 1])
    out_ref[...] = means[...]
    held_sites.wait()

    for copy in started:
        copy.wait_send()
    for k in range(1, NZ):
        device = (lax.rem(z + k, NZ) * PLANE + spot, x)
        remote(means.at[z], means.at[z], zsend.at[k - 1], zrecv.at[k - 1], device).wait_send()

    @pl.when(core == 1)
    def _():
        to_core0.wait_send()

    @pl.when(core == 0)
    def _():
        for copy in ring + [to_core1]:
            copy.wait_send()

    @pl.when(jnp.logical_and(core == 0, sends_state))
    def _():
        for copy in steps:
            copy.wait_send()

    @pl.when(jnp.logical_and(core == 0, sends_far))
    def _():
        for copy in far_steps:
            copy.wait_send()

    @pl.when(jnp.logical_and(core == 0, lends))
    def _():
        for copy in to_odd:
            copy.wait_send()


def filtered_means(obs_rows, obs_values, obs_hours, prior_precision, transition, site_basis):
    any_space = pl.BlockSpec(memory_space=pltpu.MemorySpace.HBM)
    dma = pltpu.SemaphoreType.DMA
    return pl.pallas_call(
        kernel,
        out_shape=(
            jax.ShapeDtypeStruct((NZ, PLANE, HR, S), BF16),
            jax.ShapeDtypeStruct(site_basis.shape, BF16),
        ),
        in_specs=[any_space] * 6,
        out_specs=(pl.BlockSpec(memory_space=pltpu.VMEM),) * 2,
        scratch_shapes=[
            pltpu.VMEM((4, 2, 256, S), BF16),
            pltpu.VMEM((4, 4, 128), BF16),
            pltpu.VMEM((4, 1, 512), jnp.int32),
            pltpu.VMEM((S, S), F32),
            pltpu.VMEM((S, S), F32),
            pltpu.VMEM((S, S), F32),
            pltpu.VMEM((S, S), F32),
            pltpu.VMEM((PAD, S), F32),
            pltpu.VMEM((HR, 2 * S + PAD, S), F32),
            pltpu.VMEM((HR, ROWS, S), F32),
            pltpu.VMEM((ROWS, S), F32),
            pltpu.VMEM((NY, S, S), BF16),
            pltpu.VMEM((NY, 8, S), F32),
            pltpu.VMEM((NY + 1, ROWS, S), F32),
            pltpu.VMEM((ROWS, S), F32),
            pltpu.VMEM((ROWS, S), F32),
            pltpu.VMEM((2, S, S), BF16),
            pltpu.VMEM((1, S), F32),
            pltpu.VMEM((ROWS, S), F32),
            pltpu.VMEM((2, S, S), BF16),
            pltpu.VMEM((1, S), F32),
            pltpu.VMEM((HR, S, S), BF16),
            pltpu.VMEM((HR, S, S), BF16),
            pltpu.VMEM((HR, 8, S), F32),
            pltpu.VMEM((1, S), F32),
            pltpu.VMEM((1, S), F32),
            pltpu.VMEM((NZ, PLANE, HR, S), BF16),
            dma((7,)),
            dma((3, 2)), dma((3, 2)),
            dma((2, 3)), dma((2, 3)),
            dma(()), dma(()),
            dma((3,)), dma((3,)),
            dma((3,)), dma((3,)),
            dma((4,)), dma(()),
            dma((8,)), dma((8,)),
            dma((7,)), dma((7,)),
            dma((2,)), dma(()),
            pltpu.SemaphoreType.REGULAR((3,)),
        ],
        compiler_params=pltpu.CompilerParams(
            collective_id=0, has_side_effects=True, vmem_limit_bytes=32 * 1024 * 1024
        ),
    )(*(
        pltpu.with_memory_space_constraint(a, pltpu.MemorySpace.HBM)
        for a in (obs_rows, obs_values.reshape(4, 128), obs_hours[None], prior_precision, transition, site_basis)
    ))


def predict_kernel(means_ref, sites_ref, out_hbm, held, sems):
    copies = []
    for c in range(CHUNKS):
        held[c] = lax.dot_general(
            means_ref[...], sites_ref[c * WIDTH:(c + 1) * WIDTH, :],
            (((1,), (1,)), ((), ())), preferred_element_type=F32,
        ).astype(BF16)
        copies.append(
            pltpu.make_async_copy(held.at[c], out_hbm.at[:, pl.ds(c * WIDTH, WIDTH)], sems.at[c])
        )
        copies[-1].start()
    for copy in copies:
        copy.wait()


def predict(means, site_basis):
    vmem = pl.BlockSpec(memory_space=pltpu.MemorySpace.VMEM)
    hours, sites = means.shape[0], site_basis.shape[0]
    return pl.pallas_call(
        predict_kernel,
        out_shape=jax.ShapeDtypeStruct((hours, sites), BF16),
        in_specs=[vmem, vmem],
        out_specs=pl.BlockSpec(memory_space=pltpu.MemorySpace.HBM),
        scratch_shapes=[
            pltpu.VMEM((CHUNKS, hours, WIDTH), BF16),
            pltpu.SemaphoreType.DMA((CHUNKS,)),
        ],
        compiler_params=pltpu.CompilerParams(vmem_limit_bytes=16 * 1024 * 1024),
    )(means, site_basis)


def body(obs_rows, obs_values, obs_hours, prior_precision, transition, site_basis):
    means, sites = filtered_means(
        obs_rows, obs_values, obs_hours, prior_precision, transition, site_basis
    )
    return predict(means.reshape(NZ * PLANE * HR, S), sites)


def solution(mesh):
    in_specs = (
        P(("tm", "site"), None),
        P(("tm", "site")),
        P(("tm", "site")),
        P(),
        P(),
        P(("tm", "site"), None),
    )
    out_specs = P(None, ("tm", "site"))
    return jax.shard_map(body, mesh=mesh, in_specs=in_specs, out_specs=out_specs, check_vma=False)
```

```python
import jax
import jax.numpy as jnp
from jax import lax
from jax.experimental import pallas as pl
from jax.experimental.pallas import tpu as pltpu
from jax.sharding import PartitionSpec as P

F32, BF16 = jnp.float32, jnp.bfloat16
MESH = pl.DeviceIdType.MESH

S = 256
NS_ITERS = 8
HR = 4
PAD = 16
ROWS = S + PAD
NX, NY, NC, NZ = 4, 4, 2, 8
PLANE = NY * NC
CHUNKS, WIDTH = 8, 512
SOON = 6
EARLY = SOON * PLANE * HR


def split(a):
    high = a.astype(BF16)
    return high, (a - high.astype(F32)).astype(BF16)


def mm(a, b):
    return jnp.dot(a, b, preferred_element_type=F32)


def dot3(a, b):
    ah, al = a
    bh, bl = b
    return mm(ah, bh) + mm(al, bh) + mm(ah, bl)


def against(rows, sites):
    product = lax.dot_general(
        rows, sites, (((1,), (1,)), ((), ())), preferred_element_type=F32
    )
    return product.astype(BF16)


def hours_of(means, first, last):
    blocks = [means[p, b].astype(F32) for p in range(first, last) for b in range(PLANE)]
    return jnp.concatenate(blocks, axis=0).astype(BF16)


def wide(row):
    return jnp.broadcast_to(row, (PAD, S))


def kernel(
    rows_hbm, vals_hbm, hours_hbm, prior_hbm, trans_hbm, sites_hbm,
    out_ref, sites_out, early_ref,
    xs, vs, hs, prior, trans, turned_map, power, drives, work, prefix, partner,
    ydiff, yoff, pre, full, handed, planemap, planeoff, lower, lowermap, entry,
    qhi, qlo, qoff, sin, sout, means,
    load_sem, xsend, xrecv, asend, arecv, csend, crecv, ysend, yrecv, osend, orecv,
    ssend, srecv, psend, precv, zsend, zrecv, msend, mrecv, heard,
):
    tm = lax.axis_index("tm")
    x = lax.axis_index("site")
    spot = lax.rem(tm, PLANE)
    core = lax.rem(tm, NC)
    y = lax.div(spot, NC)
    z = lax.div(tm, PLANE)

    def at(zz, yy, cc):
        return zz * PLANE + yy * NC + cc

    loads = [
        pltpu.make_async_copy(rows_hbm.at[pl.ds(0, 256)], xs.at[3, 0], load_sem.at[0]),
        pltpu.make_async_copy(rows_hbm.at[pl.ds(256, 256)], xs.at[3, 1], load_sem.at[1]),
        pltpu.make_async_copy(vals_hbm, vs.at[3], load_sem.at[2]),
        pltpu.make_async_copy(hours_hbm, hs.at[3], load_sem.at[3]),
        pltpu.make_async_copy(prior_hbm, prior, load_sem.at[4]),
        pltpu.make_async_copy(trans_hbm, trans, load_sem.at[5]),
    ]
    held_sites = pltpu.make_async_copy(sites_hbm, sites_out, load_sem.at[6])
    for copy in loads:
        copy.start()

    barrier = pltpu.get_barrier_semaphore()
    beside = [(tm, lax.rem(x + k, NX)) for k in (1, NX - 1)]
    beside += [(z * PLANE + lax.rem(spot + k, PLANE), x) for k in range(1, PLANE)]

    def both_ways(sem, reach):
        @pl.when(z >= reach)
        def _():
            pl.semaphore_signal(
                sem, inc=1, device_id=(tm - reach * PLANE, x), device_id_type=MESH
            )

        @pl.when(z < NZ - reach)
        def _():
            pl.semaphore_signal(
                sem, inc=1, device_id=(tm + reach * PLANE, x), device_id_type=MESH
            )

    def ways(reach):
        return jnp.where(z >= reach, 1, 0) + jnp.where(z < NZ - reach, 1, 0)

    for device in beside:
        pl.semaphore_signal(barrier, inc=1, device_id=device, device_id_type=MESH)
    both_ways(barrier, 1)
    pl.semaphore_wait(barrier, len(beside) + ways(1))

    def tell(turn):
        both_ways(heard.at[turn], 2 ** turn)

    def hear(turn):
        pl.semaphore_wait(heard.at[turn], ways(2 ** turn))

    started = []

    def remote(src, dst, send_sem, recv_sem, device):
        return pltpu.make_async_remote_copy(
            src_ref=src, dst_ref=dst, send_sem=send_sem, recv_sem=recv_sem,
            device_id=device, device_id_type=MESH,
        )

    def send(*args):
        copy = remote(*args)
        copy.start()
        started.append(copy)

    def arrived(ref, send_sem, recv_sem):
        remote(ref, ref, send_sem, recv_sem, (tm, x)).wait_recv()

    right, left = ((tm, lax.rem(x + k, NX)) for k in (1, 3))
    for half in (0, 1):
        part = rows_hbm.at[pl.ds(half * 256, 256)]
        send(part, xs.at[0, half], xsend.at[0, half], xrecv.at[0, half], right)
        part = rows_hbm.at[pl.ds((1 - half) * 256, 256)]
        send(part, xs.at[1, 1 - half], xsend.at[1, 1 - half], xrecv.at[1, 1 - half], left)
    for slot, device in ((0, right), (1, left)):
        send(vals_hbm, vs.at[slot], asend.at[0, slot], arecv.at[0, slot], device)
        send(hours_hbm, hs.at[slot], asend.at[1, slot], arecv.at[1, slot], device)
    tell(0)
    held_sites.start()

    for copy in loads:
        copy.wait()

    transposed = trans[...].T
    turned_map[...] = transposed
    power[...] = transposed
    for _ in range(3):
        parts = split(power[...])
        power[...] = dot3(parts, parts)

    square, drive, gain = slice(0, S), slice(S, ROWS), slice(ROWS, ROWS + S)

    def add_rows(slot, first):
        hour = hs[slot]
        value = vs[slot].astype(F32)
        value = jnp.concatenate([value[i:i + 1] for i in range(4)], axis=1)
        sub = lax.broadcasted_iota(jnp.int32, (PAD, 512), 0)
        marked = jnp.where(sub == hour, value, 0.0).astype(BF16)
        shape = (2 * 256, S)
        block = xs[slot].reshape(shape)
        turned = block.T
        total = mm(marked, block)
        drives[...] = total if first else drives[...] + total
        for h in range(HR):
            member = jnp.where(hour == h, 1.0, 0.0).astype(BF16)
            product = mm(turned * member, block)
            work[h, gain] = product if first else work[h, gain] + product

    add_rows(3, True)
    hear(0)
    tell(1)
    arrived(xs.at[0, 0], xsend.at[0, 0], xrecv.at[0, 0])
    send(xs.at[0, 0], xs.at[2, 0], xsend.at[2, 0], xrecv.at[2, 0], right)
    arrived(xs.at[1, 1], xsend.at[1, 1], xrecv.at[1, 1])
    send(xs.at[1, 1], xs.at[2, 1], xsend.at[2, 1], xrecv.at[2, 1], left)
    for slot in range(2):
        arrived(vs.at[slot], asend.at[0, slot], arecv.at[0, slot])
        arrived(hs.at[slot], asend.at[1, slot], arecv.at[1, slot])
    send(vs.at[0], vs.at[2], asend.at[0, 2], arecv.at[0, 2], right)
    send(hs.at[0], hs.at[2], asend.at[1, 2], arecv.at[1, 2], right)
    arrived(xs.at[0, 1], xsend.at[0, 1], xrecv.at[0, 1])
    add_rows(0, False)
    arrived(xs.at[1, 0], xsend.at[1, 0], xrecv.at[1, 0])
    add_rows(1, False)
    arrived(vs.at[2], asend.at[0, 2], arecv.at[0, 2])
    arrived(hs.at[2], asend.at[1, 2], arecv.at[1, 2])
    arrived(xs.at[2, 0], xsend.at[2, 0], xrecv.at[2, 0])
    arrived(xs.at[2, 1], xsend.at[2, 1], xrecv.at[2, 1])
    add_rows(2, False)

    hear(1)
    tell(2)
    eye = (
        lax.broadcasted_iota(jnp.int32, (S, S), 0) == lax.broadcasted_iota(jnp.int32, (S, S), 1)
    ).astype(F32)
    scales = []
    for h in range(HR):
        lam = prior[...] + work[h, gain]
        bound = jnp.max(jnp.sum(jnp.abs(lam), axis=0, keepdims=True), axis=1, keepdims=True)
        scales.append(1.0 / bound)
        work[h, square] = eye - lam * scales[h]
        work[h, drive] = drives[...]

    def level(k, carry):
        for h in range(HR):
            held = work[h]
            high, low = split(held[0:ROWS])
            rows = jnp.concatenate([high, held[gain].astype(BF16), low], axis=0)
            first = mm(rows, high[square])
            exact = first[0:ROWS] + first[ROWS + S:] + mm(high, low[square])
            work[h, square] = exact[square]
            work[h, drive] = held[drive] + exact[drive]
            work[h, gain] = held[gain] + first[gain]
        return carry

    lax.fori_loop(0, NS_ITERS, level, 0)
    for h in range(HR):
        kept = eye - work[h, square] - work[h, gain] * scales[h]
        work[h, gain] = dot3(split(turned_map[...]), split(kept))
        work[h, drive] = work[h, drive] * scales[h]

    def after(earlier, later_map, later_off):
        joined = dot3(split(earlier), split(later_map))
        return joined[0:S], joined[S:ROWS] + wide(later_off)

    def hour(h):
        return work[h, gain], work[h, S + h:S + h + 1]

    def put(ref, mapped):
        ref[0:S] = mapped[0]
        ref[S:ROWS] = mapped[1]

    for h in (0, 2):
        put(prefix.at[h], (hour(h)[0], wide(hour(h)[1])))
    put(prefix.at[1], after(prefix[0], *hour(1)))
    put(handed, after(prefix[2], *hour(3)))
    put(prefix.at[3], after(prefix[1], handed[0:S], handed[S:S + 1]))

    to_core0 = remote(prefix.at[HR - 1], partner, csend, crecv, (at(z, y, 0), x))
    to_core1 = remote(handed, full, psend.at[7], precv.at[7], (at(z, y, 1), x))

    y_right, y_left, y_across = ((at(z, lax.rem(y + k, NY), 0), x) for k in (1, 3, 2))
    ring = []
    for slot, device in ((2, y_across), (0, y_right), (1, y_left)):
        ring.append(remote(yoff.at[y], yoff.at[y], osend.at[slot], orecv.at[slot], device))
        ring.append(remote(ydiff.at[y], ydiff.at[y], ysend.at[slot], yrecv.at[slot], device))
    behind, ahead, opposite = (lax.rem(y + k, NY) for k in (3, 1, 2))
    def state_to(slot, zz, cc):
        return remote(sout, sin, ssend.at[slot], srecv, (at(jnp.minimum(zz, NZ - 1), y, cc), x))

    steps = [state_to(0, z + 1, 0), state_to(1, z + 1, 1)]
    far_steps = [state_to(2, z + 2, 0), state_to(3, z + 2, 1)]
    to_odd = [
        remote(pre.at[NY], lower, msend.at[c], mrecv, (at(jnp.minimum(z + 1, NZ - 1), y, c), x))
        for c in range(NC)
    ]
    odd = lax.rem(z, 2) == 1
    paired = jnp.logical_and(odd, z >= 3)
    lends = jnp.logical_and(jnp.logical_not(odd), z >= 2)
    sends_state = jnp.logical_or(z == 0, jnp.logical_and(odd, z < NZ - 1))
    sends_far = jnp.logical_and(odd, z < NZ - 1)

    def ready_means():
        for h in range(HR):
            m, o = after(full[...], prefix[h, 0:S], prefix[h, S:S + 1])
            high, low = split(m)
            qhi[h] = high
            qlo[h] = low
            qoff[h] = o[0:8]

    def apply(state, high, low):
        sh, sl = split(wide(state))
        both = mm(jnp.concatenate([sh, sl], axis=0), high)
        return both[0:1] + both[PAD:PAD + 1] + mm(sh, low)[0:1]

    @pl.when(core == 1)
    def _():
        to_core0.start()

    @pl.when(core == 0)
    def _():
        arrived(partner, csend, crecv)
        m, o = after(prefix[HR - 1], partner[0:S], partner[S:S + 1])
        ydiff[y] = (power[...] - m).astype(BF16)
        yoff[y] = o[0:8]
        for copy in ring:
            copy.start()


    put(prefix.at[2], after(prefix[1], *hour(2)))
    @pl.when(core == 1)
    def _():
        arrived(full, psend.at[7], precv.at[7])

    @pl.when(core == 0)
    def _():
        for slot, origin in ((0, behind), (1, ahead), (2, opposite)):
            arrived(yoff.at[origin], osend.at[slot], orecv.at[slot])
            arrived(ydiff.at[origin], ysend.at[slot], yrecv.at[slot])

        def chip(j):
            return power[...] - ydiff[j].astype(F32), yoff[j, 0:1]

        put(pre.at[0], (eye, jnp.zeros((PAD, S), F32)))
        m, o = chip(0)
        put(pre.at[1], (m, wide(o)))
        put(pre.at[2], after(pre[1], *chip(1)))
        m, o = chip(2)
        put(pre.at[3], (m, wide(o)))
        put(handed, after(pre[3], *chip(3)))
        put(pre.at[4], after(pre[2], handed[0:S], handed[S:S + 1]))

        @pl.when(z == 0)
        def _():
            sout[...] = pre[NY, S:S + 1]
            for copy in steps:
                copy.start()

        @pl.when(lends)
        def _():
            for copy in to_odd:
                copy.start()

        @pl.when(z == 1)
        def _():
            high, low = split(pre[NY, 0:S])
            planemap[0] = high
            planemap[1] = low
            planeoff[...] = pre[NY, S:S + 1]

        put(pre.at[3], after(pre[2], *chip(2)))
        full[...] = pre[y]
        put(handed, after(pre[y], prefix[HR - 1, 0:S], prefix[HR - 1, S:S + 1]))
        to_core1.start()

    hear(2)

    @pl.when(z >= 2)
    def _():
        ready_means()

    @pl.when(paired)
    def _():
        arrived(lower, msend.at[0], mrecv)
        high, low = split(lower[0:S])
        lowermap[0] = high
        lowermap[1] = low

    @pl.when(jnp.logical_and(paired, core == 0))
    def _():
        m, o = after(lower[...], pre[NY, 0:S], pre[NY, S:S + 1])
        high, low = split(m)
        planemap[0] = high
        planemap[1] = low
        planeoff[...] = o[0:1]

    @pl.when(z == 0)
    def _():
        sin[...] = jnp.zeros((1, S), F32)

    @pl.when(z > 0)
    def _():
        arrived(sin, ssend.at[0], srecv)

    entry[...] = sin[...]

    @pl.when(jnp.logical_and(core == 0, sends_far))
    def _():
        sout[...] = apply(sin[...], planemap[0], planemap[1]) + planeoff[...]
        for copy in far_steps + steps:
            copy.start()

    @pl.when(paired)
    def _():
        entry[...] = apply(sin[...], lowermap[0], lowermap[1]) + lower[S:S + 1]

    @pl.when(z < 2)
    def _():
        ready_means()

    found = [apply(entry[...], qhi[h], qlo[h]) + qoff[h, 0:1] for h in range(HR)]
    means[z, spot] = jnp.concatenate(found, axis=0).astype(BF16)

    mine = means.at[z, spot]
    for k in (4, 3, 5, 2, 6, 1, 7):
        zz = lax.rem(z + k, NZ)
        for j in range(PLANE):
            device = (zz * PLANE + lax.rem(spot + j, PLANE), x)
            remote(mine, mine, zsend.at[k - 1], zrecv.at[k - 1], device).start()
    for j in range(1, PLANE):
        device = (z * PLANE + lax.rem(spot + j, PLANE), x)
        send(mine, mine, psend.at[j - 1], precv.at[j - 1], device)
    held_sites.wait()

    def plane_here():
        for j in range(1, PLANE):
            origin = lax.rem(spot + PLANE - j, PLANE)
            arrived(means.at[z, origin], psend.at[j - 1], precv.at[j - 1])

    def plane_from(origin):
        @pl.when(z != origin)
        def _():
            slot = lax.rem(z + NZ - origin + NZ - 1, NZ)
            slot = jnp.minimum(slot, NZ - 2)
            arrived(means.at[origin], zsend.at[slot], zrecv.at[slot])

    @pl.when(z < SOON)
    def _():
        plane_here()

    for origin in range(SOON):
        plane_from(origin)
    rows = hours_of(means, 0, SOON)
    for c in range(CHUNKS):
        early_ref[:, c * WIDTH:(c + 1) * WIDTH] = against(
            rows, sites_out[c * WIDTH:(c + 1) * WIDTH, :]
        )

    @pl.when(z >= SOON)
    def _():
        plane_here()

    for origin in range(SOON, NZ):
        plane_from(origin)
    out_ref[...] = means[...]

    for copy in started:
        copy.wait_send()
    for k in range(1, NZ):
        device = (lax.rem(z + k, NZ) * PLANE + spot, x)
        remote(means.at[z], means.at[z], zsend.at[k - 1], zrecv.at[k - 1], device).wait_send()

    @pl.when(core == 1)
    def _():
        to_core0.wait_send()

    @pl.when(core == 0)
    def _():
        for copy in ring + [to_core1]:
            copy.wait_send()

    @pl.when(jnp.logical_and(core == 0, sends_state))
    def _():
        for copy in steps:
            copy.wait_send()

    @pl.when(jnp.logical_and(core == 0, sends_far))
    def _():
        for copy in far_steps:
            copy.wait_send()

    @pl.when(jnp.logical_and(core == 0, lends))
    def _():
        for copy in to_odd:
            copy.wait_send()


def filtered_means(obs_rows, obs_values, obs_hours, prior_precision, transition, site_basis):
    any_space = pl.BlockSpec(memory_space=pltpu.MemorySpace.HBM)
    dma = pltpu.SemaphoreType.DMA
    return pl.pallas_call(
        kernel,
        out_shape=(
            jax.ShapeDtypeStruct((NZ, PLANE, HR, S), BF16),
            jax.ShapeDtypeStruct(site_basis.shape, BF16),
            jax.ShapeDtypeStruct((EARLY, site_basis.shape[0]), BF16),
        ),
        in_specs=[any_space] * 6,
        out_specs=(pl.BlockSpec(memory_space=pltpu.VMEM),) * 3,
        scratch_shapes=[
            pltpu.VMEM((4, 2, 256, S), BF16),
            pltpu.VMEM((4, 4, 128), BF16),
            pltpu.VMEM((4, 1, 512), jnp.int32),
            pltpu.VMEM((S, S), F32),
            pltpu.VMEM((S, S), F32),
            pltpu.VMEM((S, S), F32),
            pltpu.VMEM((S, S), F32),
            pltpu.VMEM((PAD, S), F32),
            pltpu.VMEM((HR, 2 * S + PAD, S), F32),
            pltpu.VMEM((HR, ROWS, S), F32),
            pltpu.VMEM((ROWS, S), F32),
            pltpu.VMEM((NY, S, S), BF16),
            pltpu.VMEM((NY, 8, S), F32),
            pltpu.VMEM((NY + 1, ROWS, S), F32),
            pltpu.VMEM((ROWS, S), F32),
            pltpu.VMEM((ROWS, S), F32),
            pltpu.VMEM((2, S, S), BF16),
            pltpu.VMEM((1, S), F32),
            pltpu.VMEM((ROWS, S), F32),
            pltpu.VMEM((2, S, S), BF16),
            pltpu.VMEM((1, S), F32),
            pltpu.VMEM((HR, S, S), BF16),
            pltpu.VMEM((HR, S, S), BF16),
            pltpu.VMEM((HR, 8, S), F32),
            pltpu.VMEM((1, S), F32),
            pltpu.VMEM((1, S), F32),
            pltpu.VMEM((NZ, PLANE, HR, S), BF16),
            dma((7,)),
            dma((3, 2)), dma((3, 2)),
            dma((2, 3)), dma((2, 3)),
            dma(()), dma(()),
            dma((3,)), dma((3,)),
            dma((3,)), dma((3,)),
            dma((4,)), dma(()),
            dma((8,)), dma((8,)),
            dma((7,)), dma((7,)),
            dma((2,)), dma(()),
            pltpu.SemaphoreType.REGULAR((3,)),
        ],
        compiler_params=pltpu.CompilerParams(
            collective_id=0, has_side_effects=True, vmem_limit_bytes=32 * 1024 * 1024
        ),
    )(*(
        pltpu.with_memory_space_constraint(a, pltpu.MemorySpace.HBM)
        for a in (obs_rows, obs_values.reshape(4, 128), obs_hours[None], prior_precision, transition, site_basis)
    ))


def predict_kernel(means_ref, sites_ref, early_ref, out_hbm, held, sems):
    copies = [pltpu.make_async_copy(early_ref, out_hbm.at[pl.ds(0, EARLY)], sems.at[CHUNKS])]
    copies[0].start()
    late = hours_of(means_ref, SOON, NZ)
    for c in range(CHUNKS):
        held[c] = against(late, sites_ref[c * WIDTH:(c + 1) * WIDTH, :])
        copies.append(
            pltpu.make_async_copy(
                held.at[c],
                out_hbm.at[pl.ds(EARLY, late.shape[0]), pl.ds(c * WIDTH, WIDTH)],
                sems.at[c],
            )
        )
        copies[-1].start()
    for copy in copies:
        copy.wait()


def predict(means, sites, early):
    vmem = pl.BlockSpec(memory_space=pltpu.MemorySpace.VMEM)
    hours = NZ * PLANE * HR
    return pl.pallas_call(
        predict_kernel,
        out_shape=jax.ShapeDtypeStruct((hours, sites.shape[0]), BF16),
        in_specs=[vmem] * 3,
        out_specs=pl.BlockSpec(memory_space=pltpu.MemorySpace.HBM),
        scratch_shapes=[
            pltpu.VMEM((CHUNKS, hours - EARLY, WIDTH), BF16),
            pltpu.SemaphoreType.DMA((CHUNKS + 1,)),
        ],
        compiler_params=pltpu.CompilerParams(vmem_limit_bytes=16 * 1024 * 1024),
    )(means, sites, early)


def body(obs_rows, obs_values, obs_hours, prior_precision, transition, site_basis):
    means, sites, early = filtered_means(
        obs_rows, obs_values, obs_hours, prior_precision, transition, site_basis
    )
    return predict(means, sites, early)


def solution(mesh):
    in_specs = (
        P(("tm", "site"), None),
        P(("tm", "site")),
        P(("tm", "site")),
        P(),
        P(),
        P(("tm", "site"), None),
    )
    out_specs = P(None, ("tm", "site"))
    return jax.shard_map(body, mesh=mesh, in_specs=in_specs, out_specs=out_specs, check_vma=False)
```

```python
import jax
import jax.numpy as jnp
from jax import lax
from jax.experimental import pallas as pl
from jax.experimental.pallas import tpu as pltpu
from jax.sharding import PartitionSpec as P

F32, BF16 = jnp.float32, jnp.bfloat16
MESH = pl.DeviceIdType.MESH

S = 256
NS_ITERS = 8
HR = 4
PAD = 16
ROWS = S + PAD
NX, NY, NC, NZ = 4, 4, 2, 8
PLANE = NY * NC
CHUNKS, WIDTH = 8, 512
SOON = 6
EARLY = SOON * PLANE * HR


def split(a):
    high = a.astype(BF16)
    return high, (a - high.astype(F32)).astype(BF16)


def mm(a, b):
    return jnp.dot(a, b, preferred_element_type=F32)


def dot3(a, b):
    ah, al = a
    bh, bl = b
    return mm(ah, bh) + mm(al, bh) + mm(ah, bl)


def against(rows, sites):
    product = lax.dot_general(
        rows, sites, (((1,), (1,)), ((), ())), preferred_element_type=F32
    )
    return product.astype(BF16)


def hours_of(means, first, last):
    blocks = [means[p, b].astype(F32) for p in range(first, last) for b in range(PLANE)]
    return jnp.concatenate(blocks, axis=0).astype(BF16)


def wide(row):
    return jnp.broadcast_to(row, (PAD, S))


def kernel(
    rows_hbm, vals_hbm, hours_hbm, prior_hbm, trans_hbm, sites_hbm,
    out_ref, sites_out, early_ref,
    xs, vs, hs, prior, trans, turned_map, power, drives, work, prefix, partner,
    ydiff, yoff, pre, full, handed, planemap, planeoff, lower, lowermap, entry,
    qhi, qlo, qoff, sin, sout, means,
    load_sem, xsend, xrecv, asend, arecv, csend, crecv, ysend, yrecv, osend, orecv,
    ssend, srecv, psend, precv, zsend, zrecv, msend, mrecv, heard,
):
    tm = lax.axis_index("tm")
    x = lax.axis_index("site")
    spot = lax.rem(tm, PLANE)
    core = lax.rem(tm, NC)
    y = lax.div(spot, NC)
    z = lax.div(tm, PLANE)

    def at(zz, yy, cc):
        return zz * PLANE + yy * NC + cc

    loads = [
        pltpu.make_async_copy(rows_hbm.at[pl.ds(0, 256)], xs.at[3, 0], load_sem.at[0]),
        pltpu.make_async_copy(rows_hbm.at[pl.ds(256, 256)], xs.at[3, 1], load_sem.at[1]),
        pltpu.make_async_copy(vals_hbm, vs.at[3], load_sem.at[2]),
        pltpu.make_async_copy(hours_hbm, hs.at[3], load_sem.at[3]),
        pltpu.make_async_copy(prior_hbm, prior, load_sem.at[4]),
        pltpu.make_async_copy(trans_hbm, trans, load_sem.at[5]),
    ]
    held_sites = pltpu.make_async_copy(sites_hbm, sites_out, load_sem.at[6])
    for copy in loads:
        copy.start()

    barrier = pltpu.get_barrier_semaphore()
    beside = [(tm, lax.rem(x + k, NX)) for k in (1, NX - 1)]
    beside += [(z * PLANE + lax.rem(spot + k, PLANE), x) for k in range(1, PLANE)]

    def both_ways(sem, reach):
        @pl.when(z >= reach)
        def _():
            pl.semaphore_signal(
                sem, inc=1, device_id=(tm - reach * PLANE, x), device_id_type=MESH
            )

        @pl.when(z < NZ - reach)
        def _():
            pl.semaphore_signal(
                sem, inc=1, device_id=(tm + reach * PLANE, x), device_id_type=MESH
            )

    def ways(reach):
        return jnp.where(z >= reach, 1, 0) + jnp.where(z < NZ - reach, 1, 0)

    for device in beside:
        pl.semaphore_signal(barrier, inc=1, device_id=device, device_id_type=MESH)
    both_ways(barrier, 1)
    pl.semaphore_wait(barrier, len(beside) + ways(1))

    def tell(turn):
        both_ways(heard.at[turn], 2 ** turn)

    def hear(turn):
        pl.semaphore_wait(heard.at[turn], ways(2 ** turn))

    started = []

    def remote(src, dst, send_sem, recv_sem, device):
        return pltpu.make_async_remote_copy(
            src_ref=src, dst_ref=dst, send_sem=send_sem, recv_sem=recv_sem,
            device_id=device, device_id_type=MESH,
        )

    def send(*args):
        copy = remote(*args)
        copy.start()
        started.append(copy)

    def arrived(ref, send_sem, recv_sem):
        remote(ref, ref, send_sem, recv_sem, (tm, x)).wait_recv()

    right, left = ((tm, lax.rem(x + k, NX)) for k in (1, 3))
    for half in (0, 1):
        part = rows_hbm.at[pl.ds(half * 256, 256)]
        send(part, xs.at[0, half], xsend.at[0, half], xrecv.at[0, half], right)
        part = rows_hbm.at[pl.ds((1 - half) * 256, 256)]
        send(part, xs.at[1, 1 - half], xsend.at[1, 1 - half], xrecv.at[1, 1 - half], left)
    for slot, device in ((0, right), (1, left)):
        send(vals_hbm, vs.at[slot], asend.at[0, slot], arecv.at[0, slot], device)
        send(hours_hbm, hs.at[slot], asend.at[1, slot], arecv.at[1, slot], device)
    tell(0)
    held_sites.start()

    for copy in loads:
        copy.wait()

    transposed = trans[...].T
    turned_map[...] = transposed
    power[...] = transposed
    for _ in range(3):
        parts = split(power[...])
        power[...] = dot3(parts, parts)

    square, drive, gain = slice(0, S), slice(S, ROWS), slice(ROWS, ROWS + S)

    def add_rows(slot, first):
        hour = hs[slot]
        value = vs[slot].astype(F32)
        value = jnp.concatenate([value[i:i + 1] for i in range(4)], axis=1)
        sub = lax.broadcasted_iota(jnp.int32, (PAD, 512), 0)
        marked = jnp.where(sub == hour, value, 0.0).astype(BF16)
        shape = (2 * 256, S)
        block = xs[slot].reshape(shape)
        turned = block.T
        total = mm(marked, block)
        drives[...] = total if first else drives[...] + total
        for h in range(HR):
            member = jnp.where(hour == h, 1.0, 0.0).astype(BF16)
            product = mm(turned * member, block)
            work[h, gain] = product if first else work[h, gain] + product

    add_rows(3, True)
    hear(0)
    tell(1)
    arrived(xs.at[0, 0], xsend.at[0, 0], xrecv.at[0, 0])
    send(xs.at[0, 0], xs.at[2, 0], xsend.at[2, 0], xrecv.at[2, 0], right)
    arrived(xs.at[1, 1], xsend.at[1, 1], xrecv.at[1, 1])
    send(xs.at[1, 1], xs.at[2, 1], xsend.at[2, 1], xrecv.at[2, 1], left)
    for slot in range(2):
        arrived(vs.at[slot], asend.at[0, slot], arecv.at[0, slot])
        arrived(hs.at[slot], asend.at[1, slot], arecv.at[1, slot])
    send(vs.at[0], vs.at[2], asend.at[0, 2], arecv.at[0, 2], right)
    send(hs.at[0], hs.at[2], asend.at[1, 2], arecv.at[1, 2], right)
    arrived(xs.at[0, 1], xsend.at[0, 1], xrecv.at[0, 1])
    add_rows(0, False)
    arrived(xs.at[1, 0], xsend.at[1, 0], xrecv.at[1, 0])
    add_rows(1, False)
    arrived(vs.at[2], asend.at[0, 2], arecv.at[0, 2])
    arrived(hs.at[2], asend.at[1, 2], arecv.at[1, 2])
    arrived(xs.at[2, 0], xsend.at[2, 0], xrecv.at[2, 0])
    arrived(xs.at[2, 1], xsend.at[2, 1], xrecv.at[2, 1])
    add_rows(2, False)

    hear(1)
    tell(2)
    eye = (
        lax.broadcasted_iota(jnp.int32, (S, S), 0) == lax.broadcasted_iota(jnp.int32, (S, S), 1)
    ).astype(F32)
    scales = []
    for h in range(HR):
        lam = prior[...] + work[h, gain]
        bound = jnp.max(jnp.sum(jnp.abs(lam), axis=0, keepdims=True), axis=1, keepdims=True)
        scales.append(1.0 / bound)
        work[h, square] = eye - lam * scales[h]
        work[h, drive] = drives[...]

    def level(k, carry):
        for h in range(HR):
            held = work[h]
            high, low = split(held[0:ROWS])
            rows = jnp.concatenate([high, held[gain].astype(BF16), low], axis=0)
            first = mm(rows, high[square])
            exact = first[0:ROWS] + first[ROWS + S:] + mm(high, low[square])
            work[h, square] = exact[square]
            work[h, drive] = held[drive] + exact[drive]
            work[h, gain] = held[gain] + first[gain]
        return carry

    lax.fori_loop(0, NS_ITERS, level, 0)
    for h in range(HR):
        kept = eye - work[h, square] - work[h, gain] * scales[h]
        work[h, gain] = dot3(split(turned_map[...]), split(kept))
        work[h, drive] = work[h, drive] * scales[h]

    def after(earlier, later_map, later_off):
        joined = dot3(split(earlier), split(later_map))
        return joined[0:S], joined[S:ROWS] + wide(later_off)

    def hour(h):
        return work[h, gain], work[h, S + h:S + h + 1]

    def put(ref, mapped):
        ref[0:S] = mapped[0]
        ref[S:ROWS] = mapped[1]

    for h in (0, 2):
        put(prefix.at[h], (hour(h)[0], wide(hour(h)[1])))
    put(prefix.at[1], after(prefix[0], *hour(1)))
    put(handed, after(prefix[2], *hour(3)))
    put(prefix.at[3], after(prefix[1], handed[0:S], handed[S:S + 1]))

    to_core0 = remote(prefix.at[HR - 1], partner, csend, crecv, (at(z, y, 0), x))
    to_core1 = remote(handed, full, psend.at[7], precv.at[7], (at(z, y, 1), x))

    y_right, y_left, y_across = ((at(z, lax.rem(y + k, NY), 0), x) for k in (1, 3, 2))
    ring = []
    for slot, device in ((2, y_across), (0, y_right), (1, y_left)):
        ring.append(remote(yoff.at[y], yoff.at[y], osend.at[slot], orecv.at[slot], device))
        ring.append(remote(ydiff.at[y], ydiff.at[y], ysend.at[slot], yrecv.at[slot], device))
    behind, ahead, opposite = (lax.rem(y + k, NY) for k in (3, 1, 2))
    def state_to(slot, zz, cc):
        return remote(sout, sin, ssend.at[slot], srecv, (at(jnp.minimum(zz, NZ - 1), y, cc), x))

    steps = [state_to(0, z + 1, 0), state_to(1, z + 1, 1)]
    far_steps = [state_to(2, z + 2, 0), state_to(3, z + 2, 1)]
    to_odd = [
        remote(pre.at[NY], lower, msend.at[c], mrecv, (at(jnp.minimum(z + 1, NZ - 1), y, c), x))
        for c in range(NC)
    ]
    odd = lax.rem(z, 2) == 1
    paired = jnp.logical_and(odd, z >= 3)
    lends = jnp.logical_and(jnp.logical_not(odd), z >= 2)
    sends_state = jnp.logical_or(z == 0, jnp.logical_and(odd, z < NZ - 1))
    sends_far = jnp.logical_and(odd, z < NZ - 1)

    def ready_means():
        for h in range(HR):
            m, o = after(full[...], prefix[h, 0:S], prefix[h, S:S + 1])
            high, low = split(m)
            qhi[h] = high
            qlo[h] = low
            qoff[h] = o[0:8]

    def apply(state, high, low):
        sh, sl = split(wide(state))
        both = mm(jnp.concatenate([sh, sl], axis=0), high)
        return both[0:1] + both[PAD:PAD + 1] + mm(sh, low)[0:1]

    @pl.when(core == 1)
    def _():
        to_core0.start()

    @pl.when(core == 0)
    def _():
        arrived(partner, csend, crecv)
        m, o = after(prefix[HR - 1], partner[0:S], partner[S:S + 1])
        ydiff[y] = (power[...] - m).astype(BF16)
        yoff[y] = o[0:8]
        for copy in ring:
            copy.start()


    put(prefix.at[2], after(prefix[1], *hour(2)))
    @pl.when(core == 1)
    def _():
        arrived(full, psend.at[7], precv.at[7])

    @pl.when(core == 0)
    def _():
        for slot, origin in ((0, behind), (1, ahead), (2, opposite)):
            arrived(yoff.at[origin], osend.at[slot], orecv.at[slot])
            arrived(ydiff.at[origin], ysend.at[slot], yrecv.at[slot])

        def chip(j):
            return power[...] - ydiff[j].astype(F32), yoff[j, 0:1]

        put(pre.at[0], (eye, jnp.zeros((PAD, S), F32)))
        m, o = chip(0)
        put(pre.at[1], (m, wide(o)))
        put(pre.at[2], after(pre[1], *chip(1)))
        m, o = chip(2)
        put(pre.at[3], (m, wide(o)))
        put(handed, after(pre[3], *chip(3)))
        put(pre.at[4], after(pre[2], handed[0:S], handed[S:S + 1]))

        @pl.when(z == 0)
        def _():
            sout[...] = pre[NY, S:S + 1]
            for copy in steps:
                copy.start()

        @pl.when(lends)
        def _():
            for copy in to_odd:
                copy.start()

        @pl.when(z == 1)
        def _():
            high, low = split(pre[NY, 0:S])
            planemap[0] = high
            planemap[1] = low
            planeoff[...] = pre[NY, S:S + 1]

        put(pre.at[3], after(pre[2], *chip(2)))
        full[...] = pre[y]
        put(handed, after(pre[y], prefix[HR - 1, 0:S], prefix[HR - 1, S:S + 1]))
        to_core1.start()

    hear(2)

    @pl.when(z >= 2)
    def _():
        ready_means()

    @pl.when(paired)
    def _():
        arrived(lower, msend.at[0], mrecv)
        high, low = split(lower[0:S])
        lowermap[0] = high
        lowermap[1] = low

    @pl.when(jnp.logical_and(paired, core == 0))
    def _():
        m, o = after(lower[...], pre[NY, 0:S], pre[NY, S:S + 1])
        high, low = split(m)
        planemap[0] = high
        planemap[1] = low
        planeoff[...] = o[0:1]

    @pl.when(z == 0)
    def _():
        sin[...] = jnp.zeros((1, S), F32)

    @pl.when(z > 0)
    def _():
        arrived(sin, ssend.at[0], srecv)

    entry[...] = sin[...]

    @pl.when(jnp.logical_and(core == 0, sends_far))
    def _():
        sout[...] = apply(sin[...], planemap[0], planemap[1]) + planeoff[...]
        for copy in far_steps + steps:
            copy.start()

    @pl.when(paired)
    def _():
        entry[...] = apply(sin[...], lowermap[0], lowermap[1]) + lower[S:S + 1]

    @pl.when(z < 2)
    def _():
        ready_means()

    found = [apply(entry[...], qhi[h], qlo[h]) + qoff[h, 0:1] for h in range(HR)]
    means[z, spot] = jnp.concatenate(found, axis=0).astype(BF16)

    mine = means.at[z, spot]
    for k in (4, 3, 5, 2, 6, 1, 7):
        zz = lax.rem(z + k, NZ)
        for j in range(PLANE):
            device = (zz * PLANE + lax.rem(spot + j, PLANE), x)
            remote(mine, mine, zsend.at[k - 1], zrecv.at[k - 1], device).start()
    for j in range(1, PLANE):
        device = (z * PLANE + lax.rem(spot + j, PLANE), x)
        send(mine, mine, psend.at[j - 1], precv.at[j - 1], device)
    held_sites.wait()

    def plane_here():
        for j in range(1, PLANE):
            origin = lax.rem(spot + PLANE - j, PLANE)
            arrived(means.at[z, origin], psend.at[j - 1], precv.at[j - 1])

    def plane_from(origin):
        @pl.when(z != origin)
        def _():
            slot = lax.rem(z + NZ - origin + NZ - 1, NZ)
            slot = jnp.minimum(slot, NZ - 2)
            arrived(means.at[origin], zsend.at[slot], zrecv.at[slot])

    @pl.when(z < SOON)
    def _():
        plane_here()

    for origin in range(SOON):
        plane_from(origin)
    rows = hours_of(means, 0, SOON)
    for c in range(CHUNKS):
        early_ref[:, c * WIDTH:(c + 1) * WIDTH] = against(
            rows, sites_out[c * WIDTH:(c + 1) * WIDTH, :]
        )

    @pl.when(z >= SOON)
    def _():
        plane_here()


    for copy in started:
        copy.wait_send()
    for k in range(1, NZ):
        device = (lax.rem(z + k, NZ) * PLANE + spot, x)
        remote(means.at[z], means.at[z], zsend.at[k - 1], zrecv.at[k - 1], device).wait_send()

    @pl.when(core == 1)
    def _():
        to_core0.wait_send()

    @pl.when(core == 0)
    def _():
        for copy in ring + [to_core1]:
            copy.wait_send()

    @pl.when(jnp.logical_and(core == 0, sends_state))
    def _():
        for copy in steps:
            copy.wait_send()

    @pl.when(jnp.logical_and(core == 0, sends_far))
    def _():
        for copy in far_steps:
            copy.wait_send()

    @pl.when(jnp.logical_and(core == 0, lends))
    def _():
        for copy in to_odd:
            copy.wait_send()

    for origin in range(SOON, NZ):
        plane_from(origin)
    out_ref[...] = means[...]


def filtered_means(obs_rows, obs_values, obs_hours, prior_precision, transition, site_basis):
    any_space = pl.BlockSpec(memory_space=pltpu.MemorySpace.HBM)
    dma = pltpu.SemaphoreType.DMA
    return pl.pallas_call(
        kernel,
        out_shape=(
            jax.ShapeDtypeStruct((NZ, PLANE, HR, S), BF16),
            jax.ShapeDtypeStruct(site_basis.shape, BF16),
            jax.ShapeDtypeStruct((EARLY, site_basis.shape[0]), BF16),
        ),
        in_specs=[any_space] * 6,
        out_specs=(pl.BlockSpec(memory_space=pltpu.VMEM),) * 3,
        scratch_shapes=[
            pltpu.VMEM((4, 2, 256, S), BF16),
            pltpu.VMEM((4, 4, 128), BF16),
            pltpu.VMEM((4, 1, 512), jnp.int32),
            pltpu.VMEM((S, S), F32),
            pltpu.VMEM((S, S), F32),
            pltpu.VMEM((S, S), F32),
            pltpu.VMEM((S, S), F32),
            pltpu.VMEM((PAD, S), F32),
            pltpu.VMEM((HR, 2 * S + PAD, S), F32),
            pltpu.VMEM((HR, ROWS, S), F32),
            pltpu.VMEM((ROWS, S), F32),
            pltpu.VMEM((NY, S, S), BF16),
            pltpu.VMEM((NY, 8, S), F32),
            pltpu.VMEM((NY + 1, ROWS, S), F32),
            pltpu.VMEM((ROWS, S), F32),
            pltpu.VMEM((ROWS, S), F32),
            pltpu.VMEM((2, S, S), BF16),
            pltpu.VMEM((1, S), F32),
            pltpu.VMEM((ROWS, S), F32),
            pltpu.VMEM((2, S, S), BF16),
            pltpu.VMEM((1, S), F32),
            pltpu.VMEM((HR, S, S), BF16),
            pltpu.VMEM((HR, S, S), BF16),
            pltpu.VMEM((HR, 8, S), F32),
            pltpu.VMEM((1, S), F32),
            pltpu.VMEM((1, S), F32),
            pltpu.VMEM((NZ, PLANE, HR, S), BF16),
            dma((7,)),
            dma((3, 2)), dma((3, 2)),
            dma((2, 3)), dma((2, 3)),
            dma(()), dma(()),
            dma((3,)), dma((3,)),
            dma((3,)), dma((3,)),
            dma((4,)), dma(()),
            dma((8,)), dma((8,)),
            dma((7,)), dma((7,)),
            dma((2,)), dma(()),
            pltpu.SemaphoreType.REGULAR((3,)),
        ],
        compiler_params=pltpu.CompilerParams(
            collective_id=0, has_side_effects=True, vmem_limit_bytes=32 * 1024 * 1024
        ),
    )(*(
        pltpu.with_memory_space_constraint(a, pltpu.MemorySpace.HBM)
        for a in (obs_rows, obs_values.reshape(4, 128), obs_hours[None], prior_precision, transition, site_basis)
    ))


def predict_kernel(means_ref, sites_ref, early_ref, out_hbm, held, sems):
    copies = [pltpu.make_async_copy(early_ref, out_hbm.at[pl.ds(0, EARLY)], sems.at[CHUNKS])]
    copies[0].start()
    late = hours_of(means_ref, SOON, NZ)
    for c in range(CHUNKS):
        held[c] = against(late, sites_ref[c * WIDTH:(c + 1) * WIDTH, :])
        copies.append(
            pltpu.make_async_copy(
                held.at[c],
                out_hbm.at[pl.ds(EARLY, late.shape[0]), pl.ds(c * WIDTH, WIDTH)],
                sems.at[c],
            )
        )
        copies[-1].start()
    for copy in copies:
        copy.wait()


def predict(means, sites, early):
    vmem = pl.BlockSpec(memory_space=pltpu.MemorySpace.VMEM)
    hours = NZ * PLANE * HR
    return pl.pallas_call(
        predict_kernel,
        out_shape=jax.ShapeDtypeStruct((hours, sites.shape[0]), BF16),
        in_specs=[vmem] * 3,
        out_specs=pl.BlockSpec(memory_space=pltpu.MemorySpace.HBM),
        scratch_shapes=[
            pltpu.VMEM((CHUNKS, hours - EARLY, WIDTH), BF16),
            pltpu.SemaphoreType.DMA((CHUNKS + 1,)),
        ],
        compiler_params=pltpu.CompilerParams(vmem_limit_bytes=16 * 1024 * 1024),
    )(means, sites, early)


def body(obs_rows, obs_values, obs_hours, prior_precision, transition, site_basis):
    means, sites, early = filtered_means(
        obs_rows, obs_values, obs_hours, prior_precision, transition, site_basis
    )
    return predict(means, sites, early)


def solution(mesh):
    in_specs = (
        P(("tm", "site"), None),
        P(("tm", "site")),
        P(("tm", "site")),
        P(),
        P(),
        P(("tm", "site"), None),
    )
    out_specs = P(None, ("tm", "site"))
    return jax.shard_map(body, mesh=mesh, in_specs=in_specs, out_specs=out_specs, check_vma=False)
```
